128 devices in a mesh: px: 8 (over z, core), py: 16 (over y, x).
Axes of the slice: x: 4, y: 4, z: 4, core: 2. Of those that a mesh axis runs over, the one named last changes fastest.
Arguments:
- features: bfloat16 [98304, 768], P(('px', 'py')), may hold values from -6 to 6
- weight_one: bfloat16 [768, 768], replicated, may hold values from -0.21875 to 0.21875
- weight_two: bfloat16 [768, 768], replicated, may hold values from -0.21875 to 0.21875
- tile_values: bfloat16 [4096, 128, 128], P(('px', 'py')), may hold values from -0.375 to 0.375
- tile_rows: int32 [128, 32], P(('px', 'py')), may hold values from 0 to 5
- tile_cols: int32 [128, 32], P(('px', 'py')), may hold values from 0 to 13
- tile_count: int32 [128], P(('px', 'py')), may hold values from 4 to 32, as said below
- send_rows: int32 [128, 128, 8], P(('px', 'py')), may hold values from 0 to 767
- send_count: int32 [128, 128], P(('px', 'py')), may hold values from 1 to 8, as said below
- stale_hidden: bfloat16 [131072, 768], P(('px', 'py')), may hold values from -3 to 3
- stale_grad: bfloat16 [131072, 768], P(('px', 'py')), may hold values from -6 to 6
- out_grad: bfloat16 [98304, 768], P(('px', 'py')), may hold values from -6 to 6
Outputs:
- next_hidden: bfloat16 [131072, 768], P(('px', 'py'))
- next_grad: bfloat16 [131072, 768], P(('px', 'py'))
- grad_one: float32 [768, 768], replicated
- grad_two: float32 [768, 768], replicated
The draws below stay inside these ranges and needn't reach their ends.
Inputs may be any that keep to these rules, and one draw needn't show every extreme that they name: The tiles of a part with index below its tile_count are live, the others are ignored; some part has 32 live tiles in every draw. `tile_cols`: column tiles below 6 hold the part's own rows; the rest hold the received boundary rows, 8 slots from each part in order of the part. `send_rows`: slots at or beyond the matching send_count are unused. `send_count`: every part sends 8 rows to at least one peer in every draw.
All inputs are finite; a program needn't handle non-finite values.
Results may differ from the reference program's by a relative error of at most 0.0061.
Values may be sent and summed in bfloat16 or wider, within the bound.
No kernel may reach another device: no remote copies, remote signals or barrier semaphores. Data moves between devices by JAX's collectives and lax.ppermute only.
A program may use at most 128 MiB of HBM per device.

```python
import math
import jax
import jax.numpy as jnp
from jax import lax

D = 768
ROWS = 768
TILE = 128
TILES = 32
SLOTS = 8
PARTS_SIZE = 128
NODES = 98304
COLTILES = 14
N_PX = 8
N_PY = 16


def draw_tile_count(key, part):
    parts = N_PX * N_PY
    counts = jax.random.randint(jax.random.fold_in(key, 11), (parts,), max(1, TILES // 8), TILES // 2 + 1)
    busiest = jax.random.randint(jax.random.fold_in(key, 12), (), 0, parts)
    return jnp.where(jnp.arange(parts, dtype=jnp.int32) == busiest, TILES, counts).astype(jnp.int32)


def draw_send_count(key, part):
    parts = N_PX * N_PY
    counts = jax.random.randint(jax.random.fold_in(key, 21), (parts, parts), 1, SLOTS + 1)
    fullest = jax.random.randint(jax.random.fold_in(key, 22), (parts,), 0, parts)
    peers = jnp.arange(parts, dtype=jnp.int32)
    return jnp.where(peers[None, :] == fullest[:, None], SLOTS, counts).astype(jnp.int32)


def plant(array, key, low, largest):
    place = [jax.random.randint(jax.random.fold_in(key, axis), (), 0, length) for axis, length in enumerate(array.shape)]
    main_axis = array.shape.index(max(array.shape))
    next_to = place[:main_axis] + [(place[main_axis] + 1) % array.shape[main_axis]] + place[main_axis + 1:]
    return array.at[tuple(place)].set(low).at[tuple(next_to)].set(largest)


def block_levels(stream_key, shape, shards, low, top_value):
    def one(axis_at, shards_of):
        steps = jax.random.uniform(jax.random.fold_in(jax.random.fold_in(stream_key, 6), axis_at), (shards_of,), jnp.float32, low / len(shards), top_value / len(shards))
        return jnp.repeat(jnp.exp(steps), shape[axis_at] // shards_of).reshape((-1,) + (1,) * (len(shape) - axis_at - 1))

    level = one(*shards[0])
    for cut in shards[1:]:
        level = level * one(*cut)
    return level


def normal_values(key, extent, spread, most, split=(), held_as=jnp.bfloat16):
    result = jax.random.normal(key, extent, jnp.float32) * spread
    if len(split) > 0:
        result = block_levels(key, extent, split, -0.22, 0.18) * result
    return jnp.clip(result, min=-most, max=most).astype(held_as)


def setup_inputs(seed: int = 0) -> dict:
    splits = jax.random.split(jax.random.key(seed), 13)
    features = normal_values(splits[0], (NODES, D), 1.0, 6.0, ((0, 128),))
    weight_one = normal_values(splits[1], (D, D), D ** -0.5, 0.21875)
    weight_two = normal_values(splits[2], (D, D), D ** -0.5, 0.21875)
    tile_values = normal_values(splits[3], (PARTS_SIZE * TILES, TILE, TILE), (TILE * 2) ** -0.5, 0.375, ((0, 128),))
    tile_rows = plant(jax.random.randint(splits[4], (PARTS_SIZE, TILES), 0, ROWS // TILE), jax.random.fold_in(splits[4], 1), 0, (ROWS // TILE) - 1).astype(jnp.int32)
    tile_cols = plant(jax.random.randint(splits[5], (PARTS_SIZE, TILES), 0, COLTILES), jax.random.fold_in(splits[5], 1), 0, COLTILES - 1).astype(jnp.int32)
    tile_count = draw_tile_count(jax.random.fold_in(splits[12], 71), 0)
    send_rows = plant(jax.random.randint(splits[7], (PARTS_SIZE, PARTS_SIZE, SLOTS), 0, ROWS), jax.random.fold_in(splits[7], 1), 0, ROWS - 1).astype(jnp.int32)
    send_count = draw_send_count(jax.random.fold_in(splits[12], 71), 0)
    stale_hidden = normal_values(splits[9], (PARTS_SIZE * PARTS_SIZE * SLOTS, D), 0.5, 3.0, ((0, 128),))
    stale_grad = normal_values(splits[10], (PARTS_SIZE * PARTS_SIZE * SLOTS, D), 1.0, 6.0, ((0, 128),))
    out_grad = normal_values(splits[11], (NODES, D), 1.0, 6.0, ((0, 128),))
    return {"features": features, "weight_one": weight_one, "weight_two": weight_two, "tile_values": tile_values, "tile_rows": tile_rows, "tile_cols": tile_cols, "tile_count": tile_count, "send_rows": send_rows, "send_count": send_count, "stale_hidden": stale_hidden, "stale_grad": stale_grad, "out_grad": out_grad}


def exact_gelu(value):
    return jax.nn.gelu(value, approximate=False)

def aggregate(source, tiles, rows, cols, live):
    active = jnp.arange(tiles.shape[0], dtype=jnp.int32) < live
    values = jnp.where(active[:, None, None], tiles, jnp.zeros_like(tiles)).astype(jnp.float32)
    blocks = source.reshape(-1, TILE, D)[cols].astype(jnp.float32)
    partial_value = jnp.einsum('gij,gjd->gid', values, blocks, precision=lax.Precision.HIGHEST)
    return jax.ops.segment_sum(partial_value, rows, num_segments=ROWS // TILE).reshape(ROWS, D)

def spread_back(grads, tiles, rows, cols, live, col_tiles):
    active = jnp.arange(tiles.shape[0], dtype=jnp.int32) < live
    values = jnp.where(active[:, None, None], tiles, jnp.zeros_like(tiles)).astype(jnp.float32)
    blocks = grads.reshape(-1, TILE, D)[rows].astype(jnp.float32)
    partial_value = jnp.einsum('gji,gjd->gid', values, blocks, precision=lax.Precision.HIGHEST)
    return jax.ops.segment_sum(partial_value, cols, num_segments=col_tiles).reshape(-1, D)

def reference(features, weight_one, weight_two, tile_values, tile_rows, tile_cols, tile_count, send_rows, send_count, stale_hidden, stale_grad, out_grad):
    parts = N_PX * N_PY
    col_tiles = (ROWS + parts * SLOTS) // TILE
    slot_ids = jnp.arange(SLOTS, dtype=jnp.int32)
    sent_mask = slot_ids[None, None, :] < send_count[:, :, None]
    heard_mask = jnp.swapaxes(sent_mask, 0, 1)
    own = features.reshape(parts, ROWS, D)

    def pick(item):
        block, chosen = item
        return block[chosen]
    outgoing = lax.map(pick, (own, send_rows))
    outgoing = jnp.where(sent_mask[..., None], outgoing, jnp.zeros_like(outgoing))
    incoming = jnp.swapaxes(outgoing, 0, 1)

    def local_pass(carry, item):
        feats, tiles, rows, cols, live, chosen, sent, arrived, heard, old_hidden, old_grad, cotangent = item
        source_one = jnp.concatenate([feats, arrived.reshape(-1, D)], axis=0)
        agg_one = aggregate(source_one, tiles, rows, cols, live).astype(jnp.bfloat16)
        pre_one = jnp.dot(agg_one, weight_one, preferred_element_type=jnp.float32)
        hidden = exact_gelu(pre_one).astype(jnp.bfloat16)
        picked = hidden[chosen]
        box_hidden = jnp.where(sent[:, :, None], picked, jnp.zeros_like(picked))
        kept = jnp.where(heard.reshape(-1, 1), old_hidden, jnp.zeros_like(old_hidden))
        source_two = jnp.concatenate([hidden, kept], axis=0)
        agg_two = aggregate(source_two, tiles, rows, cols, live).astype(jnp.bfloat16)
        down = jnp.dot(cotangent, weight_two.T, preferred_element_type=jnp.float32).astype(jnp.bfloat16)
        back = spread_back(down, tiles, rows, cols, live, col_tiles)
        own_grad = back[:ROWS]
        remote = back[ROWS:].reshape(parts, SLOTS, D)
        box_grad = jnp.where(heard[:, :, None], remote, jnp.zeros_like(remote)).astype(jnp.bfloat16)
        old_back = old_grad.astype(jnp.float32)
        old_back = jnp.where(sent.reshape(-1, 1), old_back, jnp.zeros_like(old_back))
        hidden_grad = own_grad + jax.ops.segment_sum(old_back, chosen.reshape(-1), num_segments=ROWS)
        pull = jax.vjp(exact_gelu, pre_one)[1]
        pre_grad = pull(hidden_grad)[0].astype(jnp.bfloat16)
        part_one = jnp.dot(agg_one.T, pre_grad, preferred_element_type=jnp.float32)
        part_two = jnp.dot(agg_two.T, cotangent, preferred_element_type=jnp.float32)
        return ((carry[0] + part_one, carry[1] + part_two), (box_hidden, box_grad))
    items = (own, tile_values.reshape(parts, TILES, TILE, TILE), tile_rows, tile_cols, tile_count, send_rows, sent_mask, incoming, heard_mask, stale_hidden.reshape(parts, parts * SLOTS, D), stale_grad.reshape(parts, parts * SLOTS, D), out_grad.reshape(parts, ROWS, D))
    start = (jnp.zeros((D, D), jnp.float32), jnp.zeros((D, D), jnp.float32))
    sums, boxes = lax.scan(local_pass, start, items)
    scale = 1.0 / math.sqrt(ROWS * parts)
    next_hidden = jnp.swapaxes(boxes[0], 0, 1).reshape(-1, D)
    next_grad = jnp.swapaxes(boxes[1], 0, 1).reshape(-1, D)
    return (next_hidden, next_grad, sums[0] * scale, sums[1] * scale)
```

```python
import functools
import math

import jax
import jax.numpy as jnp
from jax import lax
from jax.experimental import pallas as pl
from jax.experimental.pallas import tpu as pltpu
from jax.sharding import PartitionSpec as P

BOTH = ("px", "py")
LANES = 128
VMEM = pl.BlockSpec(memory_space=pltpu.VMEM)
SMEM = pl.BlockSpec(memory_space=pltpu.SMEM)
INV_SQRT2 = 1.0 / math.sqrt(2.0)
INV_SQRT_2PI = 1.0 / math.sqrt(2.0 * math.pi)


def mm(a, b, dims=((1,), (0,))):
    return lax.dot_general(a, b, (dims, ((), ())), preferred_element_type=jnp.float32)


def fill_picks(idx_ref, pick_ref):
    rows = pick_ref.shape[1]
    lane = lax.broadcasted_iota(jnp.int32, (LANES, rows), 1)
    for j in range(idx_ref.shape[0]):
        across = jnp.broadcast_to(idx_ref[j : j + 1, :], (LANES, LANES))
        down = across.T
        wide = jnp.concatenate([down] * (rows // LANES), axis=1)
        hit = jnp.where(wide == lane, 1.0, 0.0)
        pick_ref[j * LANES : (j + 1) * LANES, :] = hit.astype(pick_ref.dtype)


def pack_kernel(idx_ref, features_ref, out_ref, pick_ref):
    width = features_ref.shape[1]
    fill_picks(idx_ref, pick_ref)
    out_ref[:, :width] = mm(pick_ref[...], features_ref[...]).astype(out_ref.dtype)
    for j in range(idx_ref.shape[0]):
        across = jnp.broadcast_to(idx_ref[j : j + 1, :], (LANES, LANES))
        used = jnp.where(across.T >= 0, 1.0, 0.0)
        out_ref[j * LANES : (j + 1) * LANES, width:] = used.astype(out_ref.dtype)


def local_kernel(
    rows_ref,
    cols_ref,
    count_ref,
    idx_ref,
    tiles_ref,
    features_ref,
    out_grad_ref,
    weight_ref,
    stale_grad_ref,
    adj_ref,
    agg_ref,
    hidden_grad_ref,
    grad_out_ref,
    adj32,
    scatter,
):
    tile = tiles_ref.shape[1]
    own = features_ref.shape[0]
    adj32[...] = jnp.zeros_like(adj32)

    @pl.loop(0, count_ref[0])
    def _(t):
        r = pl.multiple_of(rows_ref[t] * tile, tile)
        c = pl.multiple_of(cols_ref[t] * tile, tile)
        adj32[pl.ds(r, tile), pl.ds(c, tile)] += tiles_ref[t].astype(jnp.float32)

    adj_ref[...] = adj32[...].astype(adj_ref.dtype)
    down = mm(out_grad_ref[...], weight_ref[...], ((1,), (1,))).astype(jnp.bfloat16)
    grad_out_ref[...] = mm(adj_ref[:, own:], down, ((0,), (0,))).astype(grad_out_ref.dtype)
    place = lax.broadcasted_iota(jnp.int32, (own, LANES), 0)
    for j in range(idx_ref.shape[0]):
        across = jnp.broadcast_to(idx_ref[j : j + 1, :], (own, LANES))
        hit = jnp.where(across == place, 1.0, 0.0)
        scatter[:, j * LANES : (j + 1) * LANES] = hit.astype(scatter.dtype)
    hidden_grad_ref[...] = mm(adj_ref[:, :own], down, ((0,), (0,))) + mm(
        scatter[...], stale_grad_ref[...]
    )
    agg_ref[...] = mm(adj_ref[:, :own], features_ref[...])


def main_kernel(
    core_ref,
    idx_ref,
    arrived_ref,
    adj_ref,
    agg_ref,
    weight_ref,
    hidden_grad_ref,
    stale_hidden_ref,
    out_grad_ref,
    hidden_out_ref,
    keep_ref,
    send_ref,
    pick_ref,
    kept_ref,
):
    own, width = agg_ref.shape
    agg_one = (agg_ref[...] + mm(adj_ref[:, own:], arrived_ref[:, :width])).astype(jnp.bfloat16)
    pre = mm(agg_one, weight_ref[...])
    cdf = 0.5 * (1.0 + lax.erf(pre * INV_SQRT2))
    hidden = (pre * cdf).astype(jnp.bfloat16)
    slope = cdf + pre * (jnp.exp(-0.5 * pre * pre) * INV_SQRT_2PI)
    pre_grad = (hidden_grad_ref[...] * slope).astype(jnp.bfloat16)
    fill_picks(idx_ref, pick_ref)
    hidden_out_ref[...] = mm(pick_ref[...], hidden).astype(hidden_out_ref.dtype)
    part_one = mm(agg_one, pre_grad, ((0,), (0,)))
    for k in range(width // LANES):
        at = slice(k * LANES, (k + 1) * LANES)
        heard = arrived_ref[:, width:].astype(jnp.float32) > 0.5
        stale = stale_hidden_ref[:, at].astype(jnp.float32)
        kept_ref[:, at] = jnp.where(heard, stale, 0.0).astype(kept_ref.dtype)
    agg_two = (mm(adj_ref[:, :own], hidden) + mm(adj_ref[:, own:], kept_ref[...])).astype(jnp.bfloat16)
    part_two = mm(agg_two, out_grad_ref[...], ((0,), (0,)))
    first = core_ref[0] == 0
    for k in range(width // LANES):
        at = slice(k * LANES, (k + 1) * LANES)
        one, two = part_one[:, at], part_two[:, at]
        keep_ref[k] = jnp.where(first, one, two)
        send_ref[k] = jnp.where(first, two, one).astype(send_ref.dtype)


def call(kernel, out_shape, scalars, scratch):
    def run(*args):
        return pl.pallas_call(
            kernel,
            out_shape=out_shape,
            in_specs=[SMEM] * scalars + [VMEM] * (len(args) - scalars),
            out_specs=jax.tree.map(lambda _: VMEM, out_shape),
            scratch_shapes=scratch,
            compiler_params=pltpu.CompilerParams(vmem_limit_bytes=48 * 1024 * 1024),
        )(*args)

    return run


def trade(value, axis, groups=None):
    return lax.all_to_all(
        value, axis, split_axis=0, concat_axis=0, tiled=True, axis_index_groups=groups
    )


def spread(value, count):
    return jnp.broadcast_to(value[None], (count, *value.shape))


def local(
    features,
    weight_one,
    weight_two,
    tile_values,
    tile_rows,
    tile_cols,
    tile_count,
    send_rows,
    send_count,
    stale_hidden,
    stale_grad,
    out_grad,
):
    bf16, f32 = jnp.bfloat16, jnp.float32
    parts = lax.axis_size(BOTH)
    n_px, n_py = lax.axis_size("px"), lax.axis_size("py")
    n_z = n_px // 2
    own, width = features.shape
    slots = send_rows.shape[2]
    boundary = parts * slots
    cols = own + boundary
    shape = jax.ShapeDtypeStruct
    slot_ids = jnp.arange(slots, dtype=jnp.int32)
    sent = slot_ids[None, :] < send_count[0][:, None]
    idx = jnp.where(sent, send_rows[0], -1).reshape(boundary // LANES, LANES)

    outgoing = call(
        pack_kernel,
        shape((boundary, width + LANES), bf16),
        0,
        [pltpu.VMEM((boundary, own), bf16)],
    )(idx, features)
    arrived = trade(outgoing.reshape(parts, slots, -1), BOTH).reshape(boundary, -1)

    adj, agg, hidden_grad, grad_out = call(
        local_kernel,
        (
            shape((own, cols), bf16),
            shape((own, width), f32),
            shape((own, width), f32),
            shape((boundary, width), bf16),
        ),
        3,
        [pltpu.VMEM((own, cols), f32), pltpu.VMEM((own, boundary), bf16)],
    )(tile_rows[0], tile_cols[0], tile_count, idx, tile_values, features, out_grad, weight_two, stale_grad)
    grads = trade(grad_out.reshape(parts, slots, width), BOTH)
    next_grad = jnp.where(sent[:, :, None], grads, jnp.zeros_like(grads)).reshape(boundary, width)

    core = (lax.axis_index("px") % 2).astype(jnp.int32).reshape(1)
    blocks = width // LANES
    hidden_out, keep, send = call(
        main_kernel,
        (
            shape((boundary, width), bf16),
            shape((blocks, width, LANES), f32),
            shape((blocks, width, LANES), bf16),
        ),
        1,
        [pltpu.VMEM((boundary, own), bf16), pltpu.VMEM((boundary, width), bf16)],
    )(core, idx, arrived, adj, agg, weight_one, hidden_grad, stale_hidden, out_grad)

    swap = [(i, i ^ 1) for i in range(n_px)]
    z_groups = [[i for i in range(n_px) if i % 2 == c] for c in range(2)]
    lines = blocks * width
    other = lax.ppermute(send, "px", swap)
    mine = (keep + other.astype(f32)).astype(bf16).reshape(n_py, lines // n_py, LANES)
    mine = trade(mine, "py").astype(f32).sum(0).astype(bf16)
    mine = trade(mine.reshape(n_z, lines // (n_py * n_z), LANES), "px", z_groups)
    mine = mine.astype(f32).sum(0).astype(bf16)
    mine = trade(spread(mine, n_z), "px", z_groups).reshape(lines // n_py, LANES)
    mine = trade(spread(mine, n_py), "py").reshape(blocks, width, LANES)
    other = lax.ppermute(mine, "px", swap)

    next_hidden = trade(hidden_out.reshape(parts, slots, width), BOTH).reshape(boundary, width)
    scale = 1.0 / math.sqrt(own * parts)
    one = jnp.where(core[0] == 0, mine, other).astype(f32) * scale
    two = jnp.where(core[0] == 0, other, mine).astype(f32) * scale
    one = jnp.moveaxis(one, 0, 1).reshape(width, width)
    two = jnp.moveaxis(two, 0, 1).reshape(width, width)
    return next_hidden, next_grad, one, two


def solution(mesh):
    in_specs = (
        P(BOTH, None),
        P(),
        P(),
        P(BOTH, None, None),
        P(BOTH, None),
        P(BOTH, None),
        P(BOTH),
        P(BOTH, None, None),
        P(BOTH, None),
        P(BOTH, None),
        P(BOTH, None),
        P(BOTH, None),
    )
    out_specs = (P(BOTH, None), P(BOTH, None), P(), P())
    return jax.shard_map(local, mesh=mesh, in_specs=in_specs, out_specs=out_specs, check_vma=False)
```

```python
import functools
import math

import jax
import jax.numpy as jnp
from jax import lax
from jax.experimental import pallas as pl
from jax.experimental.pallas import tpu as pltpu
from jax.sharding import PartitionSpec as P

BOTH = ("px", "py")
LANES = 128
PACK, LOCAL, MAIN = 58, 62, 56
VMEM = pl.BlockSpec(memory_space=pltpu.VMEM)
HBM = pl.BlockSpec(memory_space=pltpu.HBM)
SMEM = pl.BlockSpec(memory_space=pltpu.SMEM)
INV_SQRT2 = 1.0 / math.sqrt(2.0)
INV_SQRT_2PI = 1.0 / math.sqrt(2.0 * math.pi)


def mm(a, b, dims=((1,), (0,))):
    return lax.dot_general(a, b, (dims, ((), ())), preferred_element_type=jnp.float32)


def fill_picks(idx_ref, pick_ref):
    rows = pick_ref.shape[1]
    lane = lax.broadcasted_iota(jnp.int32, (LANES, rows), 1)
    for j in range(idx_ref.shape[0]):
        across = jnp.broadcast_to(idx_ref[j : j + 1, :], (LANES, LANES))
        down = across.T
        wide = jnp.concatenate([down] * (rows // LANES), axis=1)
        hit = jnp.where(wide == lane, 1.0, 0.0)
        pick_ref[j * LANES : (j + 1) * LANES, :] = hit.astype(pick_ref.dtype)


def copies(sems, pairs):
    started = [
        pltpu.make_async_copy(src, dst, sems.at[i]) for i, (src, dst) in enumerate(pairs)
    ]
    for copy in started:
        copy.start()
    return started


def pack_kernel(idx_ref, features_hbm, out_hbm, features, picks, out, sems):
    width = features.shape[1]
    (fetch,) = copies(sems, [(features_hbm, features)])
    fill_picks(idx_ref, picks)
    for j in range(idx_ref.shape[0]):
        across = jnp.broadcast_to(idx_ref[j : j + 1, :], (LANES, LANES))
        used = jnp.where(across.T >= 0, 1.0, 0.0)
        out[j * LANES : (j + 1) * LANES, width:] = used.astype(out.dtype)
    fetch.wait()
    step = out.shape[0] // 4
    stores = []
    for k in range(4):
        at = pl.ds(k * step, step)
        out[at, :width] = mm(picks[at, :], features[...]).astype(out.dtype)
        store = pltpu.make_async_copy(out.at[at, :], out_hbm.at[at, :], sems.at[1 + k])
        store.start()
        stores.append(store)
    for store in stores:
        store.wait()


def local_kernel(
    rows_ref,
    cols_ref,
    count_ref,
    idx_ref,
    tiles_hbm,
    features_hbm,
    out_grad_hbm,
    weight_hbm,
    stale_grad_hbm,
    near_hbm,
    far_hbm,
    agg_hbm,
    hidden_grad_hbm,
    box_hbm,
    tiles,
    features,
    out_grad,
    weight,
    stale_grad,
    near32,
    far32,
    near,
    far,
    scatter,
    agg,
    hidden_grad,
    grad_out,
    sems,
):
    tile = tiles.shape[1]
    own = features.shape[0]
    fetches = copies(
        sems,
        [
            (tiles_hbm, tiles),
            (out_grad_hbm, out_grad),
            (weight_hbm, weight),
            (features_hbm, features),
            (stale_grad_hbm, stale_grad),
        ],
    )
    near32[...] = jnp.zeros_like(near32)
    far32[...] = jnp.zeros_like(far32)
    fetches[0].wait()

    @pl.loop(0, count_ref[0])
    def _(t):
        r = pl.multiple_of(rows_ref[t] * tile, tile)
        c = pl.multiple_of(cols_ref[t] * tile, tile)
        value = tiles[t].astype(jnp.float32)

        @pl.when(c < own)
        def _():
            near32[pl.ds(r, tile), pl.ds(c, tile)] += value

        @pl.when(c >= own)
        def _():
            far32[pl.ds(r, tile), pl.ds(pl.multiple_of(c - own, tile), tile)] += value

    near[...] = near32[...].astype(near.dtype)
    far[...] = far32[...].astype(far.dtype)
    saves = copies(sems.at[pl.ds(5, 2)], [(near, near_hbm), (far, far_hbm)])
    fetches[3].wait()
    agg[...] = mm(near[...], features[...])
    saves += copies(sems.at[pl.ds(7, 1)], [(agg, agg_hbm)])
    fetches[1].wait()
    fetches[2].wait()
    down = mm(out_grad[...], weight[...], ((1,), (1,))).astype(jnp.bfloat16)
    remote = mm(far[...], down, ((0,), (0,)))
    grad_out[...] = remote.reshape(grad_out.shape).astype(grad_out.dtype)
    slots = grad_out.shape[1]
    saves += copies(sems.at[pl.ds(8, 1)], [(grad_out, box_hbm.at[:, slots:, :])])
    place = lax.broadcasted_iota(jnp.int32, (own, LANES), 0)
    for j in range(idx_ref.shape[0]):
        across = jnp.broadcast_to(idx_ref[j : j + 1, :], (own, LANES))
        hit = jnp.where(across == place, 1.0, 0.0)
        scatter[:, j * LANES : (j + 1) * LANES] = hit.astype(scatter.dtype)
    fetches[4].wait()
    hidden_grad[...] = mm(near[...], down, ((0,), (0,))) + mm(scatter[...], stale_grad[...])
    saves += copies(sems.at[pl.ds(9, 1)], [(hidden_grad, hidden_grad_hbm)])
    for save in saves:
        save.wait()


def main_kernel(
    core_ref,
    idx_ref,
    arrived_hbm,
    near_hbm,
    far_hbm,
    agg_hbm,
    weight_hbm,
    hidden_grad_hbm,
    stale_hidden_hbm,
    out_grad_hbm,
    _,
    box_hbm,
    keep_hbm,
    send_hbm,
    arrived,
    near,
    far,
    agg,
    weight,
    hidden_grad,
    stale_hidden,
    out_grad,
    picks,
    hidden_out,
    keep,
    send,
    sems,
):
    own, width = agg.shape
    fetches = copies(
        sems,
        [
            (arrived_hbm, arrived),
            (far_hbm, far),
            (agg_hbm, agg),
            (weight_hbm, weight),
            (hidden_grad_hbm, hidden_grad),
            (near_hbm, near),
            (stale_hidden_hbm, stale_hidden),
            (out_grad_hbm, out_grad),
        ],
    )
    fill_picks(idx_ref, picks)
    for fetch in fetches[:3]:
        fetch.wait()
    agg_one = (agg[...] + mm(far[...], arrived[:, :width])).astype(jnp.bfloat16)
    fetches[3].wait()
    pre = mm(agg_one, weight[...])
    cdf = 0.5 * (1.0 + lax.erf(pre * INV_SQRT2))
    hidden = (pre * cdf).astype(jnp.bfloat16)
    picked = mm(picks[...], hidden).reshape(hidden_out.shape)
    hidden_out[...] = picked.astype(hidden_out.dtype)
    slots = hidden_out.shape[1]
    saves = copies(sems.at[pl.ds(8, 1)], [(hidden_out, box_hbm.at[:, :slots, :])])
    fetches[6].wait()
    heard = arrived[:, width:].astype(jnp.float32) > 0.5
    for k in range(width // LANES):
        at = slice(k * LANES, (k + 1) * LANES)
        stale = stale_hidden[:, at].astype(jnp.float32)
        stale_hidden[:, at] = jnp.where(heard, stale, 0.0).astype(stale_hidden.dtype)
    fetches[5].wait()
    agg_two = (mm(near[...], hidden) + mm(far[...], stale_hidden[...])).astype(jnp.bfloat16)
    fetches[7].wait()
    part_two = mm(agg_two, out_grad[...], ((0,), (0,)))
    slope = cdf + pre * (jnp.exp(-0.5 * pre * pre) * INV_SQRT_2PI)
    fetches[4].wait()
    pre_grad = (hidden_grad[...] * slope).astype(jnp.bfloat16)
    part_one = mm(agg_one, pre_grad, ((0,), (0,)))
    first = core_ref[0] == 0
    for k in range(width // LANES):
        at = slice(k * LANES, (k + 1) * LANES)
        one, two = part_one[:, at], part_two[:, at]
        lines = pl.ds(k * width, width)
        keep[lines, :] = jnp.where(first, one, two)
        send[lines, :] = jnp.where(first, two, one).astype(send.dtype)
    saves += copies(sems.at[pl.ds(9, 2)], [(send, send_hbm), (keep, keep_hbm)])
    for save in saves:
        save.wait()


def chunk(ref, base, index, size):
    return ref[pl.ds(pl.multiple_of(base + index * size, 8), size), :]


def split_kernel(at_ref, keep_ref, other_ref, own_a, own_b, *sends):
    size = own_a.shape[0]
    half = 4 * size
    for step in range(4):
        for side, (base, at, own) in enumerate(((0, at_ref[0], own_a), (half, at_ref[1], own_b))):
            index = (at + step) & 3
            value = chunk(keep_ref, base, index, size)
            value = value + chunk(other_ref, base, index, size).astype(jnp.float32)
            if step == 0:
                own[...] = value
            else:
                to = sends[side * 3 + step - 1]
                to[...] = value.astype(to.dtype)


def second_kernel(at_ref, own_a, own_b, a1, a2, a3, b1, b2, b3, next_a, next_b, *refs):
    sends, (sum_a, sum_b) = refs[:6], refs[6:]
    size = next_a.shape[0]
    for own, one, two, three, total in ((own_a, a1, a2, a3, sum_a), (own_b, b1, b2, b3, sum_b)):
        total[...] = own[...] + (
            one[...].astype(jnp.float32)
            + two[...].astype(jnp.float32)
            + three[...].astype(jnp.float32)
        )
    for step in range(4):
        for side, (at, total, own) in enumerate(
            ((at_ref[1], sum_a, next_a), (at_ref[0], sum_b, next_b))
        ):
            value = chunk(total, 0, (at + step) & 3, size)
            if step == 0:
                own[...] = value
            else:
                to = sends[side * 3 + step - 1]
                to[...] = value.astype(to.dtype)


def third_kernel(own_a, own_b, a1, a2, a3, b1, b2, b3, out_ref):
    size = own_a.shape[0]
    for base, own, one, two, three in ((0, own_a, a1, a2, a3), (size, own_b, b1, b2, b3)):
        total = own[...] + (
            one[...].astype(jnp.float32)
            + two[...].astype(jnp.float32)
            + three[...].astype(jnp.float32)
        )
        out_ref[base : base + size, :] = total.astype(out_ref.dtype)


def ring_kernel(own, one, two, three, out_a, out_b):
    f32 = jnp.float32
    total = (own[...].astype(f32) + two[...].astype(f32)) + (
        one[...].astype(f32) + three[...].astype(f32)
    )
    size = out_a.shape[0]
    out_a[...] = total[:size].astype(out_a.dtype)
    out_b[...] = total[size:].astype(out_b.dtype)


def place(out_ref, base, at, pieces):
    size = pieces[0].shape[0]
    for step, piece in enumerate(pieces):
        index = (at - step) & 3
        out_ref[pl.ds(pl.multiple_of(base + index * size, 8), size), :] = piece[...]


def join_kernel(at_ref, own_a, own_b, a1, a2, a3, b1, b2, b3, out_a, out_b):
    place(out_a, 0, at_ref[1], (own_a, a1, a2, a3))
    place(out_b, 0, at_ref[0], (own_b, b1, b2, b3))


def whole_kernel(at_ref, own_a, own_b, a1, a2, a3, b1, b2, b3, out_ref):
    place(out_ref, 0, at_ref[0], (own_a, a1, a2, a3))
    place(out_ref, out_ref.shape[0] // 2, at_ref[1], (own_b, b1, b2, b3))


def finish_kernel(scale, core_ref, mine_ref, other_ref, one_ref, two_ref):
    width = one_ref.shape[1]
    first = core_ref[0] == 0
    for k in range(width // LANES):
        lines = pl.ds(k * width, width)
        at = slice(k * LANES, (k + 1) * LANES)
        mine = mine_ref[lines, :].astype(jnp.float32) * scale
        other = other_ref[lines, :].astype(jnp.float32) * scale
        one_ref[:, at] = jnp.where(first, mine, other)
        two_ref[:, at] = jnp.where(first, other, mine)


def in_vmem(*refs):
    return [pltpu.VMEM(r.shape, r.dtype) for r in refs]


def call(kernel, out_shape, scalars, scratch=(), vmem=None, limit=6, aliases=None):
    def run(*args):
        n_vmem = len(args) - scalars if vmem is None else vmem
        size = sum(a.size * a.dtype.itemsize for a in (*args, *jax.tree.leaves(out_shape)))
        out_spec = VMEM if vmem is None else HBM
        return pl.pallas_call(
            kernel,
            out_shape=out_shape,
            in_specs=[SMEM] * scalars + [VMEM] * n_vmem + [HBM] * (len(args) - scalars - n_vmem),
            out_specs=jax.tree.map(lambda _: out_spec, out_shape),
            scratch_shapes=scratch,
            input_output_aliases=aliases or {},
            cost_estimate=pl.CostEstimate(flops=0, transcendentals=0, bytes_accessed=size),
            compiler_params=pltpu.CompilerParams(vmem_limit_bytes=limit * 1024 * 1024),
        )(*args)

    return run


def trade(value):
    return lax.all_to_all(value, BOTH, split_axis=0, concat_axis=0, tiled=True)


def along_x(value, step):
    n = lax.axis_size("py")
    return lax.ppermute(value, "py", [(i, (i & ~3) | ((i + step) & 3)) for i in range(n)])


def along_y(value, step):
    n = lax.axis_size("py")
    return lax.ppermute(value, "py", [(i, (i + 4 * step) % n) for i in range(n)])


def along_z(value, step):
    n = lax.axis_size("px")
    return lax.ppermute(value, "px", [(i, (i + 2 * step) % n) for i in range(n)])


def sibling(value):
    n = lax.axis_size("px")
    return lax.ppermute(value, "px", [(i, i ^ 1) for i in range(n)])


def local(
    features,
    weight_one,
    weight_two,
    tile_values,
    tile_rows,
    tile_cols,
    tile_count,
    send_rows,
    send_count,
    stale_hidden,
    stale_grad,
    out_grad,
):
    bf16, f32 = jnp.bfloat16, jnp.float32
    parts = lax.axis_size(BOTH)
    own, width = features.shape
    slots = send_rows.shape[2]
    boundary = parts * slots
    cols = own + boundary
    shape = jax.ShapeDtypeStruct
    slot_ids = jnp.arange(slots, dtype=jnp.int32)
    sent = slot_ids[None, :] < send_count[0][:, None]
    idx = jnp.where(sent, send_rows[0], -1).reshape(boundary // LANES, LANES)
    core = (lax.axis_index("px") % 2).astype(jnp.int32).reshape(1)
    py = lax.axis_index("py").astype(jnp.int32)
    at = jnp.stack([py % 4, py // 4])

    pack = shape((boundary, width + LANES), bf16)
    square, square32 = shape((own, width), bf16), shape((own, width), f32)
    near, far = shape((own, own), bf16), shape((own, boundary), bf16)
    near32, far32 = shape((own, own), f32), shape((own, boundary), f32)
    slab, slots_in = shape((boundary, width), bf16), shape((parts, slots, width), bf16)
    box = shape((parts, 2 * slots, width), bf16)
    weight = shape(weight_one.shape, bf16)
    picks = shape((boundary, own), bf16)
    semaphores = lambda count: [pltpu.SemaphoreType.DMA((count,))]
    lines = width * width // LANES
    keep, send = shape((lines, LANES), f32), shape((lines, LANES), bf16)

    outgoing = call(
        pack_kernel,
        pack,
        0,
        in_vmem(square, picks, pack) + semaphores(5),
        1,
        PACK,
    )(idx, features)
    arrived = trade(outgoing.reshape(parts, slots, -1)).reshape(boundary, -1)

    *kept, boxes = call(
        local_kernel,
        (near, far, square32, square32, box),
        3,
        in_vmem(
            tile_values, square, square, weight, slab, near32, far32, near, far, far, square32, square32, slots_in
        )
        + semaphores(10),
        1,
        LOCAL,
    )(tile_rows[0], tile_cols[0], tile_count, idx, tile_values, features, out_grad, weight_two, stale_grad)
    near_adj, far_adj, agg, hidden_grad = kept

    boxes, keep, send = call(
        main_kernel,
        (box, keep, send),
        1,
        in_vmem(
            pack, near, far, square32, weight, square32, slab, square, picks, slots_in, keep, send
        )
        + semaphores(11),
        1,
        MAIN,
        {10: 0},
    )(core, idx, arrived, near_adj, far_adj, agg, weight_one, hidden_grad, stale_hidden, out_grad, boxes)

    big, small = lines // 8, lines // 32
    six = lambda size: (shape((size, LANES), bf16),) * 6
    pair = lambda size, dtype: (shape((size, LANES), dtype),) * 2
    own_a, own_b, *out = call(split_kernel, pair(big, f32) + six(big), 1)(at, keep, sibling(send))
    got = [along_x(out[k], k + 1) for k in range(3)] + [along_y(out[3 + k], k + 1) for k in range(3)]
    own_a, own_b, *out = call(
        second_kernel,
        pair(small, f32) + six(small),
        1,
        [pltpu.VMEM((big, LANES), f32)] * 2,
    )(at, own_a, own_b, *got)
    got = [along_y(out[k], k + 1) for k in range(3)] + [along_x(out[3 + k], k + 1) for k in range(3)]
    total = call(third_kernel, shape((2 * small, LANES), bf16), 0)(own_a, own_b, *got)
    got = [along_z(total, k + 1) for k in range(3)]
    own_a, own_b = call(ring_kernel, pair(small, bf16), 0)(total, *got)
    got = [along_y(own_a, k + 1) for k in range(3)] + [along_x(own_b, k + 1) for k in range(3)]
    own_a, own_b = call(join_kernel, pair(big, bf16), 1)(at, own_a, own_b, *got)
    got = [along_x(own_a, k + 1) for k in range(3)] + [along_y(own_b, k + 1) for k in range(3)]
    mine = call(whole_kernel, shape((lines, LANES), bf16), 1)(at, own_a, own_b, *got)
    scale = 1.0 / math.sqrt(own * parts)
    one, two = call(
        functools.partial(finish_kernel, scale),
        (shape((width, width), f32),) * 2,
        1,
    )(core, mine, sibling(mine))

    boxes = trade(boxes)
    next_hidden = boxes[:, :slots].reshape(boundary, width)
    grads = boxes[:, slots:]
    next_grad = jnp.where(sent[:, :, None], grads, jnp.zeros_like(grads)).reshape(boundary, width)
    return next_hidden, next_grad, one, two


def solution(mesh):
    in_specs = (
        P(BOTH, None),
        P(),
        P(),
        P(BOTH, None, None),
        P(BOTH, None),
        P(BOTH, None),
        P(BOTH),
        P(BOTH, None, None),
        P(BOTH, None),
        P(BOTH, None),
        P(BOTH, None),
        P(BOTH, None),
    )
    out_specs = (P(BOTH, None), P(BOTH, None), P(), P())
    return jax.shard_map(local, mesh=mesh, in_specs=in_specs, out_specs=out_specs, check_vma=False)
```

```python
import functools
import math

import jax
import jax.numpy as jnp
from jax import lax
from jax.experimental import pallas as pl
from jax.experimental.pallas import tpu as pltpu
from jax.sharding import PartitionSpec as P

BOTH = ("px", "py")
LANES = 128
PACK, LOCAL, MAIN = 58, 62, 56
BOX, PIECE, SUM, FINISH = 20, 12, 8, 12
VMEM = pl.BlockSpec(memory_space=pltpu.VMEM)
HBM = pl.BlockSpec(memory_space=pltpu.HBM)
SMEM = pl.BlockSpec(memory_space=pltpu.SMEM)
INV_SQRT2 = 1.0 / math.sqrt(2.0)
INV_SQRT_2PI = 1.0 / math.sqrt(2.0 * math.pi)


def mm(a, b, dims=((1,), (0,))):
    return lax.dot_general(a, b, (dims, ((), ())), preferred_element_type=jnp.float32)


def fill_picks(idx_ref, pick_ref):
    rows = pick_ref.shape[1]
    lane = lax.broadcasted_iota(jnp.int32, (LANES, rows), 1)
    for j in range(idx_ref.shape[0]):
        across = jnp.broadcast_to(idx_ref[j : j + 1, :], (LANES, LANES))
        down = across.T
        wide = jnp.concatenate([down] * (rows // LANES), axis=1)
        hit = jnp.where(wide == lane, 1.0, 0.0)
        pick_ref[j * LANES : (j + 1) * LANES, :] = hit.astype(pick_ref.dtype)


def copies(sems, pairs):
    started = [
        pltpu.make_async_copy(src, dst, sems.at[i]) for i, (src, dst) in enumerate(pairs)
    ]
    for copy in started:
        copy.start()
    return started


def pack_kernel(rows_ref, counts_ref, features_hbm, out_hbm, idx_ref, features, picks, out, sems):
    width = features.shape[1]
    (fetch,) = copies(sems, [(features_hbm, features)])
    groups, parts = rows_ref.shape[0], counts_ref.shape[1]
    slots = groups * LANES // parts
    peers = parts // groups
    group = lax.broadcasted_iota(jnp.int32, (groups, parts), 0)
    peer = lax.broadcasted_iota(jnp.int32, (groups, parts), 1)
    counts = jnp.broadcast_to(counts_ref[...].astype(jnp.float32), (groups, parts))
    counts = jnp.where(peer // peers == group, counts, 0.0).astype(jnp.bfloat16)
    down = lax.broadcasted_iota(jnp.int32, (parts, LANES), 0)
    lane = lax.broadcasted_iota(jnp.int32, (parts, LANES), 1)
    expand = jnp.where(down % peers == lane // slots, 1.0, 0.0).astype(jnp.bfloat16)
    limit = mm(counts, expand)
    slot = (lax.broadcasted_iota(jnp.int32, (groups, LANES), 1) % slots).astype(jnp.float32)
    idx_ref[...] = jnp.where(slot < limit, rows_ref[...], -1)
    fill_picks(idx_ref, picks)
    for j in range(idx_ref.shape[0]):
        across = jnp.broadcast_to(idx_ref[j : j + 1, :], (LANES, LANES))
        used = jnp.where(across.T >= 0, 1.0, 0.0)
        out[j * LANES : (j + 1) * LANES, width:] = used.astype(out.dtype)
    fetch.wait()
    step = out.shape[0] // 4
    stores = []
    for k in range(4):
        at = pl.ds(k * step, step)
        out[at, :width] = mm(picks[at, :], features[...]).astype(out.dtype)
        store = pltpu.make_async_copy(out.at[at, :], out_hbm.at[at, :], sems.at[1 + k])
        store.start()
        stores.append(store)
    for store in stores:
        store.wait()


def local_kernel(
    rows_ref,
    cols_ref,
    count_ref,
    idx_ref,
    tiles_hbm,
    features_hbm,
    out_grad_hbm,
    weight_hbm,
    stale_grad_hbm,
    near_hbm,
    far_hbm,
    agg_hbm,
    hidden_grad_hbm,
    grad_out_hbm,
    tiles,
    features,
    out_grad,
    weight,
    stale_grad,
    near32,
    far32,
    near,
    far,
    scatter,
    agg,
    hidden_grad,
    grad_out,
    sems,
):
    tile = tiles.shape[1]
    own = features.shape[0]
    fetches = copies(
        sems,
        [
            (tiles_hbm, tiles),
            (out_grad_hbm, out_grad),
            (weight_hbm, weight),
            (features_hbm, features),
            (stale_grad_hbm, stale_grad),
        ],
    )
    near32[...] = jnp.zeros_like(near32)
    far32[...] = jnp.zeros_like(far32)
    fetches[0].wait()

    @pl.loop(0, count_ref[0])
    def _(t):
        r = pl.multiple_of(rows_ref[t] * tile, tile)
        c = pl.multiple_of(cols_ref[t] * tile, tile)
        value = tiles[t].astype(jnp.float32)

        @pl.when(c < own)
        def _():
            near32[pl.ds(r, tile), pl.ds(c, tile)] += value

        @pl.when(c >= own)
        def _():
            far32[pl.ds(r, tile), pl.ds(pl.multiple_of(c - own, tile), tile)] += value

    near[...] = near32[...].astype(near.dtype)
    far[...] = far32[...].astype(far.dtype)
    saves = copies(sems.at[pl.ds(5, 2)], [(near, near_hbm), (far, far_hbm)])
    fetches[3].wait()
    agg[...] = mm(near[...], features[...])
    saves += copies(sems.at[pl.ds(7, 1)], [(agg, agg_hbm)])
    fetches[1].wait()
    fetches[2].wait()
    down = mm(out_grad[...], weight[...], ((1,), (1,))).astype(jnp.bfloat16)
    remote = mm(far[...], down, ((0,), (0,)))
    grad_out[...] = remote.reshape(grad_out.shape).astype(grad_out.dtype)
    saves += copies(sems.at[pl.ds(8, 1)], [(grad_out, grad_out_hbm)])
    place = lax.broadcasted_iota(jnp.int32, (own, LANES), 0)
    for j in range(idx_ref.shape[0]):
        across = jnp.broadcast_to(idx_ref[j : j + 1, :], (own, LANES))
        hit = jnp.where(across == place, 1.0, 0.0)
        scatter[:, j * LANES : (j + 1) * LANES] = hit.astype(scatter.dtype)
    fetches[4].wait()
    hidden_grad[...] = mm(near[...], down, ((0,), (0,))) + mm(scatter[...], stale_grad[...])
    saves += copies(sems.at[pl.ds(9, 1)], [(hidden_grad, hidden_grad_hbm)])
    for save in saves:
        save.wait()


def main_kernel(
    core_ref,
    arrived_hbm,
    near_hbm,
    far_hbm,
    agg_hbm,
    weight_hbm,
    hidden_grad_hbm,
    stale_hidden_hbm,
    out_grad_hbm,
    hidden_hbm,
    keep_hbm,
    send_hbm,
    arrived,
    near,
    far,
    agg,
    weight,
    hidden_grad,
    stale_hidden,
    out_grad,
    hidden,
    keep,
    send,
    sems,
):
    own, width = agg.shape
    fetches = copies(
        sems,
        [
            (arrived_hbm, arrived),
            (far_hbm, far),
            (agg_hbm, agg),
            (weight_hbm, weight),
            (stale_hidden_hbm, stale_hidden),
            (near_hbm, near),
            (out_grad_hbm, out_grad),
            (hidden_grad_hbm, hidden_grad),
        ],
    )
    for fetch in fetches[:3]:
        fetch.wait()
    agg_one = (agg[...] + mm(far[...], arrived[:, :width])).astype(jnp.bfloat16)
    fetches[3].wait()
    pre = mm(agg_one, weight[...])
    cdf = 0.5 * (1.0 + lax.erf(pre * INV_SQRT2))
    hidden[...] = (pre * cdf).astype(jnp.bfloat16)
    saves = copies(sems.at[pl.ds(8, 1)], [(hidden, hidden_hbm)])
    fetches[4].wait()
    heard = arrived[:, width:].astype(jnp.float32) > 0.5
    for k in range(width // LANES):
        at = slice(k * LANES, (k + 1) * LANES)
        stale = stale_hidden[:, at].astype(jnp.float32)
        stale_hidden[:, at] = jnp.where(heard, stale, 0.0).astype(stale_hidden.dtype)
    fetches[5].wait()
    agg_two = mm(near[...], hidden[...]) + mm(far[...], stale_hidden[...])
    fetches[6].wait()
    part_two = mm(agg_two.astype(jnp.bfloat16), out_grad[...], ((0,), (0,)))
    slope = cdf + pre * (jnp.exp(-0.5 * pre * pre) * INV_SQRT_2PI)
    fetches[7].wait()
    pre_grad = (hidden_grad[...] * slope).astype(jnp.bfloat16)
    part_one = mm(agg_one, pre_grad, ((0,), (0,)))
    first = core_ref[0] == 0
    for k in range(width // LANES):
        at = slice(k * LANES, (k + 1) * LANES)
        one, two = part_one[:, at], part_two[:, at]
        lines = pl.ds(k * width, width)
        keep[lines, :] = jnp.where(first, one, two)
        send[lines, :] = jnp.where(first, two, one).astype(send.dtype)
    saves += copies(sems.at[pl.ds(9, 2)], [(send, send_hbm), (keep, keep_hbm)])
    for save in saves:
        save.wait()


def box_kernel(idx_ref, hidden_hbm, mail_hbm, hidden, picks, box, sems):
    (fetch,) = copies(sems, [(hidden_hbm, hidden)])
    fill_picks(idx_ref, picks)
    fetch.wait()
    parts, blocks = box.shape[0], hidden.shape[1] // LANES
    slots = box.shape[1] // blocks
    picked = mm(picks[...], hidden[...])
    for k in range(blocks):
        block = picked[:, k * LANES : (k + 1) * LANES].reshape(parts, slots, LANES)
        box[:, k * slots : (k + 1) * slots, :] = block.astype(box.dtype)
    (save,) = copies(sems.at[pl.ds(1, 1)], [(box, mail_hbm.at[:, : box.shape[1], :])])
    save.wait()


def piece_kernel(keep_ref, other_ref, _, mail_hbm, pieces, sems):
    parts, size = pieces.shape[0], pieces.shape[1]
    total = keep_ref[...] + other_ref[...].astype(jnp.float32)
    whole = total.shape[0] // size
    rest = total.shape[0] - whole * size
    pieces[:whole] = total[: whole * size].reshape(whole, size, LANES).astype(pieces.dtype)
    pieces[whole:] = jnp.zeros((parts - whole, size, LANES), pieces.dtype)
    if rest:
        pieces[whole, :rest] = total[whole * size :].astype(pieces.dtype)
    start = mail_hbm.shape[1] - size
    (save,) = copies(sems, [(pieces, mail_hbm.at[:, start:, :])])
    save.wait()


def sum_kernel(n_z, n_py, mail_hbm, out_ref, pieces, sems):
    parts, size = pieces.shape[0], pieces.shape[1]
    start = mail_hbm.shape[1] - size
    (fetch,) = copies(sems, [(mail_hbm.at[:, start:, :], pieces)])
    fetch.wait()
    for c in range(2):
        total = None
        for z in range(n_z):
            first = (z * 2 + c) * n_py
            block = pieces[first : first + n_py].astype(jnp.float32).sum(0)
            total = block if total is None else total + block
        rounded = total.astype(out_ref.dtype)
        out_ref[:, c * size : (c + 1) * size, :] = jnp.broadcast_to(
            rounded[None], (out_ref.shape[0], size, LANES)
        )


def finish_kernel(scale, n_py, core_ref, mine_ref, other_ref, one_ref, two_ref):
    size = mine_ref.shape[1] // 2
    width = one_ref.shape[0]
    lines = width * width // LANES

    def fill(sources):
        for q in range(2 * mine_ref.shape[0]):
            row, py = divmod(q, n_py)
            z, c = divmod(row, 2)
            for g, out_ref in enumerate((one_ref, two_ref)):
                line = q * size
                end = min(line + size, lines)
                while line < end:
                    k, r = divmod(line, width)
                    count = min(end - line, width - r)
                    at = g * size + line - q * size
                    value = sources[c][z * n_py + py, at : at + count, :]
                    out_ref[r : r + count, k * LANES : (k + 1) * LANES] = (
                        value.astype(jnp.float32) * scale
                    )
                    line += count

    @pl.when(core_ref[0] == 0)
    def _():
        fill((mine_ref, other_ref))

    @pl.when(core_ref[0] != 0)
    def _():
        fill((other_ref, mine_ref))


def in_vmem(*refs):
    return [pltpu.VMEM(r.shape, r.dtype) for r in refs]


def call(kernel, out_shape, scalars, scratch=(), vmem=None, limit=6, aliases=None, out=None):
    def run(*args):
        n_vmem = len(args) - scalars if vmem is None else vmem
        size = sum(a.size * a.dtype.itemsize for a in (*args, *jax.tree.leaves(out_shape)))
        out_spec = (VMEM if vmem is None else HBM) if out is None else out
        return pl.pallas_call(
            kernel,
            out_shape=out_shape,
            in_specs=[SMEM] * scalars + [VMEM] * n_vmem + [HBM] * (len(args) - scalars - n_vmem),
            out_specs=jax.tree.map(lambda _: out_spec, out_shape) if out is None else out,
            scratch_shapes=scratch,
            input_output_aliases=aliases or {},
            cost_estimate=pl.CostEstimate(flops=0, transcendentals=0, bytes_accessed=size),
            compiler_params=pltpu.CompilerParams(vmem_limit_bytes=limit * 1024 * 1024),
        )(*args)

    return run


def trade(value, groups=None):
    return lax.all_to_all(
        value, BOTH, split_axis=0, concat_axis=0, tiled=True, axis_index_groups=groups
    )


def sibling(value):
    n = lax.axis_size("px")
    return lax.ppermute(value, "px", [(i, i ^ 1) for i in range(n)])


def local(
    features,
    weight_one,
    weight_two,
    tile_values,
    tile_rows,
    tile_cols,
    tile_count,
    send_rows,
    send_count,
    stale_hidden,
    stale_grad,
    out_grad,
):
    bf16, f32 = jnp.bfloat16, jnp.float32
    parts = lax.axis_size(BOTH)
    own, width = features.shape
    slots = send_rows.shape[2]
    boundary = parts * slots
    shape = jax.ShapeDtypeStruct
    slot_ids = jnp.arange(slots, dtype=jnp.int32)
    core = (lax.axis_index("px") % 2).astype(jnp.int32).reshape(1)
    n_z, n_py = lax.axis_size("px") // 2, lax.axis_size("py")

    pack = shape((boundary, width + LANES), bf16)
    square, square32 = shape((own, width), bf16), shape((own, width), f32)
    near, far = shape((own, own), bf16), shape((own, boundary), bf16)
    near32, far32 = shape((own, own), f32), shape((own, boundary), f32)
    slab, slots_in = shape((boundary, width), bf16), shape((parts, slots, width), bf16)
    weight = shape(weight_one.shape, bf16)
    picks = shape((boundary, own), bf16)
    semaphores = lambda count: [pltpu.SemaphoreType.DMA((count,))]
    lines = width * width // LANES
    keep, send = shape((lines, LANES), f32), shape((lines, LANES), bf16)
    groups = boundary // LANES

    outgoing, idx = call(
        pack_kernel,
        (pack, shape((groups, LANES), jnp.int32)),
        0,
        in_vmem(square, picks, pack) + semaphores(5),
        2,
        PACK,
        None,
        (HBM, VMEM),
    )(send_rows.reshape(groups, LANES), send_count, features)
    arrived = trade(outgoing.reshape(parts, slots, -1)).reshape(boundary, -1)

    near_adj, far_adj, agg, hidden_grad, grad_out = call(
        local_kernel,
        (near, far, square32, square32, slots_in),
        3,
        in_vmem(
            tile_values, square, square, weight, slab, near32, far32, near, far, far, square32, square32, slots_in
        )
        + semaphores(10),
        1,
        LOCAL,
    )(tile_rows[0], tile_cols[0], tile_count, idx, tile_values, features, out_grad, weight_two, stale_grad)

    arrived, grad_out = lax.optimization_barrier((arrived, grad_out))
    grads = trade(grad_out)
    hidden, keep, send = call(
        main_kernel,
        (square, keep, send),
        1,
        in_vmem(pack, near, far, square32, weight, square32, slab, square, square, keep, send)
        + semaphores(11),
        0,
        MAIN,
    )(core, arrived, near_adj, far_adj, agg, weight_one, hidden_grad, stale_hidden, out_grad)

    other = sibling(send)
    size = -(-lines // (parts * 8)) * 8
    rows = slots * width // LANES
    mail = call(
        box_kernel,
        shape((parts, rows + size, LANES), bf16),
        0,
        in_vmem(square, picks, shape((parts, rows, LANES), bf16)) + semaphores(2),
        1,
        BOX,
    )(idx, hidden)
    mail = call(
        piece_kernel,
        shape(mail.shape, bf16),
        0,
        in_vmem(shape((parts, size, LANES), bf16)) + semaphores(1),
        2,
        PIECE,
        {2: 0},
    )(keep, other, mail)
    mail, grads = lax.optimization_barrier((mail, grads))
    mail = trade(mail)
    chips = parts // 2
    mine = call(
        functools.partial(sum_kernel, n_z, n_py),
        shape((chips, 2 * size, LANES), bf16),
        0,
        in_vmem(shape((parts, size, LANES), bf16)) + semaphores(1),
        0,
        SUM,
        None,
        VMEM,
    )(mail)
    same_core = [[(2 * z + c) * n_py + i for z in range(n_z) for i in range(n_py)] for c in range(2)]
    mine = trade(mine, same_core)
    next_hidden = mail[:, :rows].reshape(parts, width // LANES, slots, LANES)
    next_hidden = jnp.swapaxes(next_hidden, 1, 2).reshape(boundary, width)
    sent = slot_ids[None, :] < send_count[0][:, None]
    next_grad = jnp.where(sent[:, :, None], grads, jnp.zeros_like(grads)).reshape(boundary, width)
    mine, next_hidden, next_grad = lax.optimization_barrier((mine, next_hidden, next_grad))
    scale = 1.0 / math.sqrt(own * parts)
    one, two = call(
        functools.partial(finish_kernel, scale, n_py),
        (shape((width, width), f32),) * 2,
        1,
        (),
        None,
        FINISH,
    )(core, mine, sibling(mine))

    return next_hidden, next_grad, one, two


def solution(mesh):
    in_specs = (
        P(BOTH, None),
        P(),
        P(),
        P(BOTH, None, None),
        P(BOTH, None),
        P(BOTH, None),
        P(BOTH),
        P(BOTH, None, None),
        P(BOTH, None),
        P(BOTH, None),
        P(BOTH, None),
        P(BOTH, None),
    )
    out_specs = (P(BOTH, None), P(BOTH, None), P(), P())
    return jax.shard_map(local, mesh=mesh, in_specs=in_specs, out_specs=out_specs, check_vma=False)
```

```python
import functools
import math

import jax
import jax.numpy as jnp
from jax import lax
from jax.experimental import pallas as pl
from jax.experimental.pallas import tpu as pltpu
from jax.sharding import PartitionSpec as P

BOTH = ("px", "py")
LANES = 128
UNUSED = 2.0**126
PACK, LOCAL, MAIN = 58, 63, 56
BOX, PIECE, SUM, FINISH = 63, 63, 63, 16
VMEM = pl.BlockSpec(memory_space=pltpu.VMEM)
HBM = pl.BlockSpec(memory_space=pltpu.HBM)
SMEM = pl.BlockSpec(memory_space=pltpu.SMEM)
INV_SQRT2 = 1.0 / math.sqrt(2.0)
INV_SQRT_2PI = 1.0 / math.sqrt(2.0 * math.pi)


def mm(a, b, dims=((1,), (0,))):
    return lax.dot_general(a, b, (dims, ((), ())), preferred_element_type=jnp.float32)


def copies(sems, pairs):
    started = [
        pltpu.make_async_copy(src, dst, sems.at[i]) for i, (src, dst) in enumerate(pairs)
    ]
    for copy in started:
        copy.start()
    return started


def pack_kernel(
    rows_ref, counts_ref, features_hbm, out_hbm, picks_hbm, features, listed, wanted, picks, out, sems
):
    f32, bf16 = jnp.float32, jnp.bfloat16
    (fetch,) = copies(sems, [(features_hbm, features)])
    parts, slots = rows_ref.shape[1:]
    boundary, own = picks.shape
    counts = jnp.broadcast_to(counts_ref[...], (LANES, parts)).T
    listed[...] = jnp.zeros_like(listed)
    listed[:, :slots] = rows_ref[0] + 1
    lane = lax.broadcasted_iota(jnp.int32, (parts, LANES), 1)
    value = jnp.where(lane < counts, listed[...], 0)
    step = boundary // 4
    slot = lax.broadcasted_iota(jnp.int32, (step, LANES), 0)
    lane = lax.broadcasted_iota(jnp.int32, (step, LANES), 1)
    mine = lane == slot % slots
    ones = jnp.ones((LANES, LANES), bf16)
    across = lax.broadcasted_iota(jnp.int32, (step, own), 1).astype(f32)
    saves = []
    for k in range(4):
        at = pl.ds(k * step, step)
        peer = jnp.where(lane == slot // slots + k * (step // slots), 1.0, 0.0).astype(bf16)
        index = jnp.full((step, LANES), -1.0, f32)
        for part, weight in ((value >> 5, 32.0), (value & 31, 1.0)):
            spread = mm(peer, part.astype(f32).astype(bf16))
            index += weight * mm(jnp.where(mine, spread, 0.0).astype(bf16), ones)
        wanted[at, :] = index
        wide = jnp.concatenate([index] * (own // LANES), axis=1)
        picks[at, :] = jnp.where(wide == across, 1.0, 0.0).astype(bf16)
        saves += copies(sems.at[pl.ds(1 + k, 1)], [(picks.at[at, :], picks_hbm.at[at, :])])
    fetch.wait()
    for k in range(4):
        at = pl.ds(k * step, step)
        row = mm(picks[at, :], features[...])
        unused = wanted[at, :] < 0.0
        for j in range(own // LANES):
            block = slice(j * LANES, (j + 1) * LANES)
            out[at, block] = jnp.where(unused, UNUSED, row[:, block]).astype(bf16)
        saves += copies(sems.at[pl.ds(5 + k, 1)], [(out.at[at, :], out_hbm.at[at, :])])
    for save in saves:
        save.wait()


def local_kernel(
    rows_ref,
    cols_ref,
    count_ref,
    tiles_hbm,
    features_hbm,
    out_grad_hbm,
    weight_hbm,
    stale_grad_hbm,
    picks_hbm,
    near_hbm,
    far_hbm,
    agg_hbm,
    hidden_grad_hbm,
    grad_out_hbm,
    tiles,
    features,
    out_grad,
    weight,
    stale_grad,
    near32,
    far32,
    near,
    far,
    picks,
    agg,
    hidden_grad,
    grad_out,
    sems,
):
    tile = tiles.shape[1]
    own = features.shape[0]
    fetches = copies(
        sems,
        [
            (tiles_hbm, tiles),
            (out_grad_hbm, out_grad),
            (weight_hbm, weight),
            (features_hbm, features),
            (stale_grad_hbm, stale_grad),
            (picks_hbm, picks),
        ],
    )
    near32[...] = jnp.zeros_like(near32)
    far32[...] = jnp.zeros_like(far32)
    fetches[0].wait()

    @pl.loop(0, count_ref[0])
    def _(t):
        r = pl.multiple_of(rows_ref[t] * tile, tile)
        c = pl.multiple_of(cols_ref[t] * tile, tile)
        value = tiles[t].astype(jnp.float32)

        @pl.when(c < own)
        def _():
            near32[pl.ds(r, tile), pl.ds(c, tile)] += value

        @pl.when(c >= own)
        def _():
            far32[pl.ds(r, tile), pl.ds(pl.multiple_of(c - own, tile), tile)] += value

    near[...] = near32[...].astype(near.dtype)
    far[...] = far32[...].astype(far.dtype)
    saves = copies(sems.at[pl.ds(6, 2)], [(near, near_hbm), (far, far_hbm)])
    fetches[3].wait()
    agg[...] = mm(near[...], features[...])
    saves += copies(sems.at[pl.ds(8, 1)], [(agg, agg_hbm)])
    fetches[1].wait()
    fetches[2].wait()
    down = mm(out_grad[...], weight[...], ((1,), (1,))).astype(jnp.bfloat16)
    remote = mm(far[...], down, ((0,), (0,)))
    grad_out[...] = remote.reshape(grad_out.shape).astype(grad_out.dtype)
    saves += copies(sems.at[pl.ds(9, 1)], [(grad_out, grad_out_hbm)])
    fetches[4].wait()
    fetches[5].wait()
    hidden_grad[...] = mm(near[...], down, ((0,), (0,))) + mm(
        picks[...], stale_grad[...], ((0,), (0,))
    )
    saves += copies(sems.at[pl.ds(10, 1)], [(hidden_grad, hidden_grad_hbm)])
    for save in saves:
        save.wait()


def main_kernel(
    core_ref,
    arrived_hbm,
    near_hbm,
    far_hbm,
    agg_hbm,
    weight_hbm,
    hidden_grad_hbm,
    stale_hidden_hbm,
    out_grad_hbm,
    hidden_hbm,
    keep_hbm,
    send_hbm,
    arrived,
    near,
    far,
    agg,
    weight,
    hidden_grad,
    stale_hidden,
    out_grad,
    hidden,
    keep,
    send,
    first_agg,
    pre_grad,
    sems,
):
    own, width = agg.shape
    step = 256
    blocks = own // step
    loads = [(arrived_hbm, arrived)]
    for i in range(blocks):
        at = pl.ds(i * step, step)
        loads += [(far_hbm.at[at, :], far.at[at, :]), (agg_hbm.at[at, :], agg.at[at, :])]
        if i == 0:
            loads += [(weight_hbm, weight)]
    loads += [
        (stale_hidden_hbm, stale_hidden),
        (hidden_grad_hbm, hidden_grad),
        (near_hbm, near),
        (out_grad_hbm, out_grad),
    ]
    fetches = copies(sems, loads)
    n = len(fetches)
    fetches[0].wait()
    fetches[n - 4].wait()
    for k in range(width // LANES):
        at = slice(k * LANES, (k + 1) * LANES)
        came = arrived[:, at].astype(jnp.float32)
        heard = came != UNUSED
        arrived[:, at] = jnp.where(heard, came, 0.0).astype(arrived.dtype)
        stale = stale_hidden[:, at].astype(jnp.float32)
        stale_hidden[:, at] = jnp.where(heard, stale, 0.0).astype(stale_hidden.dtype)
    for i in range(blocks):
        at = pl.ds(i * step, step)
        for fetch in fetches[1:4] if i == 0 else fetches[2 + 2 * i : 4 + 2 * i]:
            fetch.wait()
        agg_one = (agg[at, :] + mm(far[at, :], arrived[...])).astype(jnp.bfloat16)
        first_agg[at, :] = agg_one
        pre = mm(agg_one, weight[...])
        cdf = 0.5 * (1.0 + lax.erf(pre * INV_SQRT2))
        hidden[at, :] = (pre * cdf).astype(jnp.bfloat16)
        slope = cdf + pre * (jnp.exp(-0.5 * pre * pre) * INV_SQRT_2PI)
        if i == 0:
            fetches[n - 3].wait()
        pre_grad[at, :] = (hidden_grad[at, :] * slope).astype(jnp.bfloat16)
    saves = copies(sems.at[pl.ds(n, 1)], [(hidden, hidden_hbm)])
    fetches[n - 2].wait()
    agg_two = (mm(far[...], stale_hidden[...]) + mm(near[...], hidden[...])).astype(jnp.bfloat16)
    fetches[n - 1].wait()
    part_two = mm(agg_two, out_grad[...], ((0,), (0,)))
    part_one = mm(first_agg[...], pre_grad[...], ((0,), (0,)))
    first = core_ref[0] == 0
    for k in range(width // LANES):
        at = slice(k * LANES, (k + 1) * LANES)
        one, two = part_one[:, at], part_two[:, at]
        rows = pl.ds(k * width, width)
        keep[rows, :] = jnp.where(first, one, two)
        send[rows, :] = jnp.where(first, two, one).astype(send.dtype)
        saves += copies(
            sems.at[pl.ds(n + 1 + 2 * k, 2)],
            [(send.at[rows, :], send_hbm.at[rows, :]), (keep.at[rows, :], keep_hbm.at[rows, :])],
        )
    for save in saves:
        save.wait()


def box_kernel(picks_hbm, hidden_hbm, mail_hbm, hidden, picks, box, sems):
    for fetch in copies(sems, [(hidden_hbm, hidden), (picks_hbm, picks)]):
        fetch.wait()
    parts, blocks = box.shape[0], hidden.shape[1] // LANES
    slots = box.shape[1] // blocks
    picked = mm(picks[...], hidden[...])
    for k in range(blocks):
        block = picked[:, k * LANES : (k + 1) * LANES].reshape(parts, slots, LANES)
        box[:, k * slots : (k + 1) * slots, :] = block.astype(box.dtype)
    (save,) = copies(sems.at[pl.ds(2, 1)], [(box, mail_hbm.at[:, : box.shape[1], :])])
    save.wait()


def piece_kernel(keep_ref, other_ref, _, mail_hbm, pieces, sems):
    parts, size = pieces.shape[0], pieces.shape[1]
    total = keep_ref[...] + other_ref[...].astype(jnp.float32)
    whole = total.shape[0] // size
    rest = total.shape[0] - whole * size
    pieces[:whole] = total[: whole * size].reshape(whole, size, LANES).astype(pieces.dtype)
    pieces[whole:] = jnp.zeros((parts - whole, size, LANES), pieces.dtype)
    if rest:
        pieces[whole, :rest] = total[whole * size :].astype(pieces.dtype)
    start = mail_hbm.shape[1] - size
    (save,) = copies(sems, [(pieces, mail_hbm.at[:, start:, :])])
    save.wait()


def sum_kernel(n_z, n_py, mail_hbm, out_ref, pieces, sems):
    parts, size = pieces.shape[0], pieces.shape[1]
    start = mail_hbm.shape[1] - size
    (fetch,) = copies(sems, [(mail_hbm.at[:, start:, :], pieces)])
    fetch.wait()
    for c in range(2):
        total = None
        for z in range(n_z):
            first = (z * 2 + c) * n_py
            block = pieces[first : first + n_py].astype(jnp.float32).sum(0)
            total = block if total is None else total + block
        rounded = total.astype(out_ref.dtype)
        out_ref[:, c * size : (c + 1) * size, :] = jnp.broadcast_to(
            rounded[None], (out_ref.shape[0], size, LANES)
        )


def finish_kernel(scale, n_py, core_ref, mine_ref, other_ref, one_hbm, two_hbm, one, two, sems):
    size = mine_ref.shape[1] // 2
    width = one.shape[0]
    lines = width * width // LANES

    def fill(sources):
        saves = []
        for q in range(2 * mine_ref.shape[0]):
            row, py = divmod(q, n_py)
            z, c = divmod(row, 2)
            line = q * size
            end = min(line + size, lines)
            while line < end:
                k, r = divmod(line, width)
                block = slice(k * LANES, (k + 1) * LANES)
                count = min(end - line, width - r)
                for g, out in enumerate((one, two)):
                    at = g * size + line - q * size
                    value = sources[c][z * n_py + py, at : at + count, :]
                    out[r : r + count, block] = value.astype(jnp.float32) * scale
                line += count
                if r + count == width:
                    saves += copies(
                        sems.at[pl.ds(2 * k, 2)],
                        [(one.at[:, block], one_hbm.at[:, block]), (two.at[:, block], two_hbm.at[:, block])],
                    )
        for save in saves:
            save.wait()

    @pl.when(core_ref[0] == 0)
    def _():
        fill((mine_ref, other_ref))

    @pl.when(core_ref[0] != 0)
    def _():
        fill((other_ref, mine_ref))


def in_vmem(*refs):
    return [pltpu.VMEM(r.shape, r.dtype) for r in refs]


def call(kernel, out_shape, scalars, scratch=(), vmem=None, limit=6, aliases=None, out=None):
    def run(*args):
        n_vmem = len(args) - scalars if vmem is None else vmem
        size = sum(a.size * a.dtype.itemsize for a in (*args, *jax.tree.leaves(out_shape)))
        out_spec = (VMEM if vmem is None else HBM) if out is None else out
        return pl.pallas_call(
            kernel,
            out_shape=out_shape,
            in_specs=[SMEM] * scalars + [VMEM] * n_vmem + [HBM] * (len(args) - scalars - n_vmem),
            out_specs=jax.tree.map(lambda _: out_spec, out_shape),
            scratch_shapes=scratch,
            input_output_aliases=aliases or {},
            cost_estimate=pl.CostEstimate(flops=0, transcendentals=0, bytes_accessed=size),
            compiler_params=pltpu.CompilerParams(vmem_limit_bytes=limit * 1024 * 1024),
        )(*args)

    return run


def trade(value, groups=None):
    return lax.all_to_all(
        value, BOTH, split_axis=0, concat_axis=0, tiled=True, axis_index_groups=groups
    )


def sibling(value):
    n = lax.axis_size("px")
    return lax.ppermute(value, "px", [(i, i ^ 1) for i in range(n)])


def local(
    features,
    weight_one,
    weight_two,
    tile_values,
    tile_rows,
    tile_cols,
    tile_count,
    send_rows,
    send_count,
    stale_hidden,
    stale_grad,
    out_grad,
):
    bf16, f32 = jnp.bfloat16, jnp.float32
    parts = lax.axis_size(BOTH)
    own, width = features.shape
    slots = send_rows.shape[2]
    boundary = parts * slots
    shape = jax.ShapeDtypeStruct
    slot_ids = jnp.arange(slots, dtype=jnp.int32)
    core = (lax.axis_index("px") % 2).astype(jnp.int32).reshape(1)
    n_z, n_py = lax.axis_size("px") // 2, lax.axis_size("py")

    square, square32 = shape((own, width), bf16), shape((own, width), f32)
    near, far = shape((own, own), bf16), shape((own, boundary), bf16)
    near32, far32 = shape((own, own), f32), shape((own, boundary), f32)
    slab, slots_in = shape((boundary, width), bf16), shape((parts, slots, width), bf16)
    weight = shape(weight_one.shape, bf16)
    picks = shape((boundary, own), bf16)
    semaphores = lambda count: [pltpu.SemaphoreType.DMA((count,))]
    lines = width * width // LANES
    keep, send = shape((lines, LANES), f32), shape((lines, LANES), bf16)

    outgoing, picked = call(
        pack_kernel,
        (slab, picks),
        0,
        in_vmem(
            square, shape((parts, LANES), jnp.int32), shape((boundary, LANES), f32), picks, slab
        )
        + semaphores(9),
        2,
        PACK,
    )(send_rows, send_count, features)
    arrived = trade(outgoing.reshape(parts, slots, -1)).reshape(boundary, -1)

    near_adj, far_adj, agg, hidden_grad, grad_out = call(
        local_kernel,
        (near, far, square32, square32, slots_in),
        3,
        in_vmem(
            tile_values, square, square, weight, slab, near32, far32, near, far, picks, square32, square32, slots_in
        )
        + semaphores(11),
        0,
        LOCAL,
    )(tile_rows[0], tile_cols[0], tile_count, tile_values, features, out_grad, weight_two, stale_grad, picked)

    arrived, grad_out = lax.optimization_barrier((arrived, grad_out))
    grads = trade(grad_out)
    hidden, keep, send = call(
        main_kernel,
        (square, keep, send),
        1,
        in_vmem(
            slab, near, far, square32, weight, square32, slab, square, square, keep, send, square, square
        )
        + semaphores(32),
        0,
        MAIN,
    )(core, arrived, near_adj, far_adj, agg, weight_one, hidden_grad, stale_hidden, out_grad)

    other = sibling(send)
    size = -(-lines // (parts * 8)) * 8
    rows = slots * width // LANES
    mail = call(
        box_kernel,
        shape((parts, rows + size, LANES), bf16),
        0,
        in_vmem(square, picks, shape((parts, rows, LANES), bf16)) + semaphores(3),
        0,
        BOX,
    )(picked, hidden)
    mail = call(
        piece_kernel,
        shape(mail.shape, bf16),
        0,
        in_vmem(shape((parts, size, LANES), bf16)) + semaphores(1),
        2,
        PIECE,
        {2: 0},
    )(keep, other, mail)
    mail, grads = lax.optimization_barrier((mail, grads))
    mail = trade(mail)
    chips = parts // 2
    mine = call(
        functools.partial(sum_kernel, n_z, n_py),
        shape((chips, 2 * size, LANES), bf16),
        0,
        in_vmem(shape((parts, size, LANES), bf16)) + semaphores(1),
        0,
        SUM,
        None,
        VMEM,
    )(mail)
    same_core = [[(2 * z + c) * n_py + i for z in range(n_z) for i in range(n_py)] for c in range(2)]
    mine = trade(mine, same_core)
    next_hidden = mail[:, :rows].reshape(parts, width // LANES, slots, LANES)
    next_hidden = jnp.swapaxes(next_hidden, 1, 2).reshape(boundary, width)
    sent = slot_ids[None, :] < send_count[0][:, None]
    next_grad = jnp.where(sent[:, :, None], grads, jnp.zeros_like(grads)).reshape(boundary, width)
    mine, next_hidden, next_grad = lax.optimization_barrier((mine, next_hidden, next_grad))
    scale = 1.0 / math.sqrt(own * parts)
    one, two = call(
        functools.partial(finish_kernel, scale, n_py),
        (shape((width, width), f32),) * 2,
        1,
        in_vmem(*(shape((width, width), f32),) * 2) + semaphores(2 * (width // LANES)),
        None,
        FINISH,
        None,
        HBM,
    )(core, mine, sibling(mine))

    return next_hidden, next_grad, one, two


def solution(mesh):
    in_specs = (
        P(BOTH, None),
        P(),
        P(),
        P(BOTH, None, None),
        P(BOTH, None),
        P(BOTH, None),
        P(BOTH),
        P(BOTH, None, None),
        P(BOTH, None),
        P(BOTH, None),
        P(BOTH, None),
        P(BOTH, None),
    )
    out_specs = (P(BOTH, None), P(BOTH, None), P(), P())
    return jax.shard_map(local, mesh=mesh, in_specs=in_specs, out_specs=out_specs, check_vma=False)
```

```python
import functools
import math

import jax
import jax.numpy as jnp
from jax import lax
from jax.experimental import pallas as pl
from jax.experimental.pallas import tpu as pltpu
from jax.sharding import PartitionSpec as P

BOTH = ("px", "py")
LANES = 128
UNUSED = 2.0**126
PACK, LOCAL, MAIN = 58, 63, 56
BOX, PIECE, SUM, FINISH = 20, 12, 8, 16
VMEM = pl.BlockSpec(memory_space=pltpu.VMEM)
HBM = pl.BlockSpec(memory_space=pltpu.HBM)
SMEM = pl.BlockSpec(memory_space=pltpu.SMEM)
INV_SQRT2 = 1.0 / math.sqrt(2.0)
INV_SQRT_2PI = 1.0 / math.sqrt(2.0 * math.pi)


def mm(a, b, dims=((1,), (0,))):
    return lax.dot_general(a, b, (dims, ((), ())), preferred_element_type=jnp.float32)


def copies(sems, pairs):
    started = [
        pltpu.make_async_copy(src, dst, sems.at[i]) for i, (src, dst) in enumerate(pairs)
    ]
    for copy in started:
        copy.start()
    return started


def pack_kernel(
    rows_ref, counts_ref, features_hbm, out_hbm, picks_hbm, features, listed, wanted, picks, out, sems
):
    f32, bf16 = jnp.float32, jnp.bfloat16
    (fetch,) = copies(sems, [(features_hbm, features)])
    slots, parts = rows_ref.shape
    boundary, own = picks.shape
    listed[...] = jnp.zeros_like(listed)
    place = lax.broadcasted_iota(jnp.int32, (slots, parts), 0)
    counts = jnp.broadcast_to(counts_ref[...], (slots, parts))
    listed[:slots, :] = jnp.where(place < counts, rows_ref[...] + 1, 0)
    value = listed[...]
    step = boundary // 4
    slot = lax.broadcasted_iota(jnp.int32, (step, LANES), 0)
    lane = lax.broadcasted_iota(jnp.int32, (step, LANES), 1)
    mine = lane == slot % slots
    ones = jnp.ones((LANES, LANES), bf16)
    across = lax.broadcasted_iota(jnp.int32, (step, own), 1).astype(f32)
    saves = []
    for k in range(4):
        at = pl.ds(k * step, step)
        peer = jnp.where(lane == slot // slots + k * (step // slots), 1.0, 0.0).astype(bf16)
        index = jnp.full((step, LANES), -1.0, f32)
        for part, weight in ((value >> 5, 32.0), (value & 31, 1.0)):
            spread = mm(peer, part.astype(f32).astype(bf16), ((1,), (1,)))
            index += weight * mm(jnp.where(mine, spread, 0.0).astype(bf16), ones)
        wanted[at, :] = index
        wide = jnp.concatenate([index] * (own // LANES), axis=1)
        picks[at, :] = jnp.where(wide == across, 1.0, 0.0).astype(bf16)
        saves += copies(sems.at[pl.ds(1 + k, 1)], [(picks.at[at, :], picks_hbm.at[at, :])])
    fetch.wait()
    for k in range(4):
        at = pl.ds(k * step, step)
        row = mm(picks[at, :], features[...])
        unused = wanted[at, :] < 0.0
        for j in range(own // LANES):
            block = slice(j * LANES, (j + 1) * LANES)
            out[at, block] = jnp.where(unused, UNUSED, row[:, block]).astype(bf16)
        saves += copies(sems.at[pl.ds(5 + k, 1)], [(out.at[at, :], out_hbm.at[at, :])])
    for save in saves:
        save.wait()


def local_kernel(
    rows_ref,
    cols_ref,
    count_ref,
    tiles_hbm,
    features_hbm,
    out_grad_hbm,
    weight_hbm,
    stale_grad_hbm,
    picks_hbm,
    near_hbm,
    far_hbm,
    agg_hbm,
    hidden_grad_hbm,
    grad_out_hbm,
    tiles,
    features,
    out_grad,
    weight,
    stale_grad,
    near32,
    far32,
    near,
    far,
    picks,
    agg,
    hidden_grad,
    grad_out,
    sems,
):
    tile = tiles.shape[1]
    own = features.shape[0]
    fetches = copies(
        sems,
        [
            (tiles_hbm, tiles),
            (out_grad_hbm, out_grad),
            (weight_hbm, weight),
            (features_hbm, features),
            (stale_grad_hbm, stale_grad),
            (picks_hbm, picks),
        ],
    )
    near32[...] = jnp.zeros_like(near32)
    far32[...] = jnp.zeros_like(far32)
    fetches[0].wait()

    @pl.loop(0, count_ref[0])
    def _(t):
        r = pl.multiple_of(rows_ref[t] * tile, tile)
        c = pl.multiple_of(cols_ref[t] * tile, tile)
        value = tiles[t].astype(jnp.float32)

        @pl.when(c < own)
        def _():
            near32[pl.ds(r, tile), pl.ds(c, tile)] += value

        @pl.when(c >= own)
        def _():
            far32[pl.ds(r, tile), pl.ds(pl.multiple_of(c - own, tile), tile)] += value

    near[...] = near32[...].astype(near.dtype)
    far[...] = far32[...].astype(far.dtype)
    saves = copies(sems.at[pl.ds(6, 2)], [(near, near_hbm), (far, far_hbm)])
    fetches[3].wait()
    agg[...] = mm(near[...], features[...])
    saves += copies(sems.at[pl.ds(8, 1)], [(agg, agg_hbm)])
    fetches[1].wait()
    fetches[2].wait()
    down = mm(out_grad[...], weight[...], ((1,), (1,))).astype(jnp.bfloat16)
    remote = mm(far[...], down, ((0,), (0,)))
    grad_out[...] = remote.reshape(grad_out.shape).astype(grad_out.dtype)
    saves += copies(sems.at[pl.ds(9, 1)], [(grad_out, grad_out_hbm)])
    fetches[4].wait()
    fetches[5].wait()
    hidden_grad[...] = mm(near[...], down, ((0,), (0,))) + mm(
        picks[...], stale_grad[...], ((0,), (0,))
    )
    saves += copies(sems.at[pl.ds(10, 1)], [(hidden_grad, hidden_grad_hbm)])
    for save in saves:
        save.wait()


def main_kernel(
    core_ref,
    arrived_hbm,
    near_hbm,
    far_hbm,
    agg_hbm,
    weight_hbm,
    hidden_grad_hbm,
    stale_hidden_hbm,
    out_grad_hbm,
    hidden_hbm,
    keep_hbm,
    send_hbm,
    arrived,
    near,
    far,
    agg,
    weight,
    hidden_grad,
    stale_hidden,
    out_grad,
    hidden,
    keep,
    send,
    first_agg,
    pre_grad,
    sems,
):
    own, width = agg.shape
    step = 256
    blocks = own // step
    loads = [(arrived_hbm, arrived)]
    for i in range(blocks):
        at = pl.ds(i * step, step)
        loads += [(far_hbm.at[at, :], far.at[at, :]), (agg_hbm.at[at, :], agg.at[at, :])]
        if i == 0:
            loads += [(weight_hbm, weight)]
    loads += [
        (stale_hidden_hbm, stale_hidden),
        (hidden_grad_hbm, hidden_grad),
        (near_hbm, near),
        (out_grad_hbm, out_grad),
    ]
    fetches = copies(sems, loads)
    n = len(fetches)
    fetches[0].wait()
    fetches[n - 4].wait()
    for k in range(width // LANES):
        at = slice(k * LANES, (k + 1) * LANES)
        came = arrived[:, at].astype(jnp.float32)
        heard = came != UNUSED
        arrived[:, at] = jnp.where(heard, came, 0.0).astype(arrived.dtype)
        stale = stale_hidden[:, at].astype(jnp.float32)
        stale_hidden[:, at] = jnp.where(heard, stale, 0.0).astype(stale_hidden.dtype)
    for i in range(blocks):
        at = pl.ds(i * step, step)
        for fetch in fetches[1:4] if i == 0 else fetches[2 + 2 * i : 4 + 2 * i]:
            fetch.wait()
        agg_one = (agg[at, :] + mm(far[at, :], arrived[...])).astype(jnp.bfloat16)
        first_agg[at, :] = agg_one
        pre = mm(agg_one, weight[...])
        cdf = 0.5 * (1.0 + lax.erf(pre * INV_SQRT2))
        hidden[at, :] = (pre * cdf).astype(jnp.bfloat16)
        slope = cdf + pre * (jnp.exp(-0.5 * pre * pre) * INV_SQRT_2PI)
        if i == 0:
            fetches[n - 3].wait()
        pre_grad[at, :] = (hidden_grad[at, :] * slope).astype(jnp.bfloat16)
    saves = copies(sems.at[pl.ds(n, 1)], [(hidden, hidden_hbm)])
    fetches[n - 2].wait()
    agg_two = (mm(far[...], stale_hidden[...]) + mm(near[...], hidden[...])).astype(jnp.bfloat16)
    fetches[n - 1].wait()
    part_two = mm(agg_two, out_grad[...], ((0,), (0,)))
    part_one = mm(first_agg[...], pre_grad[...], ((0,), (0,)))
    first = core_ref[0] == 0
    for k in range(width // LANES):
        at = slice(k * LANES, (k + 1) * LANES)
        one, two = part_one[:, at], part_two[:, at]
        rows = pl.ds(k * width, width)
        keep[rows, :] = jnp.where(first, one, two)
        send[rows, :] = jnp.where(first, two, one).astype(send.dtype)
        saves += copies(
            sems.at[pl.ds(n + 1 + 2 * k, 2)],
            [(send.at[rows, :], send_hbm.at[rows, :]), (keep.at[rows, :], keep_hbm.at[rows, :])],
        )
    for save in saves:
        save.wait()


def box_kernel(picks_hbm, hidden_hbm, mail_hbm, hidden, picks, box, sems):
    for fetch in copies(sems, [(hidden_hbm, hidden), (picks_hbm, picks)]):
        fetch.wait()
    parts, blocks = box.shape[0], hidden.shape[1] // LANES
    slots = box.shape[1] // blocks
    picked = mm(picks[...], hidden[...])
    for k in range(blocks):
        block = picked[:, k * LANES : (k + 1) * LANES].reshape(parts, slots, LANES)
        box[:, k * slots : (k + 1) * slots, :] = block.astype(box.dtype)
    (save,) = copies(sems.at[pl.ds(2, 1)], [(box, mail_hbm.at[:, : box.shape[1], :])])
    save.wait()


def piece_kernel(keep_ref, other_ref, _, mail_hbm, pieces, sems):
    parts, size = pieces.shape[0], pieces.shape[1]
    total = keep_ref[...] + other_ref[...].astype(jnp.float32)
    whole = total.shape[0] // size
    rest = total.shape[0] - whole * size
    pieces[:whole] = total[: whole * size].reshape(whole, size, LANES).astype(pieces.dtype)
    pieces[whole:] = jnp.zeros((parts - whole, size, LANES), pieces.dtype)
    if rest:
        pieces[whole, :rest] = total[whole * size :].astype(pieces.dtype)
    start = mail_hbm.shape[1] - size
    (save,) = copies(sems, [(pieces, mail_hbm.at[:, start:, :])])
    save.wait()


def sum_kernel(n_z, n_py, mail_ref, out_ref, hidden_hbm, sems):
    parts, slots, width = hidden_hbm.shape
    size = out_ref.shape[1] // 2
    start = mail_ref.shape[1] - size
    saves = copies(
        sems,
        [
            (mail_ref.at[:, pl.ds(k * slots, slots), :], hidden_hbm.at[:, :, pl.ds(k * LANES, LANES)])
            for k in range(width // LANES)
        ],
    )
    for c in range(2):
        total = None
        for z in range(n_z):
            first = (z * 2 + c) * n_py
            block = mail_ref[first : first + n_py, start:, :].astype(jnp.float32).sum(0)
            total = block if total is None else total + block
        rounded = total.astype(out_ref.dtype)
        out_ref[:, c * size : (c + 1) * size, :] = jnp.broadcast_to(
            rounded[None], (out_ref.shape[0], size, LANES)
        )
    for save in saves:
        save.wait()


def finish_kernel(scale, n_py, core_ref, mine_ref, other_ref, one_hbm, two_hbm, one, two, sems):
    size = mine_ref.shape[1] // 2
    width = one.shape[0]
    lines = width * width // LANES

    def fill(sources):
        saves = []
        for q in range(2 * mine_ref.shape[0]):
            row, py = divmod(q, n_py)
            z, c = divmod(row, 2)
            line = q * size
            end = min(line + size, lines)
            while line < end:
                k, r = divmod(line, width)
                block = slice(k * LANES, (k + 1) * LANES)
                count = min(end - line, width - r)
                for g, out in enumerate((one, two)):
                    at = g * size + line - q * size
                    value = sources[c][z * n_py + py, at : at + count, :]
                    out[r : r + count, block] = value.astype(jnp.float32) * scale
                line += count
                if r + count == width:
                    saves += copies(
                        sems.at[pl.ds(2 * k, 2)],
                        [(one.at[:, block], one_hbm.at[:, block]), (two.at[:, block], two_hbm.at[:, block])],
                    )
        for save in saves:
            save.wait()

    @pl.when(core_ref[0] == 0)
    def _():
        fill((mine_ref, other_ref))

    @pl.when(core_ref[0] != 0)
    def _():
        fill((other_ref, mine_ref))


def in_vmem(*refs):
    return [pltpu.VMEM(r.shape, r.dtype) for r in refs]


def call(kernel, out_shape, scalars, scratch=(), vmem=None, limit=6, aliases=None, out=None):
    def run(*args):
        n_vmem = len(args) - scalars if vmem is None else vmem
        size = sum(a.size * a.dtype.itemsize for a in (*args, *jax.tree.leaves(out_shape)))
        out_spec = (VMEM if vmem is None else HBM) if out is None else out
        return pl.pallas_call(
            kernel,
            out_shape=out_shape,
            in_specs=[SMEM] * scalars + [VMEM] * n_vmem + [HBM] * (len(args) - scalars - n_vmem),
            out_specs=out_spec if isinstance(out, tuple) else jax.tree.map(lambda _: out_spec, out_shape),
            scratch_shapes=scratch,
            input_output_aliases=aliases or {},
            cost_estimate=pl.CostEstimate(flops=0, transcendentals=0, bytes_accessed=size),
            compiler_params=pltpu.CompilerParams(vmem_limit_bytes=limit * 1024 * 1024),
        )(*args)

    return run


def trade(value, groups=None):
    return lax.all_to_all(
        value, BOTH, split_axis=0, concat_axis=0, tiled=True, axis_index_groups=groups
    )


def sibling(value):
    n = lax.axis_size("px")
    return lax.ppermute(value, "px", [(i, i ^ 1) for i in range(n)])


def local(
    features,
    weight_one,
    weight_two,
    tile_values,
    tile_rows,
    tile_cols,
    tile_count,
    send_rows,
    send_count,
    stale_hidden,
    stale_grad,
    out_grad,
):
    bf16, f32 = jnp.bfloat16, jnp.float32
    parts = lax.axis_size(BOTH)
    own, width = features.shape
    slots = send_rows.shape[2]
    boundary = parts * slots
    shape = jax.ShapeDtypeStruct
    slot_ids = jnp.arange(slots, dtype=jnp.int32)
    core = (lax.axis_index("px") % 2).astype(jnp.int32).reshape(1)
    n_z, n_py = lax.axis_size("px") // 2, lax.axis_size("py")

    square, square32 = shape((own, width), bf16), shape((own, width), f32)
    near, far = shape((own, own), bf16), shape((own, boundary), bf16)
    near32, far32 = shape((own, own), f32), shape((own, boundary), f32)
    slab, slots_in = shape((boundary, width), bf16), shape((parts, slots, width), bf16)
    weight = shape(weight_one.shape, bf16)
    picks = shape((boundary, own), bf16)
    semaphores = lambda count: [pltpu.SemaphoreType.DMA((count,))]
    lines = width * width // LANES
    keep, send = shape((lines, LANES), f32), shape((lines, LANES), bf16)

    outgoing, picked = call(
        pack_kernel,
        (slab, picks),
        0,
        in_vmem(
            square, shape((LANES, parts), jnp.int32), shape((boundary, LANES), f32), picks, slab
        )
        + semaphores(9),
        2,
        PACK,
    )(send_rows[0].T, send_count, features)
    arrived = trade(outgoing.reshape(parts, slots, -1)).reshape(boundary, -1)

    near_adj, far_adj, agg, hidden_grad, grad_out = call(
        local_kernel,
        (near, far, square32, square32, slots_in),
        3,
        in_vmem(
            tile_values, square, square, weight, slab, near32, far32, near, far, picks, square32, square32, slots_in
        )
        + semaphores(11),
        0,
        LOCAL,
    )(tile_rows[0], tile_cols[0], tile_count, tile_values, features, out_grad, weight_two, stale_grad, picked)

    arrived, grad_out = lax.optimization_barrier((arrived, grad_out))
    grads = trade(grad_out)
    hidden, keep, send = call(
        main_kernel,
        (square, keep, send),
        1,
        in_vmem(
            slab, near, far, square32, weight, square32, slab, square, square, keep, send, square, square
        )
        + semaphores(32),
        0,
        MAIN,
    )(core, arrived, near_adj, far_adj, agg, weight_one, hidden_grad, stale_hidden, out_grad)

    other = sibling(send)
    size = -(-lines // (parts * 8)) * 8
    rows = slots * width // LANES
    mail = call(
        box_kernel,
        shape((parts, rows + size, LANES), bf16),
        0,
        in_vmem(square, picks, shape((parts, rows, LANES), bf16)) + semaphores(3),
        0,
        BOX,
    )(picked, hidden)
    mail = call(
        piece_kernel,
        shape(mail.shape, bf16),
        0,
        in_vmem(shape((parts, size, LANES), bf16)) + semaphores(1),
        2,
        PIECE,
        {2: 0},
    )(keep, other, mail)
    mail, grads = lax.optimization_barrier((mail, grads))
    mail = trade(mail)
    chips = parts // 2
    mine, next_hidden = call(
        functools.partial(sum_kernel, n_z, n_py),
        (shape((chips, 2 * size, LANES), bf16), slots_in),
        0,
        semaphores(width // LANES),
        1,
        SUM,
        None,
        (VMEM, HBM),
    )(mail)
    next_hidden = next_hidden.reshape(boundary, width)
    same_core = [[(2 * z + c) * n_py + i for z in range(n_z) for i in range(n_py)] for c in range(2)]
    mine = trade(mine, same_core)
    sent = slot_ids[None, :] < send_count[0][:, None]
    next_grad = jnp.where(sent[:, :, None], grads, jnp.zeros_like(grads)).reshape(boundary, width)
    mine, next_grad = lax.optimization_barrier((mine, next_grad))
    scale = 1.0 / math.sqrt(own * parts)
    one, two = call(
        functools.partial(finish_kernel, scale, n_py),
        (shape((width, width), f32),) * 2,
        1,
        in_vmem(*(shape((width, width), f32),) * 2) + semaphores(2 * (width // LANES)),
        None,
        FINISH,
        None,
        HBM,
    )(core, mine, sibling(mine))

    return next_hidden, next_grad, one, two


def solution(mesh):
    in_specs = (
        P(BOTH, None),
        P(),
        P(),
        P(BOTH, None, None),
        P(BOTH, None),
        P(BOTH, None),
        P(BOTH),
        P(BOTH, None, None),
        P(BOTH, None),
        P(BOTH, None),
        P(BOTH, None),
        P(BOTH, None),
    )
    out_specs = (P(BOTH, None), P(BOTH, None), P(), P())
    return jax.shard_map(local, mesh=mesh, in_specs=in_specs, out_specs=out_specs, check_vma=False)
```

```python
import functools
import math

import jax
import jax.numpy as jnp
from jax import lax
from jax.experimental import pallas as pl
from jax.experimental.pallas import tpu as pltpu
from jax.sharding import PartitionSpec as P

BOTH = ("px", "py")
LANES = 128
UNUSED = 2.0**126
PACK, LOCAL, MAIN = 58, 63, 56
BOX, PIECE, SUM, FINISH = 20, 12, 8, 16
VMEM = pl.BlockSpec(memory_space=pltpu.VMEM)
HBM = pl.BlockSpec(memory_space=pltpu.HBM)
SMEM = pl.BlockSpec(memory_space=pltpu.SMEM)
INV_SQRT2 = 1.0 / math.sqrt(2.0)
INV_SQRT_2PI = 1.0 / math.sqrt(2.0 * math.pi)


def mm(a, b, dims=((1,), (0,))):
    return lax.dot_general(a, b, (dims, ((), ())), preferred_element_type=jnp.float32)


def copies(sems, pairs):
    started = [
        pltpu.make_async_copy(src, dst, sems.at[i]) for i, (src, dst) in enumerate(pairs)
    ]
    for copy in started:
        copy.start()
    return started


def pack_kernel(
    rows_ref, counts_ref, features_hbm, out_hbm, picks_hbm, features, listed, wanted, picks, out, sems
):
    f32, bf16 = jnp.float32, jnp.bfloat16
    (fetch,) = copies(sems, [(features_hbm, features)])
    slots, parts = rows_ref.shape
    boundary, own = picks.shape
    listed[...] = jnp.zeros_like(listed)
    place = lax.broadcasted_iota(jnp.int32, (slots, parts), 0)
    counts = jnp.broadcast_to(counts_ref[...], (slots, parts))
    listed[:slots, :] = jnp.where(place < counts, rows_ref[...] + 1, 0)
    value = listed[...]
    step = boundary // 4
    slot = lax.broadcasted_iota(jnp.int32, (step, LANES), 0)
    lane = lax.broadcasted_iota(jnp.int32, (step, LANES), 1)
    mine = lane == slot % slots
    ones = jnp.ones((LANES, LANES), bf16)
    across = lax.broadcasted_iota(jnp.int32, (step, own), 1).astype(f32)
    saves = []
    for k in range(4):
        at = pl.ds(k * step, step)
        peer = jnp.where(lane == slot // slots + k * (step // slots), 1.0, 0.0).astype(bf16)
        index = jnp.full((step, LANES), -1.0, f32)
        for part, weight in ((value >> 5, 32.0), (value & 31, 1.0)):
            spread = mm(peer, part.astype(f32).astype(bf16), ((1,), (1,)))
            index += weight * mm(jnp.where(mine, spread, 0.0).astype(bf16), ones)
        wanted[at, :] = index
        wide = jnp.concatenate([index] * (own // LANES), axis=1)
        picks[at, :] = jnp.where(wide == across, 1.0, 0.0).astype(bf16)
        saves += copies(sems.at[pl.ds(1 + k, 1)], [(picks.at[at, :], picks_hbm.at[at, :])])
    fetch.wait()
    for k in range(4):
        at = pl.ds(k * step, step)
        row = mm(picks[at, :], features[...])
        unused = wanted[at, :] < 0.0
        for j in range(own // LANES):
            block = slice(j * LANES, (j + 1) * LANES)
            out[at, block] = jnp.where(unused, UNUSED, row[:, block]).astype(bf16)
        saves += copies(sems.at[pl.ds(5 + k, 1)], [(out.at[at, :], out_hbm.at[at, :])])
    for save in saves:
        save.wait()


def local_kernel(
    rows_ref,
    cols_ref,
    count_ref,
    tiles_hbm,
    features_hbm,
    out_grad_hbm,
    weight_hbm,
    stale_grad_hbm,
    picks_hbm,
    near_hbm,
    far_hbm,
    agg_hbm,
    hidden_grad_hbm,
    grad_out_hbm,
    tiles,
    features,
    out_grad,
    weight,
    stale_grad,
    near32,
    far32,
    near,
    far,
    picks,
    agg,
    hidden_grad,
    grad_out,
    sems,
):
    tile = tiles.shape[1]
    own = features.shape[0]
    fetches = copies(
        sems,
        [
            (tiles_hbm, tiles),
            (out_grad_hbm, out_grad),
            (weight_hbm, weight),
            (features_hbm, features),
            (stale_grad_hbm, stale_grad),
            (picks_hbm, picks),
        ],
    )
    near32[...] = jnp.zeros_like(near32)
    far32[...] = jnp.zeros_like(far32)
    fetches[0].wait()

    @pl.loop(0, count_ref[0])
    def _(t):
        r = pl.multiple_of(rows_ref[t] * tile, tile)
        c = pl.multiple_of(cols_ref[t] * tile, tile)
        value = tiles[t].astype(jnp.float32)

        @pl.when(c < own)
        def _():
            near32[pl.ds(r, tile), pl.ds(c, tile)] += value

        @pl.when(c >= own)
        def _():
            far32[pl.ds(r, tile), pl.ds(pl.multiple_of(c - own, tile), tile)] += value

    near[...] = near32[...].astype(near.dtype)
    far[...] = far32[...].astype(far.dtype)
    saves = copies(sems.at[pl.ds(6, 2)], [(near, near_hbm), (far, far_hbm)])
    fetches[3].wait()
    agg[...] = mm(near[...], features[...])
    saves += copies(sems.at[pl.ds(8, 1)], [(agg, agg_hbm)])
    fetches[1].wait()
    fetches[2].wait()
    down = mm(out_grad[...], weight[...], ((1,), (1,))).astype(jnp.bfloat16)
    remote = mm(far[...], down, ((0,), (0,)))
    grad_out[...] = remote.reshape(grad_out.shape).astype(grad_out.dtype)
    saves += copies(sems.at[pl.ds(9, 1)], [(grad_out, grad_out_hbm)])
    fetches[4].wait()
    fetches[5].wait()
    hidden_grad[...] = mm(near[...], down, ((0,), (0,))) + mm(
        picks[...], stale_grad[...], ((0,), (0,))
    )
    saves += copies(sems.at[pl.ds(10, 1)], [(hidden_grad, hidden_grad_hbm)])
    for save in saves:
        save.wait()


def main_kernel(
    core_ref,
    arrived_hbm,
    near_hbm,
    far_hbm,
    agg_hbm,
    weight_hbm,
    hidden_grad_hbm,
    stale_hidden_hbm,
    out_grad_hbm,
    hidden_hbm,
    keep_hbm,
    send_hbm,
    arrived,
    near,
    far,
    agg,
    weight,
    hidden_grad,
    stale_hidden,
    out_grad,
    hidden,
    keep,
    send,
    first_agg,
    pre_grad,
    sems,
):
    own, width = agg.shape
    step = 256
    blocks = own // step
    loads = [(arrived_hbm, arrived)]
    for i in range(blocks):
        at = pl.ds(i * step, step)
        loads += [(far_hbm.at[at, :], far.at[at, :]), (agg_hbm.at[at, :], agg.at[at, :])]
        if i == 0:
            loads += [(weight_hbm, weight)]
    loads += [
        (stale_hidden_hbm, stale_hidden),
        (hidden_grad_hbm, hidden_grad),
        (near_hbm, near),
        (out_grad_hbm, out_grad),
    ]
    fetches = copies(sems, loads)
    n = len(fetches)
    fetches[0].wait()
    fetches[n - 4].wait()
    for k in range(width // LANES):
        at = slice(k * LANES, (k + 1) * LANES)
        came = arrived[:, at].astype(jnp.float32)
        heard = came != UNUSED
        arrived[:, at] = jnp.where(heard, came, 0.0).astype(arrived.dtype)
        stale = stale_hidden[:, at].astype(jnp.float32)
        stale_hidden[:, at] = jnp.where(heard, stale, 0.0).astype(stale_hidden.dtype)
    for i in range(blocks):
        at = pl.ds(i * step, step)
        for fetch in fetches[1:4] if i == 0 else fetches[2 + 2 * i : 4 + 2 * i]:
            fetch.wait()
        agg_one = (agg[at, :] + mm(far[at, :], arrived[...])).astype(jnp.bfloat16)
        first_agg[at, :] = agg_one
        pre = mm(agg_one, weight[...])
        cdf = 0.5 * (1.0 + lax.erf(pre * INV_SQRT2))
        hidden[at, :] = (pre * cdf).astype(jnp.bfloat16)
        slope = cdf + pre * (jnp.exp(-0.5 * pre * pre) * INV_SQRT_2PI)
        if i == 0:
            fetches[n - 3].wait()
        pre_grad[at, :] = (hidden_grad[at, :] * slope).astype(jnp.bfloat16)
    saves = copies(sems.at[pl.ds(n, 1)], [(hidden, hidden_hbm)])
    fetches[n - 2].wait()
    agg_two = (mm(far[...], stale_hidden[...]) + mm(near[...], hidden[...])).astype(jnp.bfloat16)
    fetches[n - 1].wait()
    part_two = mm(agg_two, out_grad[...], ((0,), (0,)))
    part_one = mm(first_agg[...], pre_grad[...], ((0,), (0,)))
    first = core_ref[0] == 0
    for k in range(width // LANES):
        at = slice(k * LANES, (k + 1) * LANES)
        one, two = part_one[:, at], part_two[:, at]
        rows = pl.ds(k * width, width)
        keep[rows, :] = jnp.where(first, one, two)
        send[rows, :] = jnp.where(first, two, one).astype(send.dtype)
        saves += copies(
            sems.at[pl.ds(n + 1 + 2 * k, 2)],
            [(send.at[rows, :], send_hbm.at[rows, :]), (keep.at[rows, :], keep_hbm.at[rows, :])],
        )
    for save in saves:
        save.wait()


def box_kernel(picks_hbm, hidden_hbm, mail_hbm, hidden, picks, box, sems):
    for fetch in copies(sems, [(hidden_hbm, hidden), (picks_hbm, picks)]):
        fetch.wait()
    parts, blocks = box.shape[0], hidden.shape[1] // LANES
    slots = box.shape[1] // blocks
    picked = mm(picks[...], hidden[...])
    for k in range(blocks):
        block = picked[:, k * LANES : (k + 1) * LANES].reshape(parts, slots, LANES)
        box[:, k * slots : (k + 1) * slots, :] = block.astype(box.dtype)
    (save,) = copies(sems.at[pl.ds(2, 1)], [(box, mail_hbm.at[:, : box.shape[1], :])])
    save.wait()


def piece_kernel(keep_ref, other_ref, _, mail_hbm, pieces, sems):
    parts, size = pieces.shape[0], pieces.shape[1]
    total = keep_ref[...] + other_ref[...].astype(jnp.float32)
    whole = total.shape[0] // size
    rest = total.shape[0] - whole * size
    pieces[:whole] = total[: whole * size].reshape(whole, size, LANES).astype(pieces.dtype)
    pieces[whole:] = jnp.zeros((parts - whole, size, LANES), pieces.dtype)
    if rest:
        pieces[whole, :rest] = total[whole * size :].astype(pieces.dtype)
    start = mail_hbm.shape[1] - size
    (save,) = copies(sems, [(pieces, mail_hbm.at[:, start:, :])])
    save.wait()


def sum_kernel(n_z, n_py, mail_ref, out_ref, hidden_hbm, sems):
    size = out_ref.shape[1] // 2
    start = mail_ref.shape[1] - size
    saves = copies(sems, [(mail_ref.at[:, pl.ds(0, start), :], hidden_hbm)])
    for c in range(2):
        total = None
        for z in range(n_z):
            first = (z * 2 + c) * n_py
            block = mail_ref[first : first + n_py, start:, :].astype(jnp.float32).sum(0)
            total = block if total is None else total + block
        rounded = total.astype(out_ref.dtype)
        out_ref[:, c * size : (c + 1) * size, :] = jnp.broadcast_to(
            rounded[None], (out_ref.shape[0], size, LANES)
        )
    for save in saves:
        save.wait()


def finish_kernel(scale, n_py, core_ref, mine_ref, other_ref, one_hbm, two_hbm, one, two, sems):
    size = mine_ref.shape[1] // 2
    width = one.shape[0]
    lines = width * width // LANES

    def fill(sources):
        saves = []
        for q in range(2 * mine_ref.shape[0]):
            row, py = divmod(q, n_py)
            z, c = divmod(row, 2)
            line = q * size
            end = min(line + size, lines)
            while line < end:
                k, r = divmod(line, width)
                block = slice(k * LANES, (k + 1) * LANES)
                count = min(end - line, width - r)
                for g, out in enumerate((one, two)):
                    at = g * size + line - q * size
                    value = sources[c][z * n_py + py, at : at + count, :]
                    out[r : r + count, block] = value.astype(jnp.float32) * scale
                line += count
                if r + count == width:
                    saves += copies(
                        sems.at[pl.ds(2 * k, 2)],
                        [(one.at[:, block], one_hbm.at[:, block]), (two.at[:, block], two_hbm.at[:, block])],
                    )
        for save in saves:
            save.wait()

    @pl.when(core_ref[0] == 0)
    def _():
        fill((mine_ref, other_ref))

    @pl.when(core_ref[0] != 0)
    def _():
        fill((other_ref, mine_ref))


def in_vmem(*refs):
    return [pltpu.VMEM(r.shape, r.dtype) for r in refs]


def call(kernel, out_shape, scalars, scratch=(), vmem=None, limit=6, aliases=None, out=None):
    def run(*args):
        n_vmem = len(args) - scalars if vmem is None else vmem
        size = sum(a.size * a.dtype.itemsize for a in (*args, *jax.tree.leaves(out_shape)))
        out_spec = (VMEM if vmem is None else HBM) if out is None else out
        return pl.pallas_call(
            kernel,
            out_shape=out_shape,
            in_specs=[SMEM] * scalars + [VMEM] * n_vmem + [HBM] * (len(args) - scalars - n_vmem),
            out_specs=out_spec if isinstance(out, tuple) else jax.tree.map(lambda _: out_spec, out_shape),
            scratch_shapes=scratch,
            input_output_aliases=aliases or {},
            cost_estimate=pl.CostEstimate(flops=0, transcendentals=0, bytes_accessed=size),
            compiler_params=pltpu.CompilerParams(vmem_limit_bytes=limit * 1024 * 1024),
        )(*args)

    return run


def trade(value, groups=None):
    return lax.all_to_all(
        value, BOTH, split_axis=0, concat_axis=0, tiled=True, axis_index_groups=groups
    )


def sibling(value):
    n = lax.axis_size("px")
    return lax.ppermute(value, "px", [(i, i ^ 1) for i in range(n)])


def local(
    features,
    weight_one,
    weight_two,
    tile_values,
    tile_rows,
    tile_cols,
    tile_count,
    send_rows,
    send_count,
    stale_hidden,
    stale_grad,
    out_grad,
):
    bf16, f32 = jnp.bfloat16, jnp.float32
    parts = lax.axis_size(BOTH)
    own, width = features.shape
    slots = send_rows.shape[2]
    boundary = parts * slots
    shape = jax.ShapeDtypeStruct
    core = (lax.axis_index("px") % 2).astype(jnp.int32).reshape(1)
    n_z, n_py = lax.axis_size("px") // 2, lax.axis_size("py")

    square, square32 = shape((own, width), bf16), shape((own, width), f32)
    near, far = shape((own, own), bf16), shape((own, boundary), bf16)
    near32, far32 = shape((own, own), f32), shape((own, boundary), f32)
    slab, slots_in = shape((boundary, width), bf16), shape((parts, slots, width), bf16)
    weight = shape(weight_one.shape, bf16)
    picks = shape((boundary, own), bf16)
    semaphores = lambda count: [pltpu.SemaphoreType.DMA((count,))]
    lines = width * width // LANES
    keep, send = shape((lines, LANES), f32), shape((lines, LANES), bf16)

    outgoing, picked = call(
        pack_kernel,
        (slab, picks),
        0,
        in_vmem(
            square, shape((LANES, parts), jnp.int32), shape((boundary, LANES), f32), picks, slab
        )
        + semaphores(9),
        2,
        PACK,
    )(send_rows[0].T, send_count, features)
    arrived = trade(outgoing.reshape(parts, slots, -1)).reshape(boundary, -1)

    near_adj, far_adj, agg, hidden_grad, grad_out = call(
        local_kernel,
        (near, far, square32, square32, slots_in),
        3,
        in_vmem(
            tile_values, square, square, weight, slab, near32, far32, near, far, picks, square32, square32, slots_in
        )
        + semaphores(11),
        0,
        LOCAL,
    )(tile_rows[0], tile_cols[0], tile_count, tile_values, features, out_grad, weight_two, stale_grad, picked)

    arrived, grad_out = lax.optimization_barrier((arrived, grad_out))
    grads = trade(grad_out)
    hidden, keep, send = call(
        main_kernel,
        (square, keep, send),
        1,
        in_vmem(
            slab, near, far, square32, weight, square32, slab, square, square, keep, send, square, square
        )
        + semaphores(32),
        0,
        MAIN,
    )(core, arrived, near_adj, far_adj, agg, weight_one, hidden_grad, stale_hidden, out_grad)

    other = sibling(send)
    size = -(-lines // (parts * 8)) * 8
    rows = slots * width // LANES
    mail = call(
        box_kernel,
        shape((parts, rows + size, LANES), bf16),
        0,
        in_vmem(square, picks, shape((parts, rows, LANES), bf16)) + semaphores(3),
        0,
        BOX,
    )(picked, hidden)
    mail = call(
        piece_kernel,
        shape(mail.shape, bf16),
        0,
        in_vmem(shape((parts, size, LANES), bf16)) + semaphores(1),
        2,
        PIECE,
        {2: 0},
    )(keep, other, mail)
    mail, grads = lax.optimization_barrier((mail, grads))
    mail = trade(mail)
    chips = parts // 2
    mine, next_hidden = call(
        functools.partial(sum_kernel, n_z, n_py),
        (shape((chips, 2 * size, LANES), bf16), shape((parts, rows, LANES), bf16)),
        0,
        semaphores(1),
        1,
        SUM,
        None,
        (VMEM, HBM),
    )(mail)
    next_hidden = next_hidden.reshape(parts, width // LANES, slots, LANES)
    next_hidden = jnp.swapaxes(next_hidden, 1, 2).reshape(boundary, width)
    same_core = [[(2 * z + c) * n_py + i for z in range(n_z) for i in range(n_py)] for c in range(2)]
    mine = trade(mine, same_core)
    grads = grads.reshape(boundary, width)
    next_grad = jnp.where(outgoing == UNUSED, jnp.zeros_like(grads), grads)
    scale = 1.0 / math.sqrt(own * parts)
    one, two = call(
        functools.partial(finish_kernel, scale, n_py),
        (shape((width, width), f32),) * 2,
        1,
        in_vmem(*(shape((width, width), f32),) * 2) + semaphores(2 * (width // LANES)),
        None,
        FINISH,
        None,
        HBM,
    )(core, mine, sibling(mine))

    return next_hidden, next_grad, one, two


def solution(mesh):
    in_specs = (
        P(BOTH, None),
        P(),
        P(),
        P(BOTH, None, None),
        P(BOTH, None),
        P(BOTH, None),
        P(BOTH),
        P(BOTH, None, None),
        P(BOTH, None),
        P(BOTH, None),
        P(BOTH, None),
        P(BOTH, None),
    )
    out_specs = (P(BOTH, None), P(BOTH, None), P(), P())
    return jax.shard_map(local, mesh=mesh, in_specs=in_specs, out_specs=out_specs, check_vma=False)
```

```python
import functools
import math

import jax
import jax.numpy as jnp
from jax import lax
from jax.experimental import pallas as pl
from jax.experimental.pallas import tpu as pltpu
from jax.sharding import PartitionSpec as P

BOTH = ("px", "py")
LANES = 128
UNUSED = 2.0**126
PACK, LOCAL, MAIN = 58, 63, 56
BOX, PIECE, SUM, FINISH = 20, 12, 8, 16
VMEM = pl.BlockSpec(memory_space=pltpu.VMEM)
HBM = pl.BlockSpec(memory_space=pltpu.HBM)
SMEM = pl.BlockSpec(memory_space=pltpu.SMEM)
INV_SQRT2 = 1.0 / math.sqrt(2.0)
INV_SQRT_2PI = 1.0 / math.sqrt(2.0 * math.pi)


def mm(a, b, dims=((1,), (0,))):
    return lax.dot_general(a, b, (dims, ((), ())), preferred_element_type=jnp.float32)


def copies(sems, pairs):
    started = [
        pltpu.make_async_copy(src, dst, sems.at[i]) for i, (src, dst) in enumerate(pairs)
    ]
    for copy in started:
        copy.start()
    return started


def pack_kernel(
    rows_ref, counts_ref, features_hbm, out_hbm, picks_hbm, features, listed, wanted, picks, out, sems
):
    f32, bf16 = jnp.float32, jnp.bfloat16
    (fetch,) = copies(sems, [(features_hbm, features)])
    slots, parts = rows_ref.shape
    boundary, own = picks.shape
    listed[...] = jnp.zeros_like(listed)
    place = lax.broadcasted_iota(jnp.int32, (slots, parts), 0)
    counts = jnp.broadcast_to(counts_ref[...], (slots, parts))
    listed[:slots, :] = jnp.where(place < counts, rows_ref[...] + 1, 0)
    value = listed[...]
    step = boundary // 4
    slot = lax.broadcasted_iota(jnp.int32, (step, LANES), 0)
    lane = lax.broadcasted_iota(jnp.int32, (step, LANES), 1)
    mine = lane == slot % slots
    ones = jnp.ones((LANES, LANES), bf16)
    across = lax.broadcasted_iota(jnp.int32, (step, own), 1).astype(f32)
    saves = []
    for k in range(4):
        at = pl.ds(k * step, step)
        peer = jnp.where(lane == slot // slots + k * (step // slots), 1.0, 0.0).astype(bf16)
        index = jnp.full((step, LANES), -1.0, f32)
        for part, weight in ((value >> 5, 32.0), (value & 31, 1.0)):
            spread = mm(peer, part.astype(f32).astype(bf16), ((1,), (1,)))
            index += weight * mm(jnp.where(mine, spread, 0.0).astype(bf16), ones)
        wanted[at, :] = index
        wide = jnp.concatenate([index] * (own // LANES), axis=1)
        picks[at, :] = jnp.where(wide == across, 1.0, 0.0).astype(bf16)
        saves += copies(sems.at[pl.ds(1 + k, 1)], [(picks.at[at, :], picks_hbm.at[at, :])])
    fetch.wait()
    for k in range(4):
        at = pl.ds(k * step, step)
        row = mm(picks[at, :], features[...])
        unused = wanted[at, :] < 0.0
        for j in range(own // LANES):
            block = slice(j * LANES, (j + 1) * LANES)
            out[at, block] = jnp.where(unused, UNUSED, row[:, block]).astype(bf16)
        saves += copies(sems.at[pl.ds(5 + k, 1)], [(out.at[at, :], out_hbm.at[at, :])])
    for save in saves:
        save.wait()


def local_kernel(
    rows_ref,
    cols_ref,
    count_ref,
    tiles_hbm,
    features_hbm,
    out_grad_hbm,
    weight_hbm,
    stale_grad_hbm,
    picks_hbm,
    near_hbm,
    far_hbm,
    agg_hbm,
    hidden_grad_hbm,
    grad_out_hbm,
    tiles,
    features,
    out_grad,
    weight,
    stale_grad,
    near32,
    far32,
    near,
    far,
    picks,
    agg,
    hidden_grad,
    grad_out,
    sems,
):
    tile = tiles.shape[1]
    own = features.shape[0]
    fetches = copies(
        sems,
        [
            (tiles_hbm, tiles),
            (out_grad_hbm, out_grad),
            (weight_hbm, weight),
            (features_hbm, features),
            (stale_grad_hbm, stale_grad),
            (picks_hbm, picks),
        ],
    )
    near32[...] = jnp.zeros_like(near32)
    far32[...] = jnp.zeros_like(far32)
    fetches[0].wait()

    @pl.loop(0, count_ref[0])
    def _(t):
        r = pl.multiple_of(rows_ref[t] * tile, tile)
        c = pl.multiple_of(cols_ref[t] * tile, tile)
        value = tiles[t].astype(jnp.float32)

        @pl.when(c < own)
        def _():
            near32[pl.ds(r, tile), pl.ds(c, tile)] += value

        @pl.when(c >= own)
        def _():
            far32[pl.ds(r, tile), pl.ds(pl.multiple_of(c - own, tile), tile)] += value

    near[...] = near32[...].astype(near.dtype)
    far[...] = far32[...].astype(far.dtype)
    saves = copies(sems.at[pl.ds(6, 2)], [(near, near_hbm), (far, far_hbm)])
    fetches[3].wait()
    agg[...] = mm(near[...], features[...])
    saves += copies(sems.at[pl.ds(8, 1)], [(agg, agg_hbm)])
    fetches[1].wait()
    fetches[2].wait()
    down = mm(out_grad[...], weight[...], ((1,), (1,))).astype(jnp.bfloat16)
    remote = mm(far[...], down, ((0,), (0,)))
    grad_out[...] = remote.reshape(grad_out.shape).astype(grad_out.dtype)
    saves += copies(sems.at[pl.ds(9, 1)], [(grad_out, grad_out_hbm)])
    fetches[4].wait()
    fetches[5].wait()
    hidden_grad[...] = mm(near[...], down, ((0,), (0,))) + mm(
        picks[...], stale_grad[...], ((0,), (0,))
    )
    saves += copies(sems.at[pl.ds(10, 1)], [(hidden_grad, hidden_grad_hbm)])
    for save in saves:
        save.wait()


def main_kernel(
    core_ref,
    arrived_hbm,
    near_hbm,
    far_hbm,
    agg_hbm,
    weight_hbm,
    hidden_grad_hbm,
    stale_hidden_hbm,
    out_grad_hbm,
    hidden_hbm,
    keep_hbm,
    send_hbm,
    arrived,
    near,
    far,
    agg,
    weight,
    hidden_grad,
    stale_hidden,
    out_grad,
    hidden,
    keep,
    send,
    first_agg,
    pre_grad,
    sems,
):
    own, width = agg.shape
    step = 256
    blocks = own // step
    loads = [(arrived_hbm, arrived)]
    for i in range(blocks):
        at = pl.ds(i * step, step)
        loads += [(far_hbm.at[at, :], far.at[at, :]), (agg_hbm.at[at, :], agg.at[at, :])]
        if i == 0:
            loads += [(weight_hbm, weight)]
    loads += [
        (stale_hidden_hbm, stale_hidden),
        (hidden_grad_hbm, hidden_grad),
        (near_hbm, near),
        (out_grad_hbm, out_grad),
    ]
    fetches = copies(sems, loads)
    n = len(fetches)
    fetches[0].wait()
    fetches[n - 4].wait()
    for k in range(width // LANES):
        at = slice(k * LANES, (k + 1) * LANES)
        came = arrived[:, at].astype(jnp.float32)
        heard = came != UNUSED
        arrived[:, at] = jnp.where(heard, came, 0.0).astype(arrived.dtype)
        stale = stale_hidden[:, at].astype(jnp.float32)
        stale_hidden[:, at] = jnp.where(heard, stale, 0.0).astype(stale_hidden.dtype)
    for i in range(blocks):
        at = pl.ds(i * step, step)
        for fetch in fetches[1:4] if i == 0 else fetches[2 + 2 * i : 4 + 2 * i]:
            fetch.wait()
        agg_one = (agg[at, :] + mm(far[at, :], arrived[...])).astype(jnp.bfloat16)
        first_agg[at, :] = agg_one
        pre = mm(agg_one, weight[...])
        cdf = 0.5 * (1.0 + lax.erf(pre * INV_SQRT2))
        hidden[at, :] = (pre * cdf).astype(jnp.bfloat16)
        slope = cdf + pre * (jnp.exp(-0.5 * pre * pre) * INV_SQRT_2PI)
        if i == 0:
            fetches[n - 3].wait()
        pre_grad[at, :] = (hidden_grad[at, :] * slope).astype(jnp.bfloat16)
    saves = copies(sems.at[pl.ds(n, 1)], [(hidden, hidden_hbm)])
    fetches[n - 2].wait()
    agg_two = (mm(far[...], stale_hidden[...]) + mm(near[...], hidden[...])).astype(jnp.bfloat16)
    fetches[n - 1].wait()
    part_two = mm(agg_two, out_grad[...], ((0,), (0,)))
    part_one = mm(first_agg[...], pre_grad[...], ((0,), (0,)))
    first = core_ref[0] == 0
    for k in range(width // LANES):
        at = slice(k * LANES, (k + 1) * LANES)
        one, two = part_one[:, at], part_two[:, at]
        rows = pl.ds(k * width, width)
        keep[rows, :] = jnp.where(first, one, two)
        send[rows, :] = jnp.where(first, two, one).astype(send.dtype)
        saves += copies(
            sems.at[pl.ds(n + 1 + 2 * k, 2)],
            [(send.at[rows, :], send_hbm.at[rows, :]), (keep.at[rows, :], keep_hbm.at[rows, :])],
        )
    for save in saves:
        save.wait()


def box_kernel(picks_hbm, hidden_hbm, mail_hbm, hidden, picks, box, sems):
    for fetch in copies(sems, [(hidden_hbm, hidden), (picks_hbm, picks)]):
        fetch.wait()
    parts, blocks = box.shape[0], hidden.shape[1] // LANES
    slots = box.shape[1] // blocks
    picked = mm(picks[...], hidden[...])
    for k in range(blocks):
        block = picked[:, k * LANES : (k + 1) * LANES].reshape(parts, slots, LANES)
        box[:, k * slots : (k + 1) * slots, :] = block.astype(box.dtype)
    (save,) = copies(sems.at[pl.ds(2, 1)], [(box, mail_hbm.at[:, : box.shape[1], :])])
    save.wait()


def piece_kernel(keep_ref, other_ref, _, mail_hbm, pieces, sems):
    parts, size = pieces.shape[0], pieces.shape[1]
    share = 2 * keep_ref.shape[0] // parts
    for j in range(parts // 2):
        lines = pl.ds(j * share, share)
        total = keep_ref[lines, :] + other_ref[lines, :].astype(jnp.float32)
        pieces[2 * j] = total[:size].astype(pieces.dtype)
        pieces[2 * j + 1] = total[share - size :].astype(pieces.dtype)
    start = mail_hbm.shape[1] - size
    (save,) = copies(sems, [(pieces, mail_hbm.at[:, start:, :])])
    save.wait()


def sum_kernel(n_z, n_py, odd_ref, mail_ref, out_ref, hidden_hbm, sems):
    chips, share = out_ref.shape[:2]
    start = hidden_hbm.shape[1]
    size = mail_ref.shape[1] - start
    saves = copies(sems, [(mail_ref.at[:, pl.ds(0, start), :], hidden_hbm)])
    sums = []
    for c in range(2):
        total = None
        for z in range(n_z):
            first = (z * 2 + c) * n_py
            block = mail_ref[first : first + n_py, start:, :].astype(jnp.float32).sum(0)
            total = block if total is None else total + block
        sums.append(total)
    rest = share - size

    def give(one, two):
        both = jnp.concatenate([one, two], axis=0).astype(out_ref.dtype)
        out_ref[...] = jnp.broadcast_to(both[None], (chips, share, LANES))

    @pl.when(odd_ref[0] == 0)
    def _():
        give(sums[0], sums[1][:rest])

    @pl.when(odd_ref[0] != 0)
    def _():
        give(sums[0][size - rest :], sums[1])

    for save in saves:
        save.wait()


def finish_kernel(scale, size, n_py, core_ref, mine_ref, other_ref, one_hbm, two_hbm, one, two, sems):
    chips, share = mine_ref.shape[:2]
    rest = share - size
    width = one.shape[0]

    def fill(sources):
        saves = []
        for q in range(2 * chips):
            row, py = divmod(q, n_py)
            z, c = divmod(row, 2)
            pair, odd = divmod(q, 2)
            spans = ((size, rest, one), (rest, size, two)) if odd else ((0, size, one), (0, rest, two))
            at = 0
            for skip, count, out in spans:
                line = pair * share + skip
                end = line + count
                while line < end:
                    k, r = divmod(line, width)
                    run = min(end - line, width - r)
                    value = sources[c][z * n_py + py, at : at + run, :]
                    block = slice(k * LANES, (k + 1) * LANES)
                    out[r : r + run, block] = value.astype(jnp.float32) * scale
                    line += run
                    at += run
            done, before = (pair + 1) * share // width, pair * share // width
            for k in range(before, done if odd else before):
                block = slice(k * LANES, (k + 1) * LANES)
                saves += copies(
                    sems.at[pl.ds(2 * k, 2)],
                    [(one.at[:, block], one_hbm.at[:, block]), (two.at[:, block], two_hbm.at[:, block])],
                )
        for save in saves:
            save.wait()

    @pl.when(core_ref[0] == 0)
    def _():
        fill((mine_ref, other_ref))

    @pl.when(core_ref[0] != 0)
    def _():
        fill((other_ref, mine_ref))


def in_vmem(*refs):
    return [pltpu.VMEM(r.shape, r.dtype) for r in refs]


def call(kernel, out_shape, scalars, scratch=(), vmem=None, limit=6, aliases=None, out=None):
    def run(*args):
        n_vmem = len(args) - scalars if vmem is None else vmem
        size = sum(a.size * a.dtype.itemsize for a in (*args, *jax.tree.leaves(out_shape)))
        out_spec = (VMEM if vmem is None else HBM) if out is None else out
        return pl.pallas_call(
            kernel,
            out_shape=out_shape,
            in_specs=[SMEM] * scalars + [VMEM] * n_vmem + [HBM] * (len(args) - scalars - n_vmem),
            out_specs=out_spec if isinstance(out, tuple) else jax.tree.map(lambda _: out_spec, out_shape),
            scratch_shapes=scratch,
            input_output_aliases=aliases or {},
            cost_estimate=pl.CostEstimate(flops=0, transcendentals=0, bytes_accessed=size),
            compiler_params=pltpu.CompilerParams(vmem_limit_bytes=limit * 1024 * 1024),
        )(*args)

    return run


def trade(value, groups=None):
    return lax.all_to_all(
        value, BOTH, split_axis=0, concat_axis=0, tiled=True, axis_index_groups=groups
    )


def sibling(value):
    n = lax.axis_size("px")
    return lax.ppermute(value, "px", [(i, i ^ 1) for i in range(n)])


def local(
    features,
    weight_one,
    weight_two,
    tile_values,
    tile_rows,
    tile_cols,
    tile_count,
    send_rows,
    send_count,
    stale_hidden,
    stale_grad,
    out_grad,
):
    bf16, f32 = jnp.bfloat16, jnp.float32
    parts = lax.axis_size(BOTH)
    own, width = features.shape
    slots = send_rows.shape[2]
    boundary = parts * slots
    shape = jax.ShapeDtypeStruct
    core = (lax.axis_index("px") % 2).astype(jnp.int32).reshape(1)
    n_z, n_py = lax.axis_size("px") // 2, lax.axis_size("py")

    square, square32 = shape((own, width), bf16), shape((own, width), f32)
    near, far = shape((own, own), bf16), shape((own, boundary), bf16)
    near32, far32 = shape((own, own), f32), shape((own, boundary), f32)
    slab, slots_in = shape((boundary, width), bf16), shape((parts, slots, width), bf16)
    weight = shape(weight_one.shape, bf16)
    picks = shape((boundary, own), bf16)
    semaphores = lambda count: [pltpu.SemaphoreType.DMA((count,))]
    lines = width * width // LANES
    keep, send = shape((lines, LANES), f32), shape((lines, LANES), bf16)

    outgoing, picked = call(
        pack_kernel,
        (slab, picks),
        0,
        in_vmem(
            square, shape((LANES, parts), jnp.int32), shape((boundary, LANES), f32), picks, slab
        )
        + semaphores(9),
        2,
        PACK,
    )(send_rows[0].T, send_count, features)
    arrived = trade(outgoing.reshape(parts, slots, -1)).reshape(boundary, -1)

    near_adj, far_adj, agg, hidden_grad, grad_out = call(
        local_kernel,
        (near, far, square32, square32, slots_in),
        3,
        in_vmem(
            tile_values, square, square, weight, slab, near32, far32, near, far, picks, square32, square32, slots_in
        )
        + semaphores(11),
        0,
        LOCAL,
    )(tile_rows[0], tile_cols[0], tile_count, tile_values, features, out_grad, weight_two, stale_grad, picked)

    arrived, grad_out = lax.optimization_barrier((arrived, grad_out))
    grads = trade(grad_out)
    hidden, keep, send = call(
        main_kernel,
        (square, keep, send),
        1,
        in_vmem(
            slab, near, far, square32, weight, square32, slab, square, square, keep, send, square, square
        )
        + semaphores(32),
        0,
        MAIN,
    )(core, arrived, near_adj, far_adj, agg, weight_one, hidden_grad, stale_hidden, out_grad)

    other = sibling(send)
    share = 2 * lines // parts
    size = -(-share // 16) * 8
    rows = slots * width // LANES
    mail = call(
        box_kernel,
        shape((parts, rows + size, LANES), bf16),
        0,
        in_vmem(square, picks, shape((parts, rows, LANES), bf16)) + semaphores(3),
        0,
        BOX,
    )(picked, hidden)
    mail = call(
        piece_kernel,
        shape(mail.shape, bf16),
        0,
        in_vmem(shape((parts, size, LANES), bf16)) + semaphores(1),
        2,
        PIECE,
        {2: 0},
    )(keep, other, mail)
    odd = lax.axis_index("py").astype(jnp.int32).reshape(1) % 2
    mail, grads, odd = lax.optimization_barrier((mail, grads, odd))
    mail = trade(mail)
    chips = parts // 2
    mine, next_hidden = call(
        functools.partial(sum_kernel, n_z, n_py),
        (shape((chips, share, LANES), bf16), shape((parts, rows, LANES), bf16)),
        1,
        semaphores(1),
        1,
        SUM,
        None,
        (VMEM, HBM),
    )(odd, mail)
    next_hidden = next_hidden.reshape(parts, width // LANES, slots, LANES)
    next_hidden = jnp.swapaxes(next_hidden, 1, 2).reshape(boundary, width)
    same_core = [[(2 * z + c) * n_py + i for z in range(n_z) for i in range(n_py)] for c in range(2)]
    mine = trade(mine, same_core)
    grads = grads.reshape(boundary, width)
    next_grad = jnp.where(outgoing == UNUSED, jnp.zeros_like(grads), grads)
    scale = 1.0 / math.sqrt(own * parts)
    one, two = call(
        functools.partial(finish_kernel, scale, size, n_py),
        (shape((width, width), f32),) * 2,
        1,
        in_vmem(*(shape((width, width), f32),) * 2) + semaphores(2 * (width // LANES)),
        None,
        FINISH,
        None,
        HBM,
    )(core, mine, sibling(mine))

    return next_hidden, next_grad, one, two


def solution(mesh):
    in_specs = (
        P(BOTH, None),
        P(),
        P(),
        P(BOTH, None, None),
        P(BOTH, None),
        P(BOTH, None),
        P(BOTH),
        P(BOTH, None, None),
        P(BOTH, None),
        P(BOTH, None),
        P(BOTH, None),
        P(BOTH, None),
    )
    out_specs = (P(BOTH, None), P(BOTH, None), P(), P())
    return jax.shard_map(local, mesh=mesh, in_specs=in_specs, out_specs=out_specs, check_vma=False)
```

```python
import functools
import math

import jax
import jax.numpy as jnp
from jax import lax
from jax.experimental import pallas as pl
from jax.experimental.pallas import tpu as pltpu
from jax.sharding import PartitionSpec as P

BOTH = ("px", "py")
LANES = 128
UNUSED = 2.0**126
PACK, LOCAL, MAIN = 58, 63, 56
BOX, PIECE, SUM, FINISH = 20, 12, 8, 16
VMEM = pl.BlockSpec(memory_space=pltpu.VMEM)
HBM = pl.BlockSpec(memory_space=pltpu.HBM)
SMEM = pl.BlockSpec(memory_space=pltpu.SMEM)
INV_SQRT2 = 1.0 / math.sqrt(2.0)
INV_SQRT_2PI = 1.0 / math.sqrt(2.0 * math.pi)


def mm(a, b, dims=((1,), (0,))):
    return lax.dot_general(a, b, (dims, ((), ())), preferred_element_type=jnp.float32)


def copies(sems, pairs):
    started = [
        pltpu.make_async_copy(src, dst, sems.at[i]) for i, (src, dst) in enumerate(pairs)
    ]
    for copy in started:
        copy.start()
    return started


def pack_kernel(
    rows_ref, counts_ref, features_hbm, out_hbm, picks_hbm, features, listed, wanted, picks, out, sems
):
    f32, bf16 = jnp.float32, jnp.bfloat16
    (fetch,) = copies(sems, [(features_hbm, features)])
    slots, parts = rows_ref.shape
    boundary, own = picks.shape
    listed[...] = jnp.zeros_like(listed)
    place = lax.broadcasted_iota(jnp.int32, (slots, parts), 0)
    counts = jnp.broadcast_to(counts_ref[...], (slots, parts))
    listed[:slots, :] = jnp.where(place < counts, rows_ref[...] + 1, 0)
    value = listed[...]
    step = boundary // 4
    slot = lax.broadcasted_iota(jnp.int32, (step, LANES), 0)
    lane = lax.broadcasted_iota(jnp.int32, (step, LANES), 1)
    mine = lane == slot % slots
    ones = jnp.ones((LANES, LANES), bf16)
    across = lax.broadcasted_iota(jnp.int32, (step, own), 1).astype(f32)
    saves = []
    for k in range(4):
        at = pl.ds(k * step, step)
        peer = jnp.where(lane == slot // slots + k * (step // slots), 1.0, 0.0).astype(bf16)
        index = jnp.full((step, LANES), -1.0, f32)
        for part, weight in ((value >> 5, 32.0), (value & 31, 1.0)):
            spread = mm(peer, part.astype(f32).astype(bf16), ((1,), (1,)))
            index += weight * mm(jnp.where(mine, spread, 0.0).astype(bf16), ones)
        wanted[at, :] = index
        wide = jnp.concatenate([index] * (own // LANES), axis=1)
        picks[at, :] = jnp.where(wide == across, 1.0, 0.0).astype(bf16)
        saves += copies(sems.at[pl.ds(1 + k, 1)], [(picks.at[at, :], picks_hbm.at[at, :])])
    fetch.wait()
    for k in range(4):
        at = pl.ds(k * step, step)
        row = mm(picks[at, :], features[...])
        unused = wanted[at, :] < 0.0
        for j in range(own // LANES):
            block = slice(j * LANES, (j + 1) * LANES)
            out[at, block] = jnp.where(unused, UNUSED, row[:, block]).astype(bf16)
        saves += copies(sems.at[pl.ds(5 + k, 1)], [(out.at[at, :], out_hbm.at[at, :])])
    for save in saves:
        save.wait()


def local_kernel(
    rows_ref,
    cols_ref,
    count_ref,
    tiles_hbm,
    features_hbm,
    out_grad_hbm,
    weight_hbm,
    stale_grad_hbm,
    picks_hbm,
    near_hbm,
    far_hbm,
    agg_hbm,
    hidden_grad_hbm,
    grad_out_hbm,
    tiles,
    features,
    out_grad,
    weight,
    stale_grad,
    near32,
    far32,
    near,
    far,
    picks,
    agg,
    hidden_grad,
    grad_out,
    sems,
):
    tile = tiles.shape[1]
    own = features.shape[0]
    fetches = copies(
        sems,
        [
            (tiles_hbm, tiles),
            (out_grad_hbm, out_grad),
            (weight_hbm, weight),
            (features_hbm, features),
            (stale_grad_hbm, stale_grad),
            (picks_hbm, picks),
        ],
    )
    near32[...] = jnp.zeros_like(near32)
    far32[...] = jnp.zeros_like(far32)
    fetches[0].wait()

    @pl.loop(0, count_ref[0])
    def _(t):
        r = pl.multiple_of(rows_ref[t] * tile, tile)
        c = pl.multiple_of(cols_ref[t] * tile, tile)
        value = tiles[t].astype(jnp.float32)

        @pl.when(c < own)
        def _():
            near32[pl.ds(r, tile), pl.ds(c, tile)] += value

        @pl.when(c >= own)
        def _():
            far32[pl.ds(r, tile), pl.ds(pl.multiple_of(c - own, tile), tile)] += value

    near[...] = near32[...].astype(near.dtype)
    far[...] = far32[...].astype(far.dtype)
    saves = copies(sems.at[pl.ds(6, 2)], [(near, near_hbm), (far, far_hbm)])
    fetches[3].wait()
    agg[...] = mm(near[...], features[...])
    saves += copies(sems.at[pl.ds(8, 1)], [(agg, agg_hbm)])
    fetches[1].wait()
    fetches[2].wait()
    down = mm(out_grad[...], weight[...], ((1,), (1,))).astype(jnp.bfloat16)
    remote = mm(far[...], down, ((0,), (0,)))
    grad_out[...] = remote.reshape(grad_out.shape).astype(grad_out.dtype)
    saves += copies(sems.at[pl.ds(9, 1)], [(grad_out, grad_out_hbm)])
    fetches[4].wait()
    fetches[5].wait()
    hidden_grad[...] = mm(near[...], down, ((0,), (0,))) + mm(
        picks[...], stale_grad[...], ((0,), (0,))
    )
    saves += copies(sems.at[pl.ds(10, 1)], [(hidden_grad, hidden_grad_hbm)])
    for save in saves:
        save.wait()


def main_kernel(
    core_ref,
    arrived_hbm,
    near_hbm,
    far_hbm,
    agg_hbm,
    weight_hbm,
    hidden_grad_hbm,
    stale_hidden_hbm,
    out_grad_hbm,
    hidden_hbm,
    keep_hbm,
    send_hbm,
    arrived,
    near,
    far,
    agg,
    weight,
    hidden_grad,
    stale_hidden,
    out_grad,
    hidden,
    keep,
    send,
    first_agg,
    pre_grad,
    sems,
):
    own, width = agg.shape
    step = 256
    blocks = own // step
    loads = [(arrived_hbm, arrived)]
    for i in range(blocks):
        at = pl.ds(i * step, step)
        loads += [(far_hbm.at[at, :], far.at[at, :]), (agg_hbm.at[at, :], agg.at[at, :])]
        if i == 0:
            loads += [(weight_hbm, weight)]
    loads += [
        (stale_hidden_hbm, stale_hidden),
        (hidden_grad_hbm, hidden_grad),
        (near_hbm, near),
        (out_grad_hbm, out_grad),
    ]
    fetches = copies(sems, loads)
    n = len(fetches)
    fetches[0].wait()
    fetches[n - 4].wait()
    for k in range(width // LANES):
        at = slice(k * LANES, (k + 1) * LANES)
        came = arrived[:, at].astype(jnp.float32)
        heard = came != UNUSED
        arrived[:, at] = jnp.where(heard, came, 0.0).astype(arrived.dtype)
        stale = stale_hidden[:, at].astype(jnp.float32)
        stale_hidden[:, at] = jnp.where(heard, stale, 0.0).astype(stale_hidden.dtype)
    for i in range(blocks):
        at = pl.ds(i * step, step)
        for fetch in fetches[1:4] if i == 0 else fetches[2 + 2 * i : 4 + 2 * i]:
            fetch.wait()
        agg_one = (agg[at, :] + mm(far[at, :], arrived[...])).astype(jnp.bfloat16)
        first_agg[at, :] = agg_one
        pre = mm(agg_one, weight[...])
        cdf = 0.5 * (1.0 + lax.erf(pre * INV_SQRT2))
        hidden[at, :] = (pre * cdf).astype(jnp.bfloat16)
        slope = cdf + pre * (jnp.exp(-0.5 * pre * pre) * INV_SQRT_2PI)
        if i == 0:
            fetches[n - 3].wait()
        pre_grad[at, :] = (hidden_grad[at, :] * slope).astype(jnp.bfloat16)
    saves = copies(sems.at[pl.ds(n, 1)], [(hidden, hidden_hbm)])
    fetches[n - 2].wait()
    agg_two = (mm(far[...], stale_hidden[...]) + mm(near[...], hidden[...])).astype(jnp.bfloat16)
    fetches[n - 1].wait()
    part_two = mm(agg_two, out_grad[...], ((0,), (0,)))
    part_one = mm(first_agg[...], pre_grad[...], ((0,), (0,)))
    first = core_ref[0] == 0
    for k in range(width // LANES):
        at = slice(k * LANES, (k + 1) * LANES)
        one, two = part_one[:, at], part_two[:, at]
        rows = pl.ds(k * width, width)
        keep[rows, :] = jnp.where(first, one, two)
        send[rows, :] = jnp.where(first, two, one).astype(send.dtype)
        saves += copies(
            sems.at[pl.ds(n + 1 + 2 * k, 2)],
            [(send.at[rows, :], send_hbm.at[rows, :]), (keep.at[rows, :], keep_hbm.at[rows, :])],
        )
    for save in saves:
        save.wait()


def box_kernel(picks_hbm, hidden_hbm, mail_hbm, hidden, picks, box, sems):
    for fetch in copies(sems, [(hidden_hbm, hidden), (picks_hbm, picks)]):
        fetch.wait()
    parts, blocks = box.shape[0], hidden.shape[1] // LANES
    slots = box.shape[1] // blocks
    picked = mm(picks[...], hidden[...])
    for k in range(blocks):
        block = picked[:, k * LANES : (k + 1) * LANES].reshape(parts, slots, LANES)
        box[:, k * slots : (k + 1) * slots, :] = block.astype(box.dtype)
    (save,) = copies(sems.at[pl.ds(2, 1)], [(box, mail_hbm.at[:, : box.shape[1], :])])
    save.wait()


def piece_kernel(keep_ref, other_ref, _, mail_hbm, pieces, sems):
    parts, size = pieces.shape[0], pieces.shape[1]
    share = 2 * keep_ref.shape[0] // parts
    for j in range(parts // 2):
        lines = pl.ds(j * share, share)
        total = keep_ref[lines, :] + other_ref[lines, :].astype(jnp.float32)
        pieces[2 * j] = total[:size].astype(pieces.dtype)
        pieces[2 * j + 1] = total[share - size :].astype(pieces.dtype)
    start = mail_hbm.shape[1] - size
    (save,) = copies(sems, [(pieces, mail_hbm.at[:, start:, :])])
    save.wait()


def sum_kernel(n_z, n_py, core_ref, mail_ref, out_ref, hidden_hbm, sems):
    chips, share = out_ref.shape[:2]
    start = hidden_hbm.shape[1]
    size = mail_ref.shape[1] - start
    saves = copies(sems, [(mail_ref.at[:, pl.ds(0, start), :], hidden_hbm)])
    sums = []
    for c in range(2):
        total = None
        for z in range(n_z):
            first = (z * 2 + c) * n_py
            block = mail_ref[first : first + n_py, start:, :].astype(jnp.float32).sum(0)
            total = block if total is None else total + block
        sums.append(total)
    rest = share - size

    def give(one, two):
        both = jnp.concatenate([one, two], axis=0).astype(out_ref.dtype)
        out_ref[...] = jnp.broadcast_to(both[None], (chips, share, LANES))

    @pl.when(core_ref[1] == 0)
    def _():
        give(sums[0], sums[1][:rest])

    @pl.when(core_ref[1] != 0)
    def _():
        give(sums[0][size - rest :], sums[1])

    for save in saves:
        save.wait()


def finish_kernel(scale, size, n_py, core_ref, mine_ref, other_ref, one_hbm, two_hbm, one, two, sems):
    chips, share = mine_ref.shape[:2]
    rest = share - size
    width = one.shape[0]

    def fill(sources):
        saves = []
        for q in range(2 * chips):
            row, py = divmod(q, n_py)
            z, c = divmod(row, 2)
            pair, odd = divmod(q, 2)
            spans = ((size, rest, one), (rest, size, two)) if odd else ((0, size, one), (0, rest, two))
            at = 0
            for skip, count, out in spans:
                line = pair * share + skip
                end = line + count
                while line < end:
                    k, r = divmod(line, width)
                    run = min(end - line, width - r)
                    value = sources[c][z * n_py + py, at : at + run, :]
                    block = slice(k * LANES, (k + 1) * LANES)
                    out[r : r + run, block] = value.astype(jnp.float32) * scale
                    line += run
                    at += run
            done, before = (pair + 1) * share // width, pair * share // width
            for k in range(before, done if odd else before):
                block = slice(k * LANES, (k + 1) * LANES)
                saves += copies(
                    sems.at[pl.ds(2 * k, 2)],
                    [(one.at[:, block], one_hbm.at[:, block]), (two.at[:, block], two_hbm.at[:, block])],
                )
        for save in saves:
            save.wait()

    @pl.when(core_ref[0] == 0)
    def _():
        fill((mine_ref, other_ref))

    @pl.when(core_ref[0] != 0)
    def _():
        fill((other_ref, mine_ref))


def in_vmem(*refs):
    return [pltpu.VMEM(r.shape, r.dtype) for r in refs]


def call(kernel, out_shape, scalars, scratch=(), vmem=None, limit=6, aliases=None, out=None):
    def run(*args):
        n_vmem = len(args) - scalars if vmem is None else vmem
        size = sum(a.size * a.dtype.itemsize for a in (*args, *jax.tree.leaves(out_shape)))
        out_spec = (VMEM if vmem is None else HBM) if out is None else out
        return pl.pallas_call(
            kernel,
            out_shape=out_shape,
            in_specs=[SMEM] * scalars + [VMEM] * n_vmem + [HBM] * (len(args) - scalars - n_vmem),
            out_specs=out_spec if isinstance(out, tuple) else jax.tree.map(lambda _: out_spec, out_shape),
            scratch_shapes=scratch,
            input_output_aliases=aliases or {},
            cost_estimate=pl.CostEstimate(flops=0, transcendentals=0, bytes_accessed=size),
            compiler_params=pltpu.CompilerParams(vmem_limit_bytes=limit * 1024 * 1024),
        )(*args)

    return run


def trade(value, groups=None):
    return lax.all_to_all(
        value, BOTH, split_axis=0, concat_axis=0, tiled=True, axis_index_groups=groups
    )


def sibling(value):
    n = lax.axis_size("px")
    return lax.ppermute(value, "px", [(i, i ^ 1) for i in range(n)])


def local(
    features,
    weight_one,
    weight_two,
    tile_values,
    tile_rows,
    tile_cols,
    tile_count,
    send_rows,
    send_count,
    stale_hidden,
    stale_grad,
    out_grad,
):
    bf16, f32 = jnp.bfloat16, jnp.float32
    parts = lax.axis_size(BOTH)
    own, width = features.shape
    slots = send_rows.shape[2]
    boundary = parts * slots
    shape = jax.ShapeDtypeStruct
    core = jnp.stack([lax.axis_index("px") % 2, lax.axis_index("py") % 2]).astype(jnp.int32)
    n_z, n_py = lax.axis_size("px") // 2, lax.axis_size("py")

    square, square32 = shape((own, width), bf16), shape((own, width), f32)
    near, far = shape((own, own), bf16), shape((own, boundary), bf16)
    near32, far32 = shape((own, own), f32), shape((own, boundary), f32)
    slab, slots_in = shape((boundary, width), bf16), shape((parts, slots, width), bf16)
    weight = shape(weight_one.shape, bf16)
    picks = shape((boundary, own), bf16)
    semaphores = lambda count: [pltpu.SemaphoreType.DMA((count,))]
    lines = width * width // LANES
    keep, send = shape((lines, LANES), f32), shape((lines, LANES), bf16)

    outgoing, picked = call(
        pack_kernel,
        (slab, picks),
        0,
        in_vmem(
            square, shape((LANES, parts), jnp.int32), shape((boundary, LANES), f32), picks, slab
        )
        + semaphores(9),
        2,
        PACK,
    )(send_rows[0].T, send_count, features)
    arrived = trade(outgoing.reshape(parts, slots, -1)).reshape(boundary, -1)

    near_adj, far_adj, agg, hidden_grad, grad_out = call(
        local_kernel,
        (near, far, square32, square32, slots_in),
        3,
        in_vmem(
            tile_values, square, square, weight, slab, near32, far32, near, far, picks, square32, square32, slots_in
        )
        + semaphores(11),
        0,
        LOCAL,
    )(tile_rows[0], tile_cols[0], tile_count, tile_values, features, out_grad, weight_two, stale_grad, picked)

    arrived, grad_out = lax.optimization_barrier((arrived, grad_out))
    grads = trade(grad_out)
    hidden, keep, send = call(
        main_kernel,
        (square, keep, send),
        1,
        in_vmem(
            slab, near, far, square32, weight, square32, slab, square, square, keep, send, square, square
        )
        + semaphores(32),
        0,
        MAIN,
    )(core, arrived, near_adj, far_adj, agg, weight_one, hidden_grad, stale_hidden, out_grad)

    other = sibling(send)
    share = 2 * lines // parts
    size = -(-share // 16) * 8
    rows = slots * width // LANES
    mail = call(
        box_kernel,
        shape((parts, rows + size, LANES), bf16),
        0,
        in_vmem(square, picks, shape((parts, rows, LANES), bf16)) + semaphores(3),
        0,
        BOX,
    )(picked, hidden)
    mail = call(
        piece_kernel,
        shape(mail.shape, bf16),
        0,
        in_vmem(shape((parts, size, LANES), bf16)) + semaphores(1),
        2,
        PIECE,
        {2: 0},
    )(keep, other, mail)
    mail, grads = lax.optimization_barrier((mail, grads))
    mail = trade(mail)
    chips = parts // 2
    mine, next_hidden = call(
        functools.partial(sum_kernel, n_z, n_py),
        (shape((chips, share, LANES), bf16), shape((parts, rows, LANES), bf16)),
        1,
        semaphores(1),
        1,
        SUM,
        None,
        (VMEM, HBM),
    )(core, mail)
    next_hidden = next_hidden.reshape(parts, width // LANES, slots, LANES)
    next_hidden = jnp.swapaxes(next_hidden, 1, 2).reshape(boundary, width)
    same_core = [[(2 * z + c) * n_py + i for z in range(n_z) for i in range(n_py)] for c in range(2)]
    mine = trade(mine, same_core)
    grads = grads.reshape(boundary, width)
    next_grad = jnp.where(outgoing == UNUSED, jnp.zeros_like(grads), grads)
    scale = 1.0 / math.sqrt(own * parts)
    one, two = call(
        functools.partial(finish_kernel, scale, size, n_py),
        (shape((width, width), f32),) * 2,
        1,
        in_vmem(*(shape((width, width), f32),) * 2) + semaphores(2 * (width // LANES)),
        None,
        FINISH,
        None,
        HBM,
    )(core, mine, sibling(mine))

    return next_hidden, next_grad, one, two


def solution(mesh):
    in_specs = (
        P(BOTH, None),
        P(),
        P(),
        P(BOTH, None, None),
        P(BOTH, None),
        P(BOTH, None),
        P(BOTH),
        P(BOTH, None, None),
        P(BOTH, None),
        P(BOTH, None),
        P(BOTH, None),
        P(BOTH, None),
    )
    out_specs = (P(BOTH, None), P(BOTH, None), P(), P())
    return jax.shard_map(local, mesh=mesh, in_specs=in_specs, out_specs=out_specs, check_vma=False)
```

```python
import functools
import math

import jax
import jax.numpy as jnp
from jax import lax
from jax.experimental import pallas as pl
from jax.experimental.pallas import tpu as pltpu
from jax.sharding import PartitionSpec as P

BOTH = ("px", "py")
LANES = 128
UNUSED = 2.0**126
PACK, LOCAL, MAIN = 58, 63, 56
BOX, PIECE, SUM, FINISH = 20, 12, 8, 16
VMEM = pl.BlockSpec(memory_space=pltpu.VMEM)
HBM = pl.BlockSpec(memory_space=pltpu.HBM)
SMEM = pl.BlockSpec(memory_space=pltpu.SMEM)
INV_SQRT2 = 1.0 / math.sqrt(2.0)
INV_SQRT_2PI = 1.0 / math.sqrt(2.0 * math.pi)


def mm(a, b, dims=((1,), (0,))):
    return lax.dot_general(a, b, (dims, ((), ())), preferred_element_type=jnp.float32)


def copies(sems, pairs):
    started = [
        pltpu.make_async_copy(src, dst, sems.at[i]) for i, (src, dst) in enumerate(pairs)
    ]
    for copy in started:
        copy.start()
    return started


def pack_kernel(
    rows_ref, counts_ref, features_hbm, out_hbm, picks_hbm, features, listed, wanted, picks, out, sems
):
    f32, bf16 = jnp.float32, jnp.bfloat16
    (fetch,) = copies(sems, [(features_hbm, features)])
    slots, parts = rows_ref.shape
    boundary, own = picks.shape
    listed[...] = jnp.zeros_like(listed)
    place = lax.broadcasted_iota(jnp.int32, (slots, parts), 0)
    counts = jnp.broadcast_to(counts_ref[...], (slots, parts))
    listed[:slots, :] = jnp.where(place < counts, rows_ref[...] + 1, 0)
    value = listed[...]
    step = boundary // 4
    slot = lax.broadcasted_iota(jnp.int32, (step, LANES), 0)
    lane = lax.broadcasted_iota(jnp.int32, (step, LANES), 1)
    mine = lane == slot % slots
    ones = jnp.ones((LANES, LANES), bf16)
    across = lax.broadcasted_iota(jnp.int32, (step, own), 1).astype(f32)
    saves = []
    for k in range(4):
        at = pl.ds(k * step, step)
        peer = jnp.where(lane == slot // slots + k * (step // slots), 1.0, 0.0).astype(bf16)
        index = jnp.full((step, LANES), -1.0, f32)
        for part, weight in ((value >> 5, 32.0), (value & 31, 1.0)):
            spread = mm(peer, part.astype(f32).astype(bf16), ((1,), (1,)))
            index += weight * mm(jnp.where(mine, spread, 0.0).astype(bf16), ones)
        wanted[at, :] = index
        wide = jnp.concatenate([index] * (own // LANES), axis=1)
        picks[at, :] = jnp.where(wide == across, 1.0, 0.0).astype(bf16)
        saves += copies(sems.at[pl.ds(1 + k, 1)], [(picks.at[at, :], picks_hbm.at[at, :])])
    fetch.wait()
    for k in range(4):
        at = pl.ds(k * step, step)
        row = mm(picks[at, :], features[...])
        unused = wanted[at, :] < 0.0
        for j in range(own // LANES):
            block = slice(j * LANES, (j + 1) * LANES)
            out[at, block] = jnp.where(unused, UNUSED, row[:, block]).astype(bf16)
        saves += copies(sems.at[pl.ds(5 + k, 1)], [(out.at[at, :], out_hbm.at[at, :])])
    for save in saves:
        save.wait()


def local_kernel(
    rows_ref,
    cols_ref,
    count_ref,
    tiles_hbm,
    features_hbm,
    out_grad_hbm,
    weight_hbm,
    stale_grad_hbm,
    picks_hbm,
    near_hbm,
    far_hbm,
    agg_hbm,
    hidden_grad_hbm,
    grad_out_hbm,
    tiles,
    features,
    out_grad,
    weight,
    stale_grad,
    near32,
    far32,
    near,
    far,
    picks,
    agg,
    hidden_grad,
    grad_out,
    sems,
):
    tile = tiles.shape[1]
    own = features.shape[0]
    fetches = copies(
        sems,
        [
            (tiles_hbm, tiles),
            (out_grad_hbm, out_grad),
            (weight_hbm, weight),
            (features_hbm, features),
            (stale_grad_hbm, stale_grad),
            (picks_hbm, picks),
        ],
    )
    near32[...] = jnp.zeros_like(near32)
    far32[...] = jnp.zeros_like(far32)
    fetches[0].wait()

    @pl.loop(0, count_ref[0])
    def _(t):
        r = pl.multiple_of(rows_ref[t] * tile, tile)
        c = pl.multiple_of(cols_ref[t] * tile, tile)
        value = tiles[t].astype(jnp.float32)

        @pl.when(c < own)
        def _():
            near32[pl.ds(r, tile), pl.ds(c, tile)] += value

        @pl.when(c >= own)
        def _():
            far32[pl.ds(r, tile), pl.ds(pl.multiple_of(c - own, tile), tile)] += value

    near[...] = near32[...].astype(near.dtype)
    far[...] = far32[...].astype(far.dtype)
    saves = copies(sems.at[pl.ds(6, 2)], [(near, near_hbm), (far, far_hbm)])
    fetches[3].wait()
    agg[...] = mm(near[...], features[...])
    saves += copies(sems.at[pl.ds(8, 1)], [(agg, agg_hbm)])
    fetches[1].wait()
    fetches[2].wait()
    down = mm(out_grad[...], weight[...], ((1,), (1,))).astype(jnp.bfloat16)
    remote = mm(far[...], down, ((0,), (0,)))
    grad_out[...] = remote.reshape(grad_out.shape).astype(grad_out.dtype)
    saves += copies(sems.at[pl.ds(9, 1)], [(grad_out, grad_out_hbm)])
    fetches[4].wait()
    fetches[5].wait()
    hidden_grad[...] = mm(near[...], down, ((0,), (0,))) + mm(
        picks[...], stale_grad[...], ((0,), (0,))
    )
    saves += copies(sems.at[pl.ds(10, 1)], [(hidden_grad, hidden_grad_hbm)])
    for save in saves:
        save.wait()


def main_kernel(
    core_ref,
    arrived_hbm,
    near_hbm,
    far_hbm,
    agg_hbm,
    weight_hbm,
    hidden_grad_hbm,
    stale_hidden_hbm,
    out_grad_hbm,
    hidden_hbm,
    keep_hbm,
    send_hbm,
    arrived,
    near,
    far,
    agg,
    weight,
    hidden_grad,
    stale_hidden,
    out_grad,
    hidden,
    keep,
    send,
    first_agg,
    pre_grad,
    sems,
):
    own, width = agg.shape
    step = 256
    blocks = own // step
    loads = [(arrived_hbm, arrived)]
    for i in range(blocks):
        at = pl.ds(i * step, step)
        loads += [(far_hbm.at[at, :], far.at[at, :]), (agg_hbm.at[at, :], agg.at[at, :])]
        if i == 0:
            loads += [(weight_hbm, weight)]
    loads += [
        (stale_hidden_hbm, stale_hidden),
        (hidden_grad_hbm, hidden_grad),
        (near_hbm, near),
        (out_grad_hbm, out_grad),
    ]
    fetches = copies(sems, loads)
    n = len(fetches)
    fetches[0].wait()
    fetches[n - 4].wait()
    for k in range(width // LANES):
        at = slice(k * LANES, (k + 1) * LANES)
        came = arrived[:, at].astype(jnp.float32)
        heard = came != UNUSED
        arrived[:, at] = jnp.where(heard, came, 0.0).astype(arrived.dtype)
        stale = stale_hidden[:, at].astype(jnp.float32)
        stale_hidden[:, at] = jnp.where(heard, stale, 0.0).astype(stale_hidden.dtype)
    for i in range(blocks):
        at = pl.ds(i * step, step)
        for fetch in fetches[1:4] if i == 0 else fetches[2 + 2 * i : 4 + 2 * i]:
            fetch.wait()
        agg_one = (agg[at, :] + mm(far[at, :], arrived[...])).astype(jnp.bfloat16)
        first_agg[at, :] = agg_one
        pre = mm(agg_one, weight[...])
        cdf = 0.5 * (1.0 + lax.erf(pre * INV_SQRT2))
        hidden[at, :] = (pre * cdf).astype(jnp.bfloat16)
        slope = cdf + pre * (jnp.exp(-0.5 * pre * pre) * INV_SQRT_2PI)
        if i == 0:
            fetches[n - 3].wait()
        pre_grad[at, :] = (hidden_grad[at, :] * slope).astype(jnp.bfloat16)
    saves = copies(sems.at[pl.ds(n, 1)], [(hidden, hidden_hbm)])
    fetches[n - 2].wait()
    agg_two = (mm(far[...], stale_hidden[...]) + mm(near[...], hidden[...])).astype(jnp.bfloat16)
    fetches[n - 1].wait()
    part_two = mm(agg_two, out_grad[...], ((0,), (0,)))
    part_one = mm(first_agg[...], pre_grad[...], ((0,), (0,)))
    first = (core_ref[0] & 1) == 0
    for k in range(width // LANES):
        at = slice(k * LANES, (k + 1) * LANES)
        one, two = part_one[:, at], part_two[:, at]
        rows = pl.ds(k * width, width)
        keep[rows, :] = jnp.where(first, one, two)
        send[rows, :] = jnp.where(first, two, one).astype(send.dtype)
        saves += copies(
            sems.at[pl.ds(n + 1 + 2 * k, 2)],
            [(send.at[rows, :], send_hbm.at[rows, :]), (keep.at[rows, :], keep_hbm.at[rows, :])],
        )
    for save in saves:
        save.wait()


def box_kernel(picks_hbm, hidden_hbm, mail_hbm, hidden, picks, box, sems):
    for fetch in copies(sems, [(hidden_hbm, hidden), (picks_hbm, picks)]):
        fetch.wait()
    parts, blocks = box.shape[0], hidden.shape[1] // LANES
    slots = box.shape[1] // blocks
    picked = mm(picks[...], hidden[...])
    for k in range(blocks):
        block = picked[:, k * LANES : (k + 1) * LANES].reshape(parts, slots, LANES)
        box[:, k * slots : (k + 1) * slots, :] = block.astype(box.dtype)
    (save,) = copies(sems.at[pl.ds(2, 1)], [(box, mail_hbm.at[:, : box.shape[1], :])])
    save.wait()


def piece_kernel(keep_ref, other_ref, _, mail_hbm, pieces, sems):
    parts, size = pieces.shape[0], pieces.shape[1]
    share = 2 * keep_ref.shape[0] // parts
    for j in range(parts // 2):
        lines = pl.ds(j * share, share)
        total = keep_ref[lines, :] + other_ref[lines, :].astype(jnp.float32)
        pieces[2 * j] = total[:size].astype(pieces.dtype)
        pieces[2 * j + 1] = total[share - size :].astype(pieces.dtype)
    start = mail_hbm.shape[1] - size
    (save,) = copies(sems, [(pieces, mail_hbm.at[:, start:, :])])
    save.wait()


def sum_kernel(n_z, n_py, core_ref, mail_ref, out_ref, hidden_hbm, sems):
    chips, share = out_ref.shape[:2]
    start = hidden_hbm.shape[1]
    size = mail_ref.shape[1] - start
    saves = copies(sems, [(mail_ref.at[:, pl.ds(0, start), :], hidden_hbm)])
    sums = []
    for c in range(2):
        total = None
        for z in range(n_z):
            first = (z * 2 + c) * n_py
            block = mail_ref[first : first + n_py, start:, :].astype(jnp.float32).sum(0)
            total = block if total is None else total + block
        sums.append(total)
    rest = share - size

    def give(one, two):
        both = jnp.concatenate([one, two], axis=0).astype(out_ref.dtype)
        out_ref[...] = jnp.broadcast_to(both[None], (chips, share, LANES))

    @pl.when(core_ref[0] < 2)
    def _():
        give(sums[0], sums[1][:rest])

    @pl.when(core_ref[0] >= 2)
    def _():
        give(sums[0][size - rest :], sums[1])

    for save in saves:
        save.wait()


def finish_kernel(scale, size, n_py, core_ref, mine_ref, other_ref, one_hbm, two_hbm, one, two, sems):
    chips, share = mine_ref.shape[:2]
    rest = share - size
    width = one.shape[0]

    def fill(sources):
        saves = []
        for q in range(2 * chips):
            row, py = divmod(q, n_py)
            z, c = divmod(row, 2)
            pair, odd = divmod(q, 2)
            spans = ((size, rest, one), (rest, size, two)) if odd else ((0, size, one), (0, rest, two))
            at = 0
            for skip, count, out in spans:
                line = pair * share + skip
                end = line + count
                while line < end:
                    k, r = divmod(line, width)
                    run = min(end - line, width - r)
                    value = sources[c][z * n_py + py, at : at + run, :]
                    block = slice(k * LANES, (k + 1) * LANES)
                    out[r : r + run, block] = value.astype(jnp.float32) * scale
                    line += run
                    at += run
            done, before = (pair + 1) * share // width, pair * share // width
            for k in range(before, done if odd else before):
                block = slice(k * LANES, (k + 1) * LANES)
                saves += copies(
                    sems.at[pl.ds(2 * k, 2)],
                    [(one.at[:, block], one_hbm.at[:, block]), (two.at[:, block], two_hbm.at[:, block])],
                )
        for save in saves:
            save.wait()

    @pl.when((core_ref[0] & 1) == 0)
    def _():
        fill((mine_ref, other_ref))

    @pl.when((core_ref[0] & 1) != 0)
    def _():
        fill((other_ref, mine_ref))


def in_vmem(*refs):
    return [pltpu.VMEM(r.shape, r.dtype) for r in refs]


def call(kernel, out_shape, scalars, scratch=(), vmem=None, limit=6, aliases=None, out=None):
    def run(*args):
        n_vmem = len(args) - scalars if vmem is None else vmem
        size = sum(a.size * a.dtype.itemsize for a in (*args, *jax.tree.leaves(out_shape)))
        out_spec = (VMEM if vmem is None else HBM) if out is None else out
        return pl.pallas_call(
            kernel,
            out_shape=out_shape,
            in_specs=[SMEM] * scalars + [VMEM] * n_vmem + [HBM] * (len(args) - scalars - n_vmem),
            out_specs=out_spec if isinstance(out, tuple) else jax.tree.map(lambda _: out_spec, out_shape),
            scratch_shapes=scratch,
            input_output_aliases=aliases or {},
            cost_estimate=pl.CostEstimate(flops=0, transcendentals=0, bytes_accessed=size),
            compiler_params=pltpu.CompilerParams(vmem_limit_bytes=limit * 1024 * 1024),
        )(*args)

    return run


def trade(value, groups=None):
    return lax.all_to_all(
        value, BOTH, split_axis=0, concat_axis=0, tiled=True, axis_index_groups=groups
    )


def sibling(value):
    n = lax.axis_size("px")
    return lax.ppermute(value, "px", [(i, i ^ 1) for i in range(n)])


def local(
    features,
    weight_one,
    weight_two,
    tile_values,
    tile_rows,
    tile_cols,
    tile_count,
    send_rows,
    send_count,
    stale_hidden,
    stale_grad,
    out_grad,
):
    bf16, f32 = jnp.bfloat16, jnp.float32
    parts = lax.axis_size(BOTH)
    own, width = features.shape
    slots = send_rows.shape[2]
    boundary = parts * slots
    shape = jax.ShapeDtypeStruct
    core = ((lax.axis_index("px") & 1) + 2 * (lax.axis_index("py") & 1)).astype(jnp.int32).reshape(1)
    n_z, n_py = lax.axis_size("px") // 2, lax.axis_size("py")

    square, square32 = shape((own, width), bf16), shape((own, width), f32)
    near, far = shape((own, own), bf16), shape((own, boundary), bf16)
    near32, far32 = shape((own, own), f32), shape((own, boundary), f32)
    slab, slots_in = shape((boundary, width), bf16), shape((parts, slots, width), bf16)
    weight = shape(weight_one.shape, bf16)
    picks = shape((boundary, own), bf16)
    semaphores = lambda count: [pltpu.SemaphoreType.DMA((count,))]
    lines = width * width // LANES
    keep, send = shape((lines, LANES), f32), shape((lines, LANES), bf16)

    outgoing, picked = call(
        pack_kernel,
        (slab, picks),
        0,
        in_vmem(
            square, shape((LANES, parts), jnp.int32), shape((boundary, LANES), f32), picks, slab
        )
        + semaphores(9),
        2,
        PACK,
    )(send_rows[0].T, send_count, features)
    arrived = trade(outgoing.reshape(parts, slots, -1)).reshape(boundary, -1)

    near_adj, far_adj, agg, hidden_grad, grad_out = call(
        local_kernel,
        (near, far, square32, square32, slots_in),
        3,
        in_vmem(
            tile_values, square, square, weight, slab, near32, far32, near, far, picks, square32, square32, slots_in
        )
        + semaphores(11),
        0,
        LOCAL,
    )(tile_rows[0], tile_cols[0], tile_count, tile_values, features, out_grad, weight_two, stale_grad, picked)

    arrived, grad_out = lax.optimization_barrier((arrived, grad_out))
    grads = trade(grad_out)
    hidden, keep, send = call(
        main_kernel,
        (square, keep, send),
        1,
        in_vmem(
            slab, near, far, square32, weight, square32, slab, square, square, keep, send, square, square
        )
        + semaphores(32),
        0,
        MAIN,
    )(core, arrived, near_adj, far_adj, agg, weight_one, hidden_grad, stale_hidden, out_grad)

    other = sibling(send)
    share = 2 * lines // parts
    size = -(-share // 16) * 8
    rows = slots * width // LANES
    mail = call(
        box_kernel,
        shape((parts, rows + size, LANES), bf16),
        0,
        in_vmem(square, picks, shape((parts, rows, LANES), bf16)) + semaphores(3),
        0,
        BOX,
    )(picked, hidden)
    mail = call(
        piece_kernel,
        shape(mail.shape, bf16),
        0,
        in_vmem(shape((parts, size, LANES), bf16)) + semaphores(1),
        2,
        PIECE,
        {2: 0},
    )(keep, other, mail)
    mail, grads = lax.optimization_barrier((mail, grads))
    mail = trade(mail)
    chips = parts // 2
    mine, next_hidden = call(
        functools.partial(sum_kernel, n_z, n_py),
        (shape((chips, share, LANES), bf16), shape((parts, rows, LANES), bf16)),
        1,
        semaphores(1),
        1,
        SUM,
        None,
        (VMEM, HBM),
    )(core, mail)
    next_hidden = next_hidden.reshape(parts, width // LANES, slots, LANES)
    next_hidden = jnp.swapaxes(next_hidden, 1, 2).reshape(boundary, width)
    same_core = [[(2 * z + c) * n_py + i for z in range(n_z) for i in range(n_py)] for c in range(2)]
    mine = trade(mine, same_core)
    grads = grads.reshape(boundary, width)
    next_grad = jnp.where(outgoing == UNUSED, jnp.zeros_like(grads), grads)
    scale = 1.0 / math.sqrt(own * parts)
    one, two = call(
        functools.partial(finish_kernel, scale, size, n_py),
        (shape((width, width), f32),) * 2,
        1,
        in_vmem(*(shape((width, width), f32),) * 2) + semaphores(2 * (width // LANES)),
        None,
        FINISH,
        None,
        HBM,
    )(core, mine, sibling(mine))

    return next_hidden, next_grad, one, two


def solution(mesh):
    in_specs = (
        P(BOTH, None),
        P(),
        P(),
        P(BOTH, None, None),
        P(BOTH, None),
        P(BOTH, None),
        P(BOTH),
        P(BOTH, None, None),
        P(BOTH, None),
        P(BOTH, None),
        P(BOTH, None),
        P(BOTH, None),
    )
    out_specs = (P(BOTH, None), P(BOTH, None), P(), P())
    return jax.shard_map(local, mesh=mesh, in_specs=in_specs, out_specs=out_specs, check_vma=False)
```

```python
import functools
import math

import jax
import jax.numpy as jnp
from jax import lax
from jax.experimental import pallas as pl
from jax.experimental.pallas import tpu as pltpu
from jax.sharding import PartitionSpec as P

BOTH = ("px", "py")
LANES = 128
UNUSED = 2.0**126
PACK, LOCAL, MAIN = 58, 63, 56
BOX, PIECE, SUM, OWN, FINISH = 20, 12, 8, 20, 16
VMEM = pl.BlockSpec(memory_space=pltpu.VMEM)
HBM = pl.BlockSpec(memory_space=pltpu.HBM)
SMEM = pl.BlockSpec(memory_space=pltpu.SMEM)
INV_SQRT2 = 1.0 / math.sqrt(2.0)
INV_SQRT_2PI = 1.0 / math.sqrt(2.0 * math.pi)


def mm(a, b, dims=((1,), (0,))):
    return lax.dot_general(a, b, (dims, ((), ())), preferred_element_type=jnp.float32)


def copies(sems, pairs):
    started = [
        pltpu.make_async_copy(src, dst, sems.at[i]) for i, (src, dst) in enumerate(pairs)
    ]
    for copy in started:
        copy.start()
    return started


def pack_kernel(
    rows_ref, counts_ref, features_hbm, out_hbm, picks_hbm, features, listed, wanted, picks, out, sems
):
    f32, bf16 = jnp.float32, jnp.bfloat16
    (fetch,) = copies(sems, [(features_hbm, features)])
    slots, parts = rows_ref.shape
    boundary, own = picks.shape
    listed[...] = jnp.zeros_like(listed)
    place = lax.broadcasted_iota(jnp.int32, (slots, parts), 0)
    counts = jnp.broadcast_to(counts_ref[...], (slots, parts))
    listed[:slots, :] = jnp.where(place < counts, rows_ref[...] + 1, 0)
    value = listed[...]
    step = boundary // 4
    slot = lax.broadcasted_iota(jnp.int32, (step, LANES), 0)
    lane = lax.broadcasted_iota(jnp.int32, (step, LANES), 1)
    mine = lane == slot % slots
    ones = jnp.ones((LANES, LANES), bf16)
    across = lax.broadcasted_iota(jnp.int32, (step, own), 1).astype(f32)
    saves = []
    for k in range(4):
        at = pl.ds(k * step, step)
        peer = jnp.where(lane == slot // slots + k * (step // slots), 1.0, 0.0).astype(bf16)
        index = jnp.full((step, LANES), -1.0, f32)
        for part, weight in ((value >> 5, 32.0), (value & 31, 1.0)):
            spread = mm(peer, part.astype(f32).astype(bf16), ((1,), (1,)))
            index += weight * mm(jnp.where(mine, spread, 0.0).astype(bf16), ones)
        wanted[at, :] = index
        wide = jnp.concatenate([index] * (own // LANES), axis=1)
        picks[at, :] = jnp.where(wide == across, 1.0, 0.0).astype(bf16)
        saves += copies(sems.at[pl.ds(1 + k, 1)], [(picks.at[at, :], picks_hbm.at[at, :])])
    fetch.wait()
    for k in range(4):
        at = pl.ds(k * step, step)
        row = mm(picks[at, :], features[...])
        unused = wanted[at, :] < 0.0
        for j in range(own // LANES):
            block = slice(j * LANES, (j + 1) * LANES)
            out[at, block] = jnp.where(unused, UNUSED, row[:, block]).astype(bf16)
        saves += copies(sems.at[pl.ds(5 + k, 1)], [(out.at[at, :], out_hbm.at[at, :])])
    for save in saves:
        save.wait()


def local_kernel(
    rows_ref,
    cols_ref,
    count_ref,
    tiles_hbm,
    features_hbm,
    out_grad_hbm,
    weight_hbm,
    stale_grad_hbm,
    picks_hbm,
    near_hbm,
    far_hbm,
    agg_hbm,
    hidden_grad_hbm,
    grad_out_hbm,
    tiles,
    features,
    out_grad,
    weight,
    stale_grad,
    near32,
    far32,
    near,
    far,
    picks,
    agg,
    hidden_grad,
    grad_out,
    sems,
):
    tile = tiles.shape[1]
    own = features.shape[0]
    fetches = copies(
        sems,
        [
            (tiles_hbm, tiles),
            (out_grad_hbm, out_grad),
            (weight_hbm, weight),
            (features_hbm, features),
            (stale_grad_hbm, stale_grad),
            (picks_hbm, picks),
        ],
    )
    near32[...] = jnp.zeros_like(near32)
    far32[...] = jnp.zeros_like(far32)
    fetches[0].wait()

    @pl.loop(0, count_ref[0])
    def _(t):
        r = pl.multiple_of(rows_ref[t] * tile, tile)
        c = pl.multiple_of(cols_ref[t] * tile, tile)
        value = tiles[t].astype(jnp.float32)

        @pl.when(c < own)
        def _():
            near32[pl.ds(r, tile), pl.ds(c, tile)] += value

        @pl.when(c >= own)
        def _():
            far32[pl.ds(r, tile), pl.ds(pl.multiple_of(c - own, tile), tile)] += value

    near[...] = near32[...].astype(near.dtype)
    far[...] = far32[...].astype(far.dtype)
    saves = copies(sems.at[pl.ds(6, 2)], [(near, near_hbm), (far, far_hbm)])
    fetches[3].wait()
    agg[...] = mm(near[...], features[...])
    saves += copies(sems.at[pl.ds(8, 1)], [(agg, agg_hbm)])
    fetches[1].wait()
    fetches[2].wait()
    down = mm(out_grad[...], weight[...], ((1,), (1,))).astype(jnp.bfloat16)
    remote = mm(far[...], down, ((0,), (0,)))
    grad_out[...] = remote.reshape(grad_out.shape).astype(grad_out.dtype)
    saves += copies(sems.at[pl.ds(9, 1)], [(grad_out, grad_out_hbm)])
    fetches[4].wait()
    fetches[5].wait()
    hidden_grad[...] = mm(near[...], down, ((0,), (0,))) + mm(
        picks[...], stale_grad[...], ((0,), (0,))
    )
    saves += copies(sems.at[pl.ds(10, 1)], [(hidden_grad, hidden_grad_hbm)])
    for save in saves:
        save.wait()


def main_kernel(
    core_ref,
    arrived_hbm,
    near_hbm,
    far_hbm,
    agg_hbm,
    weight_hbm,
    hidden_grad_hbm,
    stale_hidden_hbm,
    out_grad_hbm,
    hidden_hbm,
    keep_hbm,
    send_hbm,
    arrived,
    near,
    far,
    agg,
    weight,
    hidden_grad,
    stale_hidden,
    out_grad,
    hidden,
    keep,
    send,
    first_agg,
    pre_grad,
    sems,
):
    own, width = agg.shape
    step = 256
    blocks = own // step
    loads = [(arrived_hbm, arrived)]
    for i in range(blocks):
        at = pl.ds(i * step, step)
        loads += [(far_hbm.at[at, :], far.at[at, :]), (agg_hbm.at[at, :], agg.at[at, :])]
        if i == 0:
            loads += [(weight_hbm, weight)]
    loads += [
        (stale_hidden_hbm, stale_hidden),
        (hidden_grad_hbm, hidden_grad),
        (near_hbm, near),
        (out_grad_hbm, out_grad),
    ]
    fetches = copies(sems, loads)
    n = len(fetches)
    fetches[0].wait()
    fetches[n - 4].wait()
    for k in range(width // LANES):
        at = slice(k * LANES, (k + 1) * LANES)
        came = arrived[:, at].astype(jnp.float32)
        heard = came != UNUSED
        arrived[:, at] = jnp.where(heard, came, 0.0).astype(arrived.dtype)
        stale = stale_hidden[:, at].astype(jnp.float32)
        stale_hidden[:, at] = jnp.where(heard, stale, 0.0).astype(stale_hidden.dtype)
    for i in range(blocks):
        at = pl.ds(i * step, step)
        for fetch in fetches[1:4] if i == 0 else fetches[2 + 2 * i : 4 + 2 * i]:
            fetch.wait()
        agg_one = (agg[at, :] + mm(far[at, :], arrived[...])).astype(jnp.bfloat16)
        first_agg[at, :] = agg_one
        pre = mm(agg_one, weight[...])
        cdf = 0.5 * (1.0 + lax.erf(pre * INV_SQRT2))
        hidden[at, :] = (pre * cdf).astype(jnp.bfloat16)
        slope = cdf + pre * (jnp.exp(-0.5 * pre * pre) * INV_SQRT_2PI)
        if i == 0:
            fetches[n - 3].wait()
        pre_grad[at, :] = (hidden_grad[at, :] * slope).astype(jnp.bfloat16)
    saves = copies(sems.at[pl.ds(n, 1)], [(hidden, hidden_hbm)])
    fetches[n - 2].wait()
    agg_two = (mm(far[...], stale_hidden[...]) + mm(near[...], hidden[...])).astype(jnp.bfloat16)
    fetches[n - 1].wait()
    part_two = mm(agg_two, out_grad[...], ((0,), (0,)))
    part_one = mm(first_agg[...], pre_grad[...], ((0,), (0,)))
    first = (core_ref[0] & 1) == 0
    for k in range(width // LANES):
        at = slice(k * LANES, (k + 1) * LANES)
        one, two = part_one[:, at], part_two[:, at]
        rows = pl.ds(k * width, width)
        keep[rows, :] = jnp.where(first, one, two)
        send[rows, :] = jnp.where(first, two, one).astype(send.dtype)
        saves += copies(
            sems.at[pl.ds(n + 1 + 2 * k, 2)],
            [(send.at[rows, :], send_hbm.at[rows, :]), (keep.at[rows, :], keep_hbm.at[rows, :])],
        )
    for save in saves:
        save.wait()


def box_kernel(picks_hbm, hidden_hbm, mail_hbm, hidden, picks, box, sems):
    for fetch in copies(sems, [(hidden_hbm, hidden), (picks_hbm, picks)]):
        fetch.wait()
    parts, blocks = box.shape[0], hidden.shape[1] // LANES
    slots = box.shape[1] // blocks
    picked = mm(picks[...], hidden[...])
    for k in range(blocks):
        block = picked[:, k * LANES : (k + 1) * LANES].reshape(parts, slots, LANES)
        box[:, k * slots : (k + 1) * slots, :] = block.astype(box.dtype)
    (save,) = copies(sems.at[pl.ds(2, 1)], [(box, mail_hbm.at[:, : box.shape[1], :])])
    save.wait()


def piece_kernel(keep_ref, other_ref, _, mail_hbm, pieces, sems):
    parts, size = pieces.shape[0], pieces.shape[1]
    share = 2 * keep_ref.shape[0] // parts
    for j in range(parts // 2):
        lines = pl.ds(j * share, share)
        total = keep_ref[lines, :] + other_ref[lines, :].astype(jnp.float32)
        pieces[2 * j] = total[:size].astype(pieces.dtype)
        pieces[2 * j + 1] = total[share - size :].astype(pieces.dtype)
    start = mail_hbm.shape[1] - size
    (save,) = copies(sems, [(pieces, mail_hbm.at[:, start:, :])])
    save.wait()


def sum_kernel(n_z, n_py, core_ref, mail_ref, out_ref, hidden_hbm, sems):
    chips, share = out_ref.shape[:2]
    start = hidden_hbm.shape[1]
    size = mail_ref.shape[1] - start
    saves = copies(sems, [(mail_ref.at[:, pl.ds(0, start), :], hidden_hbm)])
    sums = []
    for c in range(2):
        total = None
        for z in range(n_z):
            first = (z * 2 + c) * n_py
            block = mail_ref[first : first + n_py, start:, :].astype(jnp.float32).sum(0)
            total = block if total is None else total + block
        sums.append(total)
    rest = share - size

    def give(one, two):
        both = jnp.concatenate([one, two], axis=0).astype(out_ref.dtype)
        out_ref[...] = jnp.broadcast_to(both[None], (chips, share, LANES))

    @pl.when(core_ref[0] < 2)
    def _():
        give(sums[0], sums[1][:rest])

    @pl.when(core_ref[0] >= 2)
    def _():
        give(sums[0][size - rest :], sums[1])

    for save in saves:
        save.wait()


def fill_half(scale, size, n_py, c, source_ref, one, two, one_hbm, two_hbm, sems):
    chips, share = source_ref.shape[:2]
    rest = share - size
    width = one.shape[0]
    saves = []
    for z in range(chips // n_py):
        first = (z * 2 + c) * n_py
        for q in range(first, first + n_py):
            pair, odd = divmod(q, 2)
            spans = ((size, rest, one), (rest, size, two)) if odd else ((0, size, one), (0, rest, two))
            at = 0
            for skip, count, out in spans:
                line = pair * share + skip
                end = line + count
                while line < end:
                    k, r = divmod(line, width)
                    run = min(end - line, width - r)
                    value = source_ref[z * n_py + q - first, at : at + run, :]
                    block = slice(k * LANES, (k + 1) * LANES)
                    out[r : r + run, block] = value.astype(jnp.float32) * scale
                    line += run
                    at += run
        line, end = first * share // 2, (first + n_py) * share // 2
        while line < end:
            k, r = divmod(line, width)
            run = min(end - line, width - r)
            rows, block = slice(r, r + run), slice(k * LANES, (k + 1) * LANES)
            saves += copies(
                sems.at[pl.ds(len(saves), 2)],
                [
                    (one.at[rows, block], one_hbm.at[rows, block]),
                    (two.at[rows, block], two_hbm.at[rows, block]),
                ],
            )
            line += run
    for save in saves:
        save.wait()


def own_half_kernel(
    scale, size, n_py, core_ref, mine_ref, sent_hbm, grads_hbm, one_hbm, two_hbm, next_hbm, one, two, sent, grads, sems
):
    fetches = copies(sems, [(sent_hbm, sent), (grads_hbm, grads)])
    for c in range(2):

        @pl.when((core_ref[0] & 1) == c)
        def _():
            fill_half(scale, size, n_py, c, mine_ref, one, two, one_hbm, two_hbm, sems.at[pl.ds(6, 16)])

    for fetch in fetches:
        fetch.wait()
    saves = []
    step = grads.shape[0] // 4
    for k in range(4):
        at = pl.ds(k * step, step)
        used = sent[at, :].astype(jnp.float32) != UNUSED
        grads[at, :] = jnp.where(used, grads[at, :].astype(jnp.float32), 0.0).astype(grads.dtype)
        saves += copies(sems.at[pl.ds(2 + k, 1)], [(grads.at[at, :], next_hbm.at[at, :])])
    for save in saves:
        save.wait()


def other_half_kernel(scale, size, n_py, core_ref, other_ref, _, __, one_hbm, two_hbm, one, two, sems):
    for c in range(2):

        @pl.when((core_ref[0] & 1) != c)
        def _():
            fill_half(scale, size, n_py, c, other_ref, one, two, one_hbm, two_hbm, sems)


def in_vmem(*refs):
    return [pltpu.VMEM(r.shape, r.dtype) for r in refs]


def call(kernel, out_shape, scalars, scratch=(), vmem=None, limit=6, aliases=None, out=None):
    def run(*args):
        n_vmem = len(args) - scalars if vmem is None else vmem
        size = sum(a.size * a.dtype.itemsize for a in (*args, *jax.tree.leaves(out_shape)))
        out_spec = (VMEM if vmem is None else HBM) if out is None else out
        return pl.pallas_call(
            kernel,
            out_shape=out_shape,
            in_specs=[SMEM] * scalars + [VMEM] * n_vmem + [HBM] * (len(args) - scalars - n_vmem),
            out_specs=out_spec if isinstance(out, tuple) else jax.tree.map(lambda _: out_spec, out_shape),
            scratch_shapes=scratch,
            input_output_aliases=aliases or {},
            cost_estimate=pl.CostEstimate(flops=0, transcendentals=0, bytes_accessed=size),
            compiler_params=pltpu.CompilerParams(vmem_limit_bytes=limit * 1024 * 1024),
        )(*args)

    return run


def trade(value, groups=None):
    return lax.all_to_all(
        value, BOTH, split_axis=0, concat_axis=0, tiled=True, axis_index_groups=groups
    )


def sibling(value):
    n = lax.axis_size("px")
    return lax.ppermute(value, "px", [(i, i ^ 1) for i in range(n)])


def local(
    features,
    weight_one,
    weight_two,
    tile_values,
    tile_rows,
    tile_cols,
    tile_count,
    send_rows,
    send_count,
    stale_hidden,
    stale_grad,
    out_grad,
):
    bf16, f32 = jnp.bfloat16, jnp.float32
    parts = lax.axis_size(BOTH)
    own, width = features.shape
    slots = send_rows.shape[2]
    boundary = parts * slots
    shape = jax.ShapeDtypeStruct
    core = ((lax.axis_index("px") & 1) + 2 * (lax.axis_index("py") & 1)).astype(jnp.int32).reshape(1)
    n_z, n_py = lax.axis_size("px") // 2, lax.axis_size("py")

    square, square32 = shape((own, width), bf16), shape((own, width), f32)
    near, far = shape((own, own), bf16), shape((own, boundary), bf16)
    near32, far32 = shape((own, own), f32), shape((own, boundary), f32)
    slab, slots_in = shape((boundary, width), bf16), shape((parts, slots, width), bf16)
    weight = shape(weight_one.shape, bf16)
    picks = shape((boundary, own), bf16)
    semaphores = lambda count: [pltpu.SemaphoreType.DMA((count,))]
    lines = width * width // LANES
    keep, send = shape((lines, LANES), f32), shape((lines, LANES), bf16)

    outgoing, picked = call(
        pack_kernel,
        (slab, picks),
        0,
        in_vmem(
            square, shape((LANES, parts), jnp.int32), shape((boundary, LANES), f32), picks, slab
        )
        + semaphores(9),
        2,
        PACK,
    )(send_rows[0].T, send_count, features)
    arrived = trade(outgoing.reshape(parts, slots, -1)).reshape(boundary, -1)

    near_adj, far_adj, agg, hidden_grad, grad_out = call(
        local_kernel,
        (near, far, square32, square32, slots_in),
        3,
        in_vmem(
            tile_values, square, square, weight, slab, near32, far32, near, far, picks, square32, square32, slots_in
        )
        + semaphores(11),
        0,
        LOCAL,
    )(tile_rows[0], tile_cols[0], tile_count, tile_values, features, out_grad, weight_two, stale_grad, picked)

    arrived, grad_out = lax.optimization_barrier((arrived, grad_out))
    grads = trade(grad_out)
    hidden, keep, send = call(
        main_kernel,
        (square, keep, send),
        1,
        in_vmem(
            slab, near, far, square32, weight, square32, slab, square, square, keep, send, square, square
        )
        + semaphores(32),
        0,
        MAIN,
    )(core, arrived, near_adj, far_adj, agg, weight_one, hidden_grad, stale_hidden, out_grad)

    other = sibling(send)
    share = 2 * lines // parts
    size = -(-share // 16) * 8
    rows = slots * width // LANES
    mail = call(
        box_kernel,
        shape((parts, rows + size, LANES), bf16),
        0,
        in_vmem(square, picks, shape((parts, rows, LANES), bf16)) + semaphores(3),
        0,
        BOX,
    )(picked, hidden)
    mail = call(
        piece_kernel,
        shape(mail.shape, bf16),
        0,
        in_vmem(shape((parts, size, LANES), bf16)) + semaphores(1),
        2,
        PIECE,
        {2: 0},
    )(keep, other, mail)
    mail, grads = lax.optimization_barrier((mail, grads))
    mail = trade(mail)
    chips = parts // 2
    mine, next_hidden = call(
        functools.partial(sum_kernel, n_z, n_py),
        (shape((chips, share, LANES), bf16), shape((parts, rows, LANES), bf16)),
        1,
        semaphores(1),
        1,
        SUM,
        None,
        (VMEM, HBM),
    )(core, mail)
    next_hidden = next_hidden.reshape(parts, width // LANES, slots, LANES)
    next_hidden = jnp.swapaxes(next_hidden, 1, 2).reshape(boundary, width)
    same_core = [[(2 * z + c) * n_py + i for z in range(n_z) for i in range(n_py)] for c in range(2)]
    mine = trade(mine, same_core)
    scale = 1.0 / math.sqrt(own * parts)
    whole = shape((width, width), f32)
    other = sibling(mine)
    one, two, next_grad = call(
        functools.partial(own_half_kernel, scale, size, n_py),
        (whole, whole, slab),
        1,
        in_vmem(whole, whole, slab, slab) + semaphores(22),
        1,
        OWN,
        None,
        HBM,
    )(core, mine, outgoing, grads.reshape(boundary, width))
    one, two = call(
        functools.partial(other_half_kernel, scale, size, n_py),
        (whole, whole),
        1,
        in_vmem(whole, whole) + semaphores(16),
        1,
        FINISH,
        {2: 0, 3: 1},
        HBM,
    )(core, other, one, two)

    return next_hidden, next_grad, one, two


def solution(mesh):
    in_specs = (
        P(BOTH, None),
        P(),
        P(),
        P(BOTH, None, None),
        P(BOTH, None),
        P(BOTH, None),
        P(BOTH),
        P(BOTH, None, None),
        P(BOTH, None),
        P(BOTH, None),
        P(BOTH, None),
        P(BOTH, None),
    )
    out_specs = (P(BOTH, None), P(BOTH, None), P(), P())
    return jax.shard_map(local, mesh=mesh, in_specs=in_specs, out_specs=out_specs, check_vma=False)
```

```python
import functools
import math

import jax
import jax.numpy as jnp
from jax import lax
from jax.experimental import pallas as pl
from jax.experimental.pallas import tpu as pltpu
from jax.sharding import PartitionSpec as P

BOTH = ("px", "py")
LANES = 128
UNUSED = 2.0**126
PACK, LOCAL, MAIN = 58, 63, 56
BOX, PIECE, SUM, OWN, FINISH = 20, 12, 8, 20, 16
VMEM = pl.BlockSpec(memory_space=pltpu.VMEM)
HBM = pl.BlockSpec(memory_space=pltpu.HBM)
SMEM = pl.BlockSpec(memory_space=pltpu.SMEM)
INV_SQRT2 = 1.0 / math.sqrt(2.0)
INV_SQRT_2PI = 1.0 / math.sqrt(2.0 * math.pi)


def mm(a, b, dims=((1,), (0,))):
    return lax.dot_general(a, b, (dims, ((), ())), preferred_element_type=jnp.float32)


def copies(sems, pairs):
    started = [
        pltpu.make_async_copy(src, dst, sems.at[i]) for i, (src, dst) in enumerate(pairs)
    ]
    for copy in started:
        copy.start()
    return started


def pack_kernel(
    rows_ref, counts_ref, features_hbm, out_hbm, picks_hbm, features, listed, wanted, picks, out, sems
):
    f32, bf16 = jnp.float32, jnp.bfloat16
    (fetch,) = copies(sems, [(features_hbm, features)])
    slots, parts = rows_ref.shape
    boundary, own = picks.shape
    listed[...] = jnp.zeros_like(listed)
    place = lax.broadcasted_iota(jnp.int32, (slots, parts), 0)
    counts = jnp.broadcast_to(counts_ref[...], (slots, parts))
    listed[:slots, :] = jnp.where(place < counts, rows_ref[...] + 1, 0)
    value = listed[...]
    step = boundary // 4
    slot = lax.broadcasted_iota(jnp.int32, (step, LANES), 0)
    lane = lax.broadcasted_iota(jnp.int32, (step, LANES), 1)
    mine = lane == slot % slots
    ones = jnp.ones((LANES, LANES), bf16)
    across = lax.broadcasted_iota(jnp.int32, (step, own), 1).astype(f32)
    saves = []
    for k in range(4):
        at = pl.ds(k * step, step)
        peer = jnp.where(lane == slot // slots + k * (step // slots), 1.0, 0.0).astype(bf16)
        index = jnp.full((step, LANES), -1.0, f32)
        for part, weight in ((value >> 5, 32.0), (value & 31, 1.0)):
            spread = mm(peer, part.astype(f32).astype(bf16), ((1,), (1,)))
            index += weight * mm(jnp.where(mine, spread, 0.0).astype(bf16), ones)
        wanted[at, :] = index
        wide = jnp.concatenate([index] * (own // LANES), axis=1)
        picks[at, :] = jnp.where(wide == across, 1.0, 0.0).astype(bf16)
        saves += copies(sems.at[pl.ds(1 + k, 1)], [(picks.at[at, :], picks_hbm.at[at, :])])
    fetch.wait()
    for k in range(4):
        at = pl.ds(k * step, step)
        row = mm(picks[at, :], features[...])
        unused = wanted[at, :] < 0.0
        for j in range(own // LANES):
            block = slice(j * LANES, (j + 1) * LANES)
            out[at, block] = jnp.where(unused, UNUSED, row[:, block]).astype(bf16)
        saves += copies(sems.at[pl.ds(5 + k, 1)], [(out.at[at, :], out_hbm.at[at, :])])
    for save in saves:
        save.wait()


def local_kernel(
    rows_ref,
    cols_ref,
    count_ref,
    tiles_hbm,
    features_hbm,
    out_grad_hbm,
    weight_hbm,
    stale_grad_hbm,
    picks_hbm,
    near_hbm,
    far_hbm,
    agg_hbm,
    hidden_grad_hbm,
    grad_out_hbm,
    tiles,
    features,
    out_grad,
    weight,
    stale_grad,
    near32,
    far32,
    near,
    far,
    picks,
    agg,
    hidden_grad,
    grad_out,
    sems,
):
    tile = tiles.shape[1]
    own = features.shape[0]
    fetches = copies(
        sems,
        [
            (tiles_hbm, tiles),
            (out_grad_hbm, out_grad),
            (weight_hbm, weight),
            (features_hbm, features),
            (stale_grad_hbm, stale_grad),
            (picks_hbm, picks),
        ],
    )
    near32[...] = jnp.zeros_like(near32)
    far32[...] = jnp.zeros_like(far32)
    fetches[0].wait()

    @pl.loop(0, count_ref[0])
    def _(t):
        r = pl.multiple_of(rows_ref[t] * tile, tile)
        c = pl.multiple_of(cols_ref[t] * tile, tile)
        value = tiles[t].astype(jnp.float32)

        @pl.when(c < own)
        def _():
            near32[pl.ds(r, tile), pl.ds(c, tile)] += value

        @pl.when(c >= own)
        def _():
            far32[pl.ds(r, tile), pl.ds(pl.multiple_of(c - own, tile), tile)] += value

    near[...] = near32[...].astype(near.dtype)
    far[...] = far32[...].astype(far.dtype)
    saves = copies(sems.at[pl.ds(6, 2)], [(near, near_hbm), (far, far_hbm)])
    fetches[3].wait()
    agg[...] = mm(near[...], features[...])
    saves += copies(sems.at[pl.ds(8, 1)], [(agg, agg_hbm)])
    fetches[1].wait()
    fetches[2].wait()
    down = mm(out_grad[...], weight[...], ((1,), (1,))).astype(jnp.bfloat16)
    remote = mm(far[...], down, ((0,), (0,)))
    grad_out[...] = remote.reshape(grad_out.shape).astype(grad_out.dtype)
    saves += copies(sems.at[pl.ds(9, 1)], [(grad_out, grad_out_hbm)])
    fetches[4].wait()
    fetches[5].wait()
    hidden_grad[...] = mm(near[...], down, ((0,), (0,))) + mm(
        picks[...], stale_grad[...], ((0,), (0,))
    )
    saves += copies(sems.at[pl.ds(10, 1)], [(hidden_grad, hidden_grad_hbm)])
    for save in saves:
        save.wait()


def main_kernel(
    core_ref,
    arrived_hbm,
    near_hbm,
    far_hbm,
    agg_hbm,
    weight_hbm,
    hidden_grad_hbm,
    stale_hidden_hbm,
    out_grad_hbm,
    hidden_hbm,
    keep_hbm,
    send_hbm,
    arrived,
    near,
    far,
    agg,
    weight,
    hidden_grad,
    stale_hidden,
    out_grad,
    hidden,
    keep,
    send,
    first_agg,
    pre_grad,
    sems,
):
    own, width = agg.shape
    step = 256
    blocks = own // step
    loads = [(arrived_hbm, arrived)]
    for i in range(blocks):
        at = pl.ds(i * step, step)
        loads += [(far_hbm.at[at, :], far.at[at, :]), (agg_hbm.at[at, :], agg.at[at, :])]
        if i == 0:
            loads += [(weight_hbm, weight)]
    loads += [
        (stale_hidden_hbm, stale_hidden),
        (hidden_grad_hbm, hidden_grad),
        (near_hbm, near),
        (out_grad_hbm, out_grad),
    ]
    fetches = copies(sems, loads)
    n = len(fetches)
    fetches[0].wait()
    fetches[n - 4].wait()
    for k in range(width // LANES):
        at = slice(k * LANES, (k + 1) * LANES)
        came = arrived[:, at].astype(jnp.float32)
        heard = came != UNUSED
        arrived[:, at] = jnp.where(heard, came, 0.0).astype(arrived.dtype)
        stale = stale_hidden[:, at].astype(jnp.float32)
        stale_hidden[:, at] = jnp.where(heard, stale, 0.0).astype(stale_hidden.dtype)
    for i in range(blocks):
        at = pl.ds(i * step, step)
        for fetch in fetches[1:4] if i == 0 else fetches[2 + 2 * i : 4 + 2 * i]:
            fetch.wait()
        agg_one = (agg[at, :] + mm(far[at, :], arrived[...])).astype(jnp.bfloat16)
        first_agg[at, :] = agg_one
        pre = mm(agg_one, weight[...])
        cdf = 0.5 * (1.0 + lax.erf(pre * INV_SQRT2))
        hidden[at, :] = (pre * cdf).astype(jnp.bfloat16)
        slope = cdf + pre * (jnp.exp(-0.5 * pre * pre) * INV_SQRT_2PI)
        if i == 0:
            fetches[n - 3].wait()
        pre_grad[at, :] = (hidden_grad[at, :] * slope).astype(jnp.bfloat16)
    saves = copies(sems.at[pl.ds(n, 1)], [(hidden, hidden_hbm)])
    fetches[n - 2].wait()
    agg_two = (mm(far[...], stale_hidden[...]) + mm(near[...], hidden[...])).astype(jnp.bfloat16)
    fetches[n - 1].wait()
    part_two = mm(agg_two, out_grad[...], ((0,), (0,)))
    part_one = mm(first_agg[...], pre_grad[...], ((0,), (0,)))
    first = (core_ref[0] & 1) == 0
    for k in range(width // LANES):
        at = slice(k * LANES, (k + 1) * LANES)
        one, two = part_one[:, at], part_two[:, at]
        rows = pl.ds(k * width, width)
        keep[rows, :] = jnp.where(first, one, two)
        send[rows, :] = jnp.where(first, two, one).astype(send.dtype)
        saves += copies(
            sems.at[pl.ds(n + 1 + 2 * k, 2)],
            [(send.at[rows, :], send_hbm.at[rows, :]), (keep.at[rows, :], keep_hbm.at[rows, :])],
        )
    for save in saves:
        save.wait()


def box_kernel(picks_hbm, hidden_hbm, mail_hbm, hidden, picks, box, sems):
    for fetch in copies(sems, [(hidden_hbm, hidden), (picks_hbm, picks)]):
        fetch.wait()
    parts, blocks = box.shape[0], hidden.shape[1] // LANES
    slots = box.shape[1] // blocks
    picked = mm(picks[...], hidden[...])
    for k in range(blocks):
        block = picked[:, k * LANES : (k + 1) * LANES].reshape(parts, slots, LANES)
        box[:, k * slots : (k + 1) * slots, :] = block.astype(box.dtype)
    (save,) = copies(sems.at[pl.ds(2, 1)], [(box, mail_hbm.at[:, : box.shape[1], :])])
    save.wait()


def piece_kernel(keep_ref, other_ref, _, mail_hbm, pieces, sems):
    parts, size = pieces.shape[0], pieces.shape[1]
    share = 2 * keep_ref.shape[0] // parts
    for j in range(parts // 2):
        lines = pl.ds(j * share, share)
        total = keep_ref[lines, :] + other_ref[lines, :].astype(jnp.float32)
        pieces[2 * j] = total[:size].astype(pieces.dtype)
        pieces[2 * j + 1] = total[share - size :].astype(pieces.dtype)
    start = mail_hbm.shape[1] - size
    (save,) = copies(sems, [(pieces, mail_hbm.at[:, start:, :])])
    save.wait()


def sum_kernel(n_z, n_py, core_ref, mail_ref, out_ref, hidden_hbm, sems):
    chips, share = out_ref.shape[:2]
    start = hidden_hbm.shape[1]
    size = mail_ref.shape[1] - start
    saves = copies(sems, [(mail_ref.at[:, pl.ds(0, start), :], hidden_hbm)])
    sums = []
    for c in range(2):
        total = None
        for z in range(n_z):
            first = (z * 2 + c) * n_py
            block = mail_ref[first : first + n_py, start:, :].astype(jnp.float32).sum(0)
            total = block if total is None else total + block
        sums.append(total)
    rest = share - size

    def give(one, two):
        both = jnp.concatenate([one, two], axis=0).astype(out_ref.dtype)
        out_ref[...] = jnp.broadcast_to(both[None], (chips, share, LANES))

    @pl.when(core_ref[0] < 2)
    def _():
        give(sums[0], sums[1][:rest])

    @pl.when(core_ref[0] >= 2)
    def _():
        give(sums[0][size - rest :], sums[1])

    for save in saves:
        save.wait()


def fill_half(scale, size, n_py, c, source_ref, one, two, one_hbm, two_hbm, sems, meanwhile=None):
    chips, share = source_ref.shape[:2]
    rest = share - size
    width = one.shape[0]
    saves = []
    for z in range(chips // n_py):
        first = (z * 2 + c) * n_py
        for q in range(first, first + n_py):
            pair, odd = divmod(q, 2)
            spans = ((size, rest, one), (rest, size, two)) if odd else ((0, size, one), (0, rest, two))
            at = 0
            for skip, count, out in spans:
                line = pair * share + skip
                end = line + count
                while line < end:
                    k, r = divmod(line, width)
                    run = min(end - line, width - r)
                    value = source_ref[z * n_py + q - first, at : at + run, :]
                    block = slice(k * LANES, (k + 1) * LANES)
                    out[r : r + run, block] = value.astype(jnp.float32) * scale
                    line += run
                    at += run
        line, end = first * share // 2, (first + n_py) * share // 2
        while line < end:
            k, r = divmod(line, width)
            run = min(end - line, width - r)
            rows, block = slice(r, r + run), slice(k * LANES, (k + 1) * LANES)
            saves += copies(
                sems.at[pl.ds(len(saves), 2)],
                [
                    (one.at[rows, block], one_hbm.at[rows, block]),
                    (two.at[rows, block], two_hbm.at[rows, block]),
                ],
            )
            line += run
    if meanwhile is not None:
        saves += meanwhile()
    for save in saves:
        save.wait()


def own_half_kernel(
    scale, size, n_py, core_ref, mine_ref, sent_hbm, grads_hbm, one_hbm, two_hbm, next_hbm, one, two, sent, grads, sems
):
    fetches = copies(sems, [(sent_hbm, sent), (grads_hbm, grads)])

    def clear():
        for fetch in fetches:
            fetch.wait()
        saves = []
        step = grads.shape[0] // 4
        for k in range(4):
            at = pl.ds(k * step, step)
            used = sent[at, :].astype(jnp.float32) != UNUSED
            grads[at, :] = jnp.where(used, grads[at, :].astype(jnp.float32), 0.0).astype(grads.dtype)
            saves += copies(sems.at[pl.ds(2 + k, 1)], [(grads.at[at, :], next_hbm.at[at, :])])
        return saves

    for c in range(2):

        @pl.when((core_ref[0] & 1) == c)
        def _():
            own = sems.at[pl.ds(6, 16)]
            fill_half(scale, size, n_py, c, mine_ref, one, two, one_hbm, two_hbm, own, clear)


def other_half_kernel(scale, size, n_py, core_ref, other_ref, _, __, one_hbm, two_hbm, one, two, sems):
    for c in range(2):

        @pl.when((core_ref[0] & 1) != c)
        def _():
            fill_half(scale, size, n_py, c, other_ref, one, two, one_hbm, two_hbm, sems)


def in_vmem(*refs):
    return [pltpu.VMEM(r.shape, r.dtype) for r in refs]


def call(kernel, out_shape, scalars, scratch=(), vmem=None, limit=6, aliases=None, out=None):
    def run(*args):
        n_vmem = len(args) - scalars if vmem is None else vmem
        size = sum(a.size * a.dtype.itemsize for a in (*args, *jax.tree.leaves(out_shape)))
        out_spec = (VMEM if vmem is None else HBM) if out is None else out
        return pl.pallas_call(
            kernel,
            out_shape=out_shape,
            in_specs=[SMEM] * scalars + [VMEM] * n_vmem + [HBM] * (len(args) - scalars - n_vmem),
            out_specs=out_spec if isinstance(out, tuple) else jax.tree.map(lambda _: out_spec, out_shape),
            scratch_shapes=scratch,
            input_output_aliases=aliases or {},
            cost_estimate=pl.CostEstimate(flops=0, transcendentals=0, bytes_accessed=size),
            compiler_params=pltpu.CompilerParams(vmem_limit_bytes=limit * 1024 * 1024),
        )(*args)

    return run


def trade(value, groups=None):
    return lax.all_to_all(
        value, BOTH, split_axis=0, concat_axis=0, tiled=True, axis_index_groups=groups
    )


def sibling(value):
    n = lax.axis_size("px")
    return lax.ppermute(value, "px", [(i, i ^ 1) for i in range(n)])


def local(
    features,
    weight_one,
    weight_two,
    tile_values,
    tile_rows,
    tile_cols,
    tile_count,
    send_rows,
    send_count,
    stale_hidden,
    stale_grad,
    out_grad,
):
    bf16, f32 = jnp.bfloat16, jnp.float32
    parts = lax.axis_size(BOTH)
    own, width = features.shape
    slots = send_rows.shape[2]
    boundary = parts * slots
    shape = jax.ShapeDtypeStruct
    core = ((lax.axis_index("px") & 1) + 2 * (lax.axis_index("py") & 1)).astype(jnp.int32).reshape(1)
    n_z, n_py = lax.axis_size("px") // 2, lax.axis_size("py")

    square, square32 = shape((own, width), bf16), shape((own, width), f32)
    near, far = shape((own, own), bf16), shape((own, boundary), bf16)
    near32, far32 = shape((own, own), f32), shape((own, boundary), f32)
    slab, slots_in = shape((boundary, width), bf16), shape((parts, slots, width), bf16)
    weight = shape(weight_one.shape, bf16)
    picks = shape((boundary, own), bf16)
    semaphores = lambda count: [pltpu.SemaphoreType.DMA((count,))]
    lines = width * width // LANES
    keep, send = shape((lines, LANES), f32), shape((lines, LANES), bf16)

    outgoing, picked = call(
        pack_kernel,
        (slab, picks),
        0,
        in_vmem(
            square, shape((LANES, parts), jnp.int32), shape((boundary, LANES), f32), picks, slab
        )
        + semaphores(9),
        2,
        PACK,
    )(send_rows[0].T, send_count, features)
    arrived = trade(outgoing.reshape(parts, slots, -1)).reshape(boundary, -1)

    near_adj, far_adj, agg, hidden_grad, grad_out = call(
        local_kernel,
        (near, far, square32, square32, slots_in),
        3,
        in_vmem(
            tile_values, square, square, weight, slab, near32, far32, near, far, picks, square32, square32, slots_in
        )
        + semaphores(11),
        0,
        LOCAL,
    )(tile_rows[0], tile_cols[0], tile_count, tile_values, features, out_grad, weight_two, stale_grad, picked)

    arrived, grad_out = lax.optimization_barrier((arrived, grad_out))
    grads = trade(grad_out)
    hidden, keep, send = call(
        main_kernel,
        (square, keep, send),
        1,
        in_vmem(
            slab, near, far, square32, weight, square32, slab, square, square, keep, send, square, square
        )
        + semaphores(32),
        0,
        MAIN,
    )(core, arrived, near_adj, far_adj, agg, weight_one, hidden_grad, stale_hidden, out_grad)

    other = sibling(send)
    share = 2 * lines // parts
    size = -(-share // 16) * 8
    rows = slots * width // LANES
    mail = call(
        box_kernel,
        shape((parts, rows + size, LANES), bf16),
        0,
        in_vmem(square, picks, shape((parts, rows, LANES), bf16)) + semaphores(3),
        0,
        BOX,
    )(picked, hidden)
    mail = call(
        piece_kernel,
        shape(mail.shape, bf16),
        0,
        in_vmem(shape((parts, size, LANES), bf16)) + semaphores(1),
        2,
        PIECE,
        {2: 0},
    )(keep, other, mail)
    mail, grads = lax.optimization_barrier((mail, grads))
    mail = trade(mail)
    chips = parts // 2
    mine, next_hidden = call(
        functools.partial(sum_kernel, n_z, n_py),
        (shape((chips, share, LANES), bf16), shape((parts, rows, LANES), bf16)),
        1,
        semaphores(1),
        1,
        SUM,
        None,
        (VMEM, HBM),
    )(core, mail)
    next_hidden = next_hidden.reshape(parts, width // LANES, slots, LANES)
    next_hidden = jnp.swapaxes(next_hidden, 1, 2).reshape(boundary, width)
    same_core = [[(2 * z + c) * n_py + i for z in range(n_z) for i in range(n_py)] for c in range(2)]
    mine = trade(mine, same_core)
    scale = 1.0 / math.sqrt(own * parts)
    whole = shape((width, width), f32)
    other = sibling(mine)
    one, two, next_grad = call(
        functools.partial(own_half_kernel, scale, size, n_py),
        (whole, whole, slab),
        1,
        in_vmem(whole, whole, slab, slab) + semaphores(22),
        1,
        OWN,
        None,
        HBM,
    )(core, mine, outgoing, grads.reshape(boundary, width))
    one, two = call(
        functools.partial(other_half_kernel, scale, size, n_py),
        (whole, whole),
        1,
        in_vmem(whole, whole) + semaphores(16),
        1,
        FINISH,
        {2: 0, 3: 1},
        HBM,
    )(core, other, one, two)

    return next_hidden, next_grad, one, two


def solution(mesh):
    in_specs = (
        P(BOTH, None),
        P(),
        P(),
        P(BOTH, None, None),
        P(BOTH, None),
        P(BOTH, None),
        P(BOTH),
        P(BOTH, None, None),
        P(BOTH, None),
        P(BOTH, None),
        P(BOTH, None),
        P(BOTH, None),
    )
    out_specs = (P(BOTH, None), P(BOTH, None), P(), P())
    return jax.shard_map(local, mesh=mesh, in_specs=in_specs, out_specs=out_specs, check_vma=False)
```
